32 devices in a mesh: dp: 16 (over z, y, x), mp: 2 (over core).
Axes of the slice: x: 2, y: 2, z: 4, core: 2. Of those that a mesh axis runs over, the one named last changes fastest.
Arguments:
- tokens: bfloat16 [32, 512, 768], P('dp', 'mp'), may hold values from -6 to 6
- lengths: int32 [32, 16], P('dp'), may hold values from 0 to 512, as said below
- cotangent: bfloat16 [32, 512, 768], P('dp', 'mp'), may hold values from -6 to 6
- w_query: bfloat16 [2, 768, 768], P(None, None, 'mp'), may hold values from -0.21875 to 0.21875
- b_query: bfloat16 [2, 768], P(None, 'mp'), may hold values from -3 to 3
- w_key: bfloat16 [2, 768, 768], P(None, None, 'mp'), may hold values from -0.21875 to 0.21875
- w_value: bfloat16 [2, 768, 768], P(None, None, 'mp'), may hold values from -0.21875 to 0.21875
- b_value: bfloat16 [2, 768], P(None, 'mp'), may hold values from -3 to 3
- w_out: bfloat16 [2, 768, 768], P(None, None, 'mp'), may hold values from -1.75 to 1.75
- b_out: bfloat16 [2, 768], replicated, may hold values from -3 to 3
- first_gain: bfloat16 [2, 768], replicated, may hold values from 0.099609375 to 1.8984375
- first_shift: bfloat16 [2, 768], replicated, may hold values from -3 to 3
- w_up: bfloat16 [2, 768, 3072], P(None, None, 'mp'), may hold values from -0.21875 to 0.21875
- b_up: bfloat16 [2, 3072], P(None, 'mp'), may hold values from -3 to 3
- w_down: bfloat16 [2, 768, 3072], P(None, None, 'mp'), may hold values from -0.109375 to 0.109375
- b_down: bfloat16 [2, 768], replicated, may hold values from -3 to 3
- second_gain: bfloat16 [2, 768], replicated, may hold values from 0.099609375 to 1.8984375
- second_shift: bfloat16 [2, 768], replicated, may hold values from -3 to 3
Outputs:
- encoded: bfloat16 [32, 512, 768], P('dp', 'mp')
- token_grad: float32 [32, 512, 768], P('dp', 'mp')
- grad_w_query: float32 [2, 768, 768], P(None, 'dp', 'mp')
- grad_b_query: float32 [2, 768], P(None, 'mp')
- grad_w_key: float32 [2, 768, 768], P(None, 'dp', 'mp')
- grad_w_value: float32 [2, 768, 768], P(None, 'dp', 'mp')
- grad_b_value: float32 [2, 768], P(None, 'mp')
- grad_w_out: float32 [2, 768, 768], P(None, 'dp', 'mp')
- grad_b_out: float32 [2, 768], replicated
- grad_first_gain: float32 [2, 768], replicated
- grad_first_shift: float32 [2, 768], replicated
- grad_w_up: float32 [2, 768, 3072], P(None, 'dp', 'mp')
- grad_b_up: float32 [2, 3072], P(None, 'mp')
- grad_w_down: float32 [2, 768, 3072], P(None, 'dp', 'mp')
- grad_b_down: float32 [2, 768], replicated
- grad_second_gain: float32 [2, 768], replicated
- grad_second_shift: float32 [2, 768], replicated
The draws below stay inside these ranges and needn't reach their ends.
Inputs may be any that keep to these rules, and one draw needn't show every extreme that they name: In each row either entries 1 to 15 are 0 and entry 0 is a passage's length, at least 64, or all 16 entries are lengths of queries, each at least 1 and at most 32. Some row holds a passage of 512 slots and some query fills its 32 slots.
All inputs are finite; a program needn't handle non-finite values.
Results may differ from the reference program's by a relative error of at most 0.04.
Values may be sent and summed in bfloat16 or wider, within the bound.
No kernel may reach another device: no remote copies, remote signals or barrier semaphores. Data moves between devices by JAX's collectives and lax.ppermute only.
A program may use at most 192 MiB of HBM per device.

```python
import jax
import jax.numpy as jnp
from jax import lax

D = 768
HEADS = 12
DH = 64
FF = 3072
LAYERS = 2
SLOTS = 512
QSLOT = 32
SEGS = 16
ROWS = 32


def draw_lengths(key, part):
    kind_key, pass_key, query_key = jax.random.split(key, 3)
    row_index = jnp.arange(ROWS, dtype=jnp.int32)
    column = jnp.arange(SEGS, dtype=jnp.int32)
    is_query = jax.random.randint(kind_key, (ROWS,), 0, 4) == 0
    is_query = jnp.where(row_index == 0, False, jnp.where(row_index == 1, True, is_query))
    passage = jax.random.randint(pass_key, (ROWS,), 2 * QSLOT, SLOTS + 1)
    passage = jnp.where(row_index == 0, SLOTS, passage)
    queries = jax.random.randint(query_key, (ROWS, SEGS), 1, QSLOT + 1)
    queries = jnp.where((row_index[:, None] == 1) & (column[None, :] == 0), QSLOT, queries)
    passage_rows = jnp.where(column[None, :] == 0, passage[:, None], 0)
    return jnp.where(is_query[:, None], queries, passage_rows).astype(jnp.int32)


def with_spikes(array, rng, source, target, parts, factor):
    def block_of(dim):
        return (jnp.arange(array.shape[dim]) // (array.shape[dim] // parts)).reshape((-1,) + (1,) * (array.ndim - 1 - dim))

    one_side = jax.random.permutation(rng, parts)[block_of(target)]
    other_side = (block_of(target) + parts // 2) % parts
    return jnp.where((block_of(source) == one_side) | (block_of(source) == other_side), factor * array, array)


def levels(rng, extent, cuts, least, high):
    gain = 1.0
    for axis_at, blocks in cuts:
        steps = jax.random.uniform(jax.random.fold_in(jax.random.fold_in(rng, 6), axis_at), (blocks,), jnp.float32, least / len(cuts), high / len(cuts))
        gain = gain * jnp.repeat(jnp.exp(steps), extent[axis_at] // blocks).reshape((-1,) + (1,) * (len(extent) - 1 - axis_at))
    return gain


def bell_draw(stream_key, dims, deviation, limit, cuts=(), held_as=jnp.bfloat16):
    values = deviation * jax.random.normal(stream_key, dims, jnp.float32)
    if cuts:
        values = values * levels(stream_key, dims, cuts, -0.22, 0.18)
    return jnp.clip(values, -limit, limit).astype(held_as)


def gaussian_with(rng, extent, spread, bound, shards, heavy, held_as=jnp.bfloat16):
    values = spread * jax.random.normal(rng, extent, jnp.float32)
    if shards:
        values = values * levels(rng, extent, shards, -0.22, 0.18)
    return jnp.clip(with_spikes(values, jax.random.fold_in(rng, 3), *heavy), -bound, bound).astype(held_as)


def setup_inputs(seed: int = 0) -> dict:
    key_of = jax.random.split(jax.random.key(seed), 19)
    tokens = gaussian_with(key_of[0], (ROWS, SLOTS, D), 1.0, 6.0, ((0, 16), (1, 2)), (0, 2, 16, 2.0))
    lengths = draw_lengths(jax.random.fold_in(key_of[18], 71), 0)
    cotangent = gaussian_with(key_of[2], (ROWS, SLOTS, D), 1.0, 6.0, ((0, 16), (1, 2)), (0, 2, 16, 2.0))
    w_query = bell_draw(key_of[3], (LAYERS, D, D), D ** -0.5, 0.21875, ((2, 2),))
    b_query = bell_draw(key_of[4], (LAYERS, D), 0.5, 3.0, ((1, 2),))
    w_key = bell_draw(key_of[5], (LAYERS, D, D), D ** -0.5, 0.21875, ((2, 2),))
    w_value = bell_draw(key_of[6], (LAYERS, D, D), D ** -0.5, 0.21875, ((2, 2),))
    b_value = bell_draw(key_of[7], (LAYERS, D), 0.5, 3.0, ((1, 2),))
    w_out = bell_draw(key_of[8], (LAYERS, D, D), (D // 64) ** -0.5, 1.75, ((2, 2),))
    b_out = bell_draw(key_of[9], (LAYERS, D), 0.5, 3.0)
    first_gain = jnp.clip(1.0 + 0.18 * jax.random.normal(key_of[10], (LAYERS, D), jnp.float32), 0.099609375, 1.8984375).astype(jnp.bfloat16)
    first_shift = bell_draw(key_of[11], (LAYERS, D), 0.5, 3.0)
    w_up = bell_draw(key_of[12], (LAYERS, D, FF), D ** -0.5, 0.21875, ((2, 2),))
    b_up = bell_draw(key_of[13], (LAYERS, FF), 0.5, 3.0, ((1, 2),))
    w_down = bell_draw(key_of[14], (LAYERS, D, FF), FF ** -0.5, 0.109375, ((2, 2),))
    b_down = bell_draw(key_of[15], (LAYERS, D), 0.5, 3.0)
    second_gain = jnp.clip(1.0 + 0.18 * jax.random.normal(key_of[16], (LAYERS, D), jnp.float32), 0.099609375, 1.8984375).astype(jnp.bfloat16)
    second_shift = bell_draw(key_of[17], (LAYERS, D), 0.5, 3.0)
    return dict(tokens=tokens, lengths=lengths, cotangent=cotangent, w_query=w_query, b_query=b_query, w_key=w_key, w_value=w_value, b_value=b_value, w_out=w_out, b_out=b_out, first_gain=first_gain, first_shift=first_shift, w_up=w_up, b_up=b_up, w_down=w_down, b_down=b_down, second_gain=second_gain, second_shift=second_shift)


highest = lax.Precision.HIGHEST

@jax.custom_vjp
def low(v):
    return lax.optimization_barrier(v.astype(jnp.bfloat16)).astype(jnp.float32)

@jax.custom_vjp
def low_back(v):
    return v

def low_keep(v):
    return (low(v), None)

def low_pass(kept, grad):
    return (grad,)

def back_keep(v):
    return (v, None)

def back_low(kept, grad):
    return (low(grad),)
low.defvjp(low_keep, low_pass)
low_back.defvjp(back_keep, back_low)

def visible_mask(lengths):
    slot_index = jnp.arange(SLOTS, dtype=jnp.int32)
    is_query = lengths[:, 1] > 0
    segment_width = jnp.where(is_query, QSLOT, SLOTS).astype(jnp.int32)[:, None]
    segment = slot_index[None, :] // segment_width
    inside = slot_index[None, :] - segment * segment_width
    onehot = segment[:, :, None] == jnp.arange(SEGS, dtype=jnp.int32)[None, None, :]
    segment_length = lax.optimization_barrier(jnp.sum(jnp.where(onehot, lengths[:, None, :], 0), axis=2))
    live_keys = inside < segment_length
    same_segment = segment[:, :, None] == segment[:, None, :]
    return same_segment & live_keys[:, None, :]

def layer_norm(residual, norm_gain, norm_shift):
    average = lax.optimization_barrier(jnp.mean(residual, axis=-1, keepdims=True))
    centred = residual - average
    variance = lax.optimization_barrier(jnp.mean(centred * centred, axis=-1, keepdims=True))
    return centred * lax.rsqrt(variance + 1e-12) * norm_gain + norm_shift

def gelu_exact(argument):
    return 0.5 * argument * (1.0 + jax.scipy.special.erf(argument * 0.7071067811865476))

def attend_row(row_data):
    query_heads, key_heads, value_heads, visible = row_data
    scores = jnp.einsum('shd,thd->hst', query_heads, key_heads, precision=highest) * DH ** (-0.5)
    scores = low_back(scores)
    scores = jnp.where(visible[None], scores, -1000000000.0)
    row_peak = lax.optimization_barrier(jnp.max(scores, axis=2, keepdims=True))
    exponent = jnp.exp(scores - row_peak)
    probabilities = low(exponent / lax.optimization_barrier(jnp.sum(exponent, axis=2, keepdims=True)))
    return jnp.einsum('hst,thd->shd', probabilities, value_heads, precision=highest)

def forward_layer(block_in, weights, visibility):
    w_query, b_query, w_key, w_value, b_value, w_out, b_out, first_gain, first_shift, w_up, b_up, w_down, b_down, second_gain, second_shift = weights
    flat_rows = block_in.reshape(ROWS * SLOTS, D)
    queries = low_back(low(jnp.dot(flat_rows, w_query, precision=highest) + b_query))
    keys_all = low_back(low(jnp.dot(flat_rows, w_key, precision=highest)))
    values_all = low_back(low(jnp.dot(flat_rows, w_value, precision=highest) + b_value))
    head_shape = (ROWS, SLOTS, HEADS, DH)
    context = lax.map(jax.checkpoint(attend_row), (queries.reshape(head_shape), keys_all.reshape(head_shape), values_all.reshape(head_shape), visibility))
    context = low_back(low(context.reshape(ROWS * SLOTS, D)))
    attended = low_back(jnp.dot(context, w_out.T, precision=highest) + b_out)
    normed = layer_norm(flat_rows + attended, first_gain, first_shift)
    upward = low_back(jnp.dot(low(normed), w_up, precision=highest) + b_up)
    activated = low(gelu_exact(upward))
    downward = low_back(jnp.dot(activated, w_down.T, precision=highest) + b_down)
    result = layer_norm(normed + downward, second_gain, second_shift)
    return result.reshape(ROWS, SLOTS, D)

def reference(tokens, lengths, cotangent, w_query, b_query, w_key, w_value, b_value, w_out, b_out, first_gain, first_shift, w_up, b_up, w_down, b_down, second_gain, second_shift):
    visibility = visible_mask(lengths)
    params = tuple((member.astype(jnp.float32) for member in (w_query, b_query, w_key, w_value, b_value, w_out, b_out, first_gain, first_shift, w_up, b_up, w_down, b_down, second_gain, second_shift)))

    def forward_all(block_in, *layer_params):
        hidden = block_in
        result = block_in
        for layer_index in range(LAYERS):
            weights = tuple((member[layer_index] for member in layer_params))
            result = forward_layer(hidden, weights, visibility)
            if layer_index + 1 < LAYERS:
                hidden = low(result)
        return result
    outcome, pullback = jax.vjp(forward_all, tokens.astype(jnp.float32), *params)
    gradients = pullback(cotangent.astype(jnp.float32))
    return (outcome.astype(jnp.bfloat16), gradients[0], gradients[1], gradients[2], gradients[3], gradients[4], gradients[5], gradients[6], gradients[7], gradients[8], gradients[9], gradients[10], gradients[11], gradients[12], gradients[13], gradients[14], gradients[15])
```

```python
import functools

import jax
import jax.numpy as jnp
from jax import lax
from jax.experimental import pallas as pl
from jax.experimental.pallas import tpu as pltpu
from jax.sharding import PartitionSpec as P

DH = 64
QSLOT = 32
BF = jnp.bfloat16
F32 = jnp.float32
PAIR = 2 * DH
CHUNK = 256


def nn(left, right):
    return lax.dot_general(left, right, (((1,), (0,)), ((), ())), preferred_element_type=F32)


def nt(left, right):
    return lax.dot_general(left, right, (((1,), (1,)), ((), ())), preferred_element_type=F32)


def tn(left, right):
    return lax.dot_general(left, right, (((0,), (0,)), ((), ())), preferred_element_type=F32)


def beside(*refs):
    return jnp.concatenate([r[...] for r in refs], axis=1)


def whole(*shape):
    return pl.BlockSpec(shape, lambda i: (0,) * len(shape))


def columns(rows, width):
    return pl.BlockSpec((rows, width), lambda i: (0, i))


def layer_columns(layer, rows, width):
    return pl.BlockSpec((None, rows, width), lambda i: (layer, 0, i))


def layer_whole(layer, rows, width):
    return pl.BlockSpec((None, rows, width), lambda i: (layer, 0, 0))


def sds(shape, dtype):
    return jax.ShapeDtypeStruct(shape, dtype)


def params(megabytes):
    return pltpu.CompilerParams(vmem_limit_bytes=megabytes * 1024 * 1024)


def attend_kernel(
    segq, segk, x, wqo, wqp, wko, wkp, wvo, wvp, bqo, bqp, bvo, bvp,
    qo, qp, ko, kp, vo, vp, co, cp, lse, bias,
):
    @pl.when(pl.program_id(0) == 0)
    def _():
        bias[...] = jnp.where(segq[...] == segk[...], 0.0, -1e9)

    xv = x[...]
    q = (nn(xv, beside(wqo, wqp)) + beside(bqo, bqp)).astype(BF)
    k = nn(xv, beside(wko, wkp)).astype(BF)
    v = (nn(xv, beside(wvo, wvp)) + beside(bvo, bvp)).astype(BF)
    first = lax.broadcasted_iota(jnp.int32, (1, PAIR), 1) < DH
    lse[...] = jnp.zeros_like(lse)
    for pair, (qr, kr, vr, cr) in enumerate(((qo, ko, vo, co), (qp, kp, vp, cp))):
        at = slice(pair * PAIR, (pair + 1) * PAIR)
        qq, kk, vv = q[:, at], k[:, at], v[:, at]
        qr[...] = qq
        kr[...] = kk
        vr[...] = vv
        outs, peaks = [], []
        for head in range(2):
            mine = first if head == 0 else ~first
            qm = jnp.where(mine, qq, jnp.zeros_like(qq)) * 0.125
            s = nt(qm.astype(BF), kk) + bias[...]
            peak = jnp.max(s, axis=1, keepdims=True)
            e = jnp.exp(s - peak).astype(BF)
            outs.append(nn(e, jnp.where(mine, vv, jnp.ones_like(vv))))
            peaks.append(peak)
        total = pltpu.roll(jnp.where(first, outs[1], outs[0]), DH, 1)
        cr[...] = (jnp.where(first, outs[0], outs[1]) / total).astype(BF)
        logs = jnp.where(first, peaks[0], peaks[1]) + jnp.log(total)
        flat = logs.T
        lse[2 * pair : 2 * pair + 1, :] = flat[0:1, :]
        lse[2 * pair + 1 : 2 * pair + 2, :] = flat[DH : DH + 1, :]


def attend(layer, segq, segk, x, own, peer, biases):
    slots, width = x.shape
    half = own["w_query"].shape[2]
    steps = half // PAIR
    weight = layer_columns(layer, width, PAIR)
    act = columns(slots, PAIR)
    bias = columns(1, PAIR)
    ins = [whole(slots, 1), whole(1, slots), whole(slots, width)] + [weight] * 6 + [bias] * 4
    return pl.pallas_call(
        attend_kernel,
        grid=(steps,),
        in_specs=ins,
        out_specs=[act] * 8 + [pl.BlockSpec((None, 8, slots), lambda i: (i, 0, 0))],
        out_shape=[sds((slots, half), BF)] * 8 + [sds((steps, 8, slots), F32)],
        scratch_shapes=[pltpu.VMEM((slots, slots), F32)],
        compiler_params=params(48),
    )(
        segq, segk, x,
        own["w_query"], peer["w_query"], own["w_key"], peer["w_key"], own["w_value"], peer["w_value"],
        *biases,
    )


def normalize(r):
    mean = jnp.mean(r, axis=1, keepdims=True)
    c = r - mean
    rstd = lax.rsqrt(jnp.mean(c * c, axis=1, keepdims=True) + 1e-12)
    return c * rstd, rstd


def feed_kernel(
    x, co, cp, woo, wop, b_out, g1, s1, wuo, wup, wdo, wdp, buo, bup, b_down, g2, s2,
    n1, rstd1, hlow, acto, actp, gpo, gpp, n2, rstd2, y, h, acc,
):
    step = pl.program_id(0)

    @pl.when(step == 0)
    def _():
        att = nt(co[...], woo[...]) + nt(cp[...], wop[...]) + b_out[...]
        n, rstd = normalize(x[...].astype(F32) + att)
        n1[...] = n
        rstd1[...] = rstd
        hv = n * g1[...] + s1[...]
        h[...] = hv
        hlow[...] = hv.astype(BF)
        acc[...] = jnp.zeros_like(acc)

    u = nn(hlow[...], beside(wuo, wup)) + beside(buo, bup)
    cdf = 0.5 * (1.0 + lax.erf(u * 0.7071067811865476))
    act = (u * cdf).astype(BF)
    slope = (cdf + u * (jnp.exp(u * u * -0.5) * 0.3989422804014327)).astype(BF)
    acto[...] = act[:, :CHUNK]
    actp[...] = act[:, CHUNK:]
    gpo[...] = slope[:, :CHUNK]
    gpp[...] = slope[:, CHUNK:]
    acc[...] += nt(act, beside(wdo, wdp))

    @pl.when(step == pl.num_programs(0) - 1)
    def _():
        n, rstd = normalize(h[...] + (acc[...] + b_down[...]))
        n2[...] = n
        rstd2[...] = rstd
        y[...] = (n * g2[...] + s2[...]).astype(BF)


def feed(layer, x, ctx_own, ctx_peer, own, peer, vec, up_biases):
    slots, width = x.shape
    half = own["w_query"].shape[2]
    ff = own["w_up"].shape[2]
    weight = layer_columns(layer, width, CHUNK)
    full = whole(slots, width)
    row = whole(1, width)
    one = whole(slots, 1)
    ins = [full, whole(slots, half), whole(slots, half)]
    ins += [layer_whole(layer, width, half)] * 2 + [row] * 3 + [weight] * 4
    ins += [columns(1, CHUNK)] * 2 + [row] * 3
    outs = [full, one, full] + [columns(slots, CHUNK)] * 4 + [full, one, full]
    shapes = [sds((slots, width), F32), sds((slots, 1), F32), sds((slots, width), BF)]
    shapes += [sds((slots, ff), BF)] * 4
    shapes += [sds((slots, width), F32), sds((slots, 1), F32), sds((slots, width), BF)]
    return pl.pallas_call(
        feed_kernel,
        grid=(ff // CHUNK,),
        in_specs=ins,
        out_specs=outs,
        out_shape=shapes,
        scratch_shapes=[pltpu.VMEM((slots, width), F32)] * 2,
        compiler_params=params(56),
    )(
        x, ctx_own, ctx_peer, own["w_out"], peer["w_out"], vec["b_out"], vec["first_gain"], vec["first_shift"],
        own["w_up"], peer["w_up"], own["w_down"], peer["w_down"], *up_biases,
        vec["b_down"], vec["second_gain"], vec["second_shift"],
    )


def norm_back(dy, n, rstd, gain):
    gdy = dy * gain
    return (
        gdy - jnp.mean(gdy, axis=1, keepdims=True) - n * jnp.mean(gdy * n, axis=1, keepdims=True)
    ) * rstd


def colsum(v):
    return jnp.sum(v.astype(F32), axis=0, keepdims=True)


def norm_kernel(dy, n, rstd, gain, dr, low, sums):
    dv = dy[...].astype(F32)
    nv = n[...]
    r = norm_back(dv, nv, rstd[...], gain[...])
    lowv = r.astype(BF)
    dr[...] = r
    low[...] = lowv
    sums[...] = jnp.concatenate(
        [colsum(dv * nv), colsum(dv), colsum(lowv), jnp.zeros((5, dv.shape[1]), F32)], axis=0
    )


def norm_backward(dy, n, rstd, gain):
    slots, width = n.shape
    return pl.pallas_call(
        norm_kernel,
        out_shape=[sds((slots, width), F32), sds((slots, width), BF), sds((8, width), F32)],
        compiler_params=params(32),
    )(dy, n, rstd, gain)


def feed_back_kernel(
    dff, dr2, wdo, wdp, wuo, wup, gpo, gpp, n1, rstd1, g1,
    duo, dup, gbuo, gbup, dr1, datt, sums, acc,
):
    step = pl.program_id(0)
    dact = nn(dff[...], beside(wdo, wdp))
    du = (dact * beside(gpo, gpp).astype(F32)).astype(BF)
    duo[...] = du[:, :CHUNK]
    dup[...] = du[:, CHUNK:]
    total = colsum(du)
    gbuo[...] = total[:, :CHUNK]
    gbup[...] = total[:, CHUNK:]
    part = nt(du, beside(wuo, wup))

    @pl.when(step == 0)
    def _():
        acc[...] = dr2[...] + part

    @pl.when(step > 0)
    def _():
        acc[...] += part

    @pl.when(step == pl.num_programs(0) - 1)
    def _():
        dh = acc[...]
        n = n1[...]
        r = norm_back(dh, n, rstd1[...], g1[...])
        low = r.astype(BF)
        dr1[...] = r
        datt[...] = low
        sums[...] = jnp.concatenate(
            [colsum(dh * n), colsum(dh), colsum(low), jnp.zeros((5, dh.shape[1]), F32)], axis=0
        )


def feed_back(layer, dff, dr2, own, peer, slope_own, slope_peer, n1, rstd1, gain):
    slots, width = dff.shape
    ff = own["w_up"].shape[2]
    weight = layer_columns(layer, width, CHUNK)
    act = columns(slots, CHUNK)
    full = whole(slots, width)
    ins = [full, full] + [weight] * 4 + [act] * 2 + [full, whole(slots, 1), whole(1, width)]
    return pl.pallas_call(
        feed_back_kernel,
        grid=(ff // CHUNK,),
        in_specs=ins,
        out_specs=[act] * 2 + [columns(1, CHUNK)] * 2 + [full, full, whole(8, width)],
        out_shape=[sds((slots, ff), BF)] * 2
        + [sds((1, ff), F32)] * 2
        + [sds((slots, width), F32), sds((slots, width), BF), sds((8, width), F32)],
        scratch_shapes=[pltpu.VMEM((slots, width), F32)],
        compiler_params=params(56),
    )(
        dff, dr2, own["w_down"], peer["w_down"], own["w_up"], peer["w_up"],
        slope_own, slope_peer, n1, rstd1, gain,
    )


def attend_back_kernel(
    segk, segq, datt, dr1, woo, wop, wqo, wqp, wko, wkp, wvo, wvp,
    qo, qp, ko, kp, vo, vp, lse,
    dqo, dqp, dko, dkp, dvo, dvp, gbqo, gbqp, gbvo, gbvp, dx, bias,
):
    step = pl.program_id(0)

    @pl.when(step == 0)
    def _():
        bias[...] = jnp.where(segk[...] == segq[...], 0.0, -1e9)

    dctx = nn(datt[...], beside(woo, wop)).astype(BF)
    first = lax.broadcasted_iota(jnp.int32, (1, PAIR), 1) < DH
    grads = []
    for pair, (qr, kr, vr, dqr, dkr, dvr, gbq, gbv) in enumerate(
        ((qo, ko, vo, dqo, dko, dvo, gbqo, gbvo), (qp, kp, vp, dqp, dkp, dvp, gbqp, gbvp))
    ):
        qq, kk, vv = qr[...], kr[...], vr[...]
        do = dctx[:, pair * PAIR : (pair + 1) * PAIR]
        dq_t, dk, dv = 0.0, 0.0, 0.0
        for head in range(2):
            mine = first if head == 0 else ~first
            qm = (jnp.where(mine, qq, jnp.zeros_like(qq)) * 0.125).astype(BF)
            km = (jnp.where(mine, kk, jnp.zeros_like(kk)) * 0.125).astype(BF)
            dom = jnp.where(mine, do, jnp.zeros_like(do))
            at = 2 * pair + head
            p = jnp.exp(nt(kk, qm) + bias[...] - lse[at : at + 1, :])
            dp = nt(vv, dom)
            delta = jnp.sum(p * dp, axis=0, keepdims=True)
            ds = (p * (dp - delta)).astype(BF)
            dv += nn(p.astype(BF), dom)
            dk += nn(ds, qm)
            dq_t += nn(km.T, ds)
        dq = dq_t.T.astype(BF)
        dk = dk.astype(BF)
        dv = dv.astype(BF)
        dqr[...] = dq
        dkr[...] = dk
        dvr[...] = dv
        gbq[...] = colsum(dq)
        gbv[...] = colsum(dv)
        grads.append((dq, dk, dv))
    back = jnp.concatenate([g[i] for i in range(3) for g in grads], axis=1)
    part = nt(back, beside(wqo, wqp, wko, wkp, wvo, wvp))

    @pl.when(step == 0)
    def _():
        dx[...] = dr1[...] + part

    @pl.when(step > 0)
    def _():
        dx[...] += part


def attend_back(layer, segk, segq, datt, dr1, own, peer, saved, lse):
    slots, width = datt.shape
    half = own["w_query"].shape[2]
    steps = half // PAIR
    weight = layer_columns(layer, width, PAIR)
    act = columns(slots, PAIR)
    full = whole(slots, width)
    ins = [whole(slots, 1), whole(1, slots), full, full] + [weight] * 8 + [act] * 6
    ins += [pl.BlockSpec((None, 8, slots), lambda i: (i, 0, 0))]
    return pl.pallas_call(
        attend_back_kernel,
        grid=(steps,),
        in_specs=ins,
        out_specs=[act] * 6 + [columns(1, PAIR)] * 4 + [full],
        out_shape=[sds((slots, half), BF)] * 6 + [sds((1, half), F32)] * 4 + [sds((slots, width), F32)],
        scratch_shapes=[pltpu.VMEM((slots, slots), F32)],
        compiler_params=params(56),
    )(
        segk, segq, datt, dr1, own["w_out"], peer["w_out"],
        own["w_query"], peer["w_query"], own["w_key"], peer["w_key"], own["w_value"], peer["w_value"],
        *saved, lse,
    )


def swap(value):
    return lax.ppermute(value, "mp", [(0, 1), (1, 0)])


def flip(value, bit, size):
    return lax.ppermute(value, "dp", [(i, i ^ (1 << bit)) for i in range(size)])


def scatter_sum(grad, order, size):
    bits = size.bit_length() - 1
    me = lax.axis_index("dp")
    value = grad.astype(BF).reshape((2,) * bits + (grad.shape[0] // size, grad.shape[1]))
    left = list(range(bits - 1, -1, -1))
    for bit in order:
        axis = left.index(bit)
        left.pop(axis)
        mine = (me >> bit) & 1
        keep = lax.dynamic_index_in_dim(value, mine, axis, keepdims=False)
        send = lax.dynamic_index_in_dim(value, 1 - mine, axis, keepdims=False)
        got = flip(send, bit, size)
        value = keep.astype(F32) + got.astype(F32)
        if left:
            value = value.astype(BF)
    return value


def full_sum(value, size):
    for bit in range(size.bit_length() - 1):
        value = value + flip(value, bit, size)
    return value


NAMES = (
    "w_query", "b_query", "w_key", "w_value", "b_value", "w_out", "b_out", "first_gain", "first_shift",
    "w_up", "b_up", "w_down", "b_down", "second_gain", "second_shift",
)


def shards(dp, tokens, lengths, cotangent, *given):
    held = dict(zip(NAMES, given, strict=True))
    layers, width, half = held["w_query"].shape
    ff = held["w_up"].shape[2]
    slots = 2 * tokens.shape[1]
    me = lax.axis_index("mp")

    def pick(array, index):
        return lax.dynamic_index_in_dim(array, index, 0, keepdims=False)

    def take_row(array):
        return jnp.concatenate([pick(array, me), swap(pick(array, 1 - me))], axis=0)

    def give_row(value):
        cut = slots // 2
        mine, other = value[:cut], swap(value[cut:])
        return jnp.stack([jnp.where(me == 0, mine, other), jnp.where(me == 0, other, mine)])

    x = take_row(tokens)
    matrices = ("w_query", "w_key", "w_value", "w_out", "w_up", "w_down")
    peer = {name: swap(held[name]) for name in matrices[:3]}
    halves = jnp.concatenate([held["b_query"], held["b_value"], held["b_up"]], axis=1)
    halves_peer = swap(halves)
    for name in matrices[3:]:
        peer[name] = swap(held[name])
    dy = take_row(cotangent)

    row_lengths = pick(lengths, me)
    slot = lax.rem(jnp.arange(slots, dtype=jnp.int32) + me * (slots // 2), slots)
    seg_width = jnp.where(row_lengths[1] > 0, QSLOT, slots)
    segment = lax.div(slot, seg_width)
    inside = slot - segment * seg_width
    onehot = segment[:, None] == jnp.arange(lengths.shape[1], dtype=jnp.int32)[None, :]
    live = inside < jnp.sum(jnp.where(onehot, row_lengths[None, :], 0), axis=1)
    segk = jnp.where(live, segment, -1)
    segq_c, segq_r = segment[:, None], segment[None, :]
    segk_c, segk_r = segk[:, None], segk[None, :]

    def vectors(layer):
        names = ("b_out", "first_gain", "first_shift", "b_down", "second_gain", "second_shift")
        return {n: held[n][layer].astype(F32)[None, :] for n in names}

    kept = []
    for layer in range(layers):
        mine = halves[layer].astype(F32)[None, :]
        theirs = halves_peer[layer].astype(F32)[None, :]
        qv = (mine[:, :half], theirs[:, :half], mine[:, half : 2 * half], theirs[:, half : 2 * half])
        up = (mine[:, 2 * half :], theirs[:, 2 * half :])
        vec = vectors(layer)
        att = attend(layer, segq_c, segk_r, x, held, peer, qv)
        fed = feed(layer, x, att[6], att[7], held, peer, vec, up)
        kept.append((x, att, fed, vec))
        x = fed[-1]

    encoded = give_row(x)
    grad_shards = {name: [None] * layers for name in matrices}
    small = [None] * layers

    def weight_grad(left, right_own, right_peer, left_peer=None):
        left_peer = swap(left) if left_peer is None else left_peer
        return tn(left, right_own) + tn(left_peer, swap(right_peer))

    bits = dp.bit_length() - 1
    rest = tuple(range(4, bits)) if bits > 4 else ()

    def order(*head):
        return tuple(b for b in head if b < bits) + rest

    for layer in reversed(range(layers)):
        x_in, att, fed, vec = kept[layer]
        (qo, qp, ko, kp, vo, vp, ctx_own, ctx_peer, lse) = att
        (n1, rstd1, hlow, act_own, act_peer, slope_own, slope_peer, n2, rstd2, _) = fed
        dr2, dff, sums2 = norm_backward(dy, n2, rstd2, vec["second_gain"])
        grad_down = weight_grad(dff, act_own, act_peer)
        grad_shards["w_down"][layer] = scatter_sum(grad_down, order(0, 1, 2, 3), dp)
        du_own, du_peer, gbu_own, gbu_peer, dr1, datt, sums1 = feed_back(
            layer, dff, dr2, held, peer, slope_own, slope_peer, n1, rstd1, vec["first_gain"]
        )
        grad_up = weight_grad(hlow, du_own, du_peer)
        grad_shards["w_up"][layer] = scatter_sum(grad_up, order(1, 0, 2, 3), dp)
        grad_out = weight_grad(datt, ctx_own, ctx_peer)
        grad_shards["w_out"][layer] = scatter_sum(grad_out, order(0, 1, 2, 3), dp)
        back = attend_back(
            layer, segk_c, segq_r, datt, dr1, held, peer, (qo, qp, ko, kp, vo, vp), lse
        )
        dqo, dqp, dko, dkp, dvo, dvp, gbq_own, gbq_peer, gbv_own, gbv_peer, dy = back
        x_peer = swap(x_in)
        for name, own_part, peer_part, way in (
            ("w_query", dqo, dqp, (2, 3, 0, 1)),
            ("w_key", dko, dkp, (2, 3, 1, 0)),
            ("w_value", dvo, dvp, (1, 0, 2, 3)),
        ):
            grad = weight_grad(x_in, own_part, peer_part, x_peer)
            grad_shards[name][layer] = scatter_sum(grad, order(*way), dp)
        rows = jnp.concatenate([sums1[:3].reshape(1, -1), sums2[:3].reshape(1, -1)], axis=1)
        mine = jnp.concatenate([gbq_own, gbv_own, gbu_own, rows], axis=1)
        theirs = jnp.concatenate([gbq_peer, gbv_peer, gbu_peer, rows], axis=1)
        small[layer] = full_sum(mine + swap(theirs), dp)

    token_grad = give_row(dy.astype(BF)).astype(F32)
    stacked = {name: jnp.stack(grad_shards[name]) for name in matrices}
    packed = jnp.concatenate(small, axis=0)
    cuts = [half, half, ff] + [width] * 6
    pieces, at = [], 0
    for cut in cuts:
        pieces.append(packed[:, at : at + cut])
        at += cut
    gbq, gbv, gbu, gfg, gfs, gbo, gsg, gss, gbd = pieces
    return (
        encoded, token_grad, stacked["w_query"], gbq, stacked["w_key"], stacked["w_value"], gbv,
        stacked["w_out"], gbo, gfg, gfs, stacked["w_up"], gbu, stacked["w_down"], gbd, gsg, gss,
    )


def solution(mesh):
    cols, mats, rep = P(None, "mp"), P(None, None, "mp"), P()
    placed = (
        P("dp", "mp", None), P("dp", None), P("dp", "mp", None),
        mats, cols, mats, mats, cols, mats, rep, rep, rep, mats, cols, mats, rep, rep, rep,
    )
    grads = P(None, "dp", "mp")
    return jax.shard_map(
        functools.partial(shards, mesh.shape["dp"]),
        mesh=mesh,
        in_specs=placed,
        out_specs=(
            P("dp", "mp", None), P("dp", "mp", None), grads, cols, grads, grads, cols,
            grads, rep, rep, rep, grads, cols, grads, rep, rep, rep,
        ),
        check_vma=False,
    )
```

```python
import functools

import jax
import jax.numpy as jnp
from jax import lax
from jax.experimental import pallas as pl
from jax.experimental.pallas import tpu as pltpu
from jax.sharding import PartitionSpec as P

DH = 64
QSLOT = 32
BF = jnp.bfloat16
F32 = jnp.float32
PAIR = 2 * DH
CHUNK = 256


def nn(left, right):
    return lax.dot_general(left, right, (((1,), (0,)), ((), ())), preferred_element_type=F32)


def nt(left, right):
    return lax.dot_general(left, right, (((1,), (1,)), ((), ())), preferred_element_type=F32)


def tn(left, right):
    return lax.dot_general(left, right, (((0,), (0,)), ((), ())), preferred_element_type=F32)


def beside(*refs):
    return jnp.concatenate([r[...] for r in refs], axis=1)


def whole(*shape):
    return pl.BlockSpec(shape, lambda i, *s: (0,) * len(shape))


def columns(rows, width, start=0):
    return pl.BlockSpec((rows, width), lambda i, *s: (0, start + i))


def layer_columns(layer, rows, width):
    return pl.BlockSpec((None, rows, width), lambda i, *s: (layer, 0, i))


def layer_whole(layer, rows, width):
    return pl.BlockSpec((None, rows, width), lambda i, *s: (layer, 0, 0))


def my_row(array):
    return pl.BlockSpec((None, *array.shape[1:]), lambda i, s: (s[0], 0, 0))


def sds(shape, dtype):
    return jax.ShapeDtypeStruct(shape, dtype)


def run(kernel, grid, scalars, ins, outs, scratch, megabytes):
    return pl.pallas_call(
        kernel,
        grid_spec=pltpu.PrefetchScalarGridSpec(
            num_scalar_prefetch=1,
            grid=(grid,),
            in_specs=[b for b, _ in ins],
            out_specs=[b for b, _, _ in outs],
            scratch_shapes=scratch,
        ),
        out_shape=[sds(shape, dtype) for _, shape, dtype in outs],
        compiler_params=pltpu.CompilerParams(vmem_limit_bytes=megabytes * 1024 * 1024),
        cost_estimate=pl.CostEstimate(flops=1000, transcendentals=0, bytes_accessed=1000),
    )(scalars, *[a for _, a in ins])


def row_of(ref, layer):
    return ref[layer : layer + 1, :].astype(F32)


def segments(scalars, count, slots, dim):
    shape = (slots, 1) if dim == 0 else (1, slots)
    slot = lax.broadcasted_iota(jnp.int32, shape, dim) + scalars[0] * (slots // 2)
    slot = jnp.where(slot >= slots, slot - slots, slot)
    base = 1 + scalars[0] * count
    shift = jnp.where(scalars[base + 1] > 0, QSLOT.bit_length() - 1, slots.bit_length() - 1)
    segment = lax.shift_right_logical(slot, jnp.broadcast_to(shift, shape))
    inside = slot - lax.shift_left(segment, jnp.broadcast_to(shift, shape))
    length = jnp.zeros(shape, jnp.int32)
    for k in range(count):
        length = jnp.where(segment == k, scalars[base + k], length)
    return segment, jnp.where(inside < length, segment, -1)


def attend_kernel(layer, count, split, scalars, *refs):
    refs = list(refs)
    xs = [refs.pop(0) for _ in range(2 if split else 1)]
    wqo, wqp, wko, wkp, wvo, wvp, bqo, bqp, bvo, bvp = refs[:10]
    qo, qp, ko, kp, vo, vp, co, cp, lse = refs[10:19]
    bias = refs[-1]
    x = refs[19] if split else xs[0]
    slots = qo.shape[0]

    @pl.when(pl.program_id(0) == 0)
    def _():
        segment, _ = segments(scalars, count, slots, 0)
        _, live = segments(scalars, count, slots, 1)
        bias[...] = jnp.where(segment == live, 0.0, -1e9)
        if split:
            x[...] = jnp.concatenate([r[...] for r in xs], axis=0)

    xv = x[...]
    q = (nn(xv, beside(wqo, wqp)) + both(bqo, bqp, layer)).astype(BF)
    k = nn(xv, beside(wko, wkp)).astype(BF)
    v = (nn(xv, beside(wvo, wvp)) + both(bvo, bvp, layer)).astype(BF)
    first = lax.broadcasted_iota(jnp.int32, (1, PAIR), 1) < DH
    lse[...] = jnp.zeros_like(lse)
    for pair, (qr, kr, vr, cr) in enumerate(((qo, ko, vo, co), (qp, kp, vp, cp))):
        at = slice(pair * PAIR, (pair + 1) * PAIR)
        qq, kk, vv = q[:, at], k[:, at], v[:, at]
        qr[...] = qq
        kr[...] = kk
        vr[...] = vv
        outs, peaks = [], []
        for head in range(2):
            mine = first if head == 0 else ~first
            qm = jnp.where(mine, qq, jnp.zeros_like(qq)) * 0.125
            s = nt(qm.astype(BF), kk) + bias[...]
            peak = jnp.max(s, axis=1, keepdims=True)
            e = jnp.exp(s - peak).astype(BF)
            outs.append(nn(e, jnp.where(mine, vv, jnp.ones_like(vv))))
            peaks.append(peak)
        total = pltpu.roll(jnp.where(first, outs[1], outs[0]), DH, 1)
        cr[...] = (jnp.where(first, outs[0], outs[1]) / total).astype(BF)
        logs = jnp.where(first, peaks[0], peaks[1]) + jnp.log(total)
        flat = logs.T
        lse[2 * pair : 2 * pair + 1, :] = flat[0:1, :]
        lse[2 * pair + 1 : 2 * pair + 2, :] = flat[DH : DH + 1, :]


def both(own, peer, layer):
    return jnp.concatenate([row_of(own, layer), row_of(peer, layer)], axis=1)


def attend(layer, scalars, count, x, own, peer):
    split = isinstance(x, tuple)
    layers, width, half = own["w_query"].shape
    slots = 2 * x[0].shape[1] if split else x.shape[0]
    steps = half // PAIR
    weight = layer_columns(layer, width, PAIR)
    act = columns(slots, PAIR)
    ins = [(my_row(a), a) for a in x] if split else [(whole(slots, width), x)]
    for name in ("w_query", "w_key", "w_value"):
        ins += [(weight, own[name]), (weight, peer[name])]
    ins += [(columns(layers, PAIR), own["b_query"]), (columns(layers, PAIR), peer["biases"])]
    ins += [(columns(layers, PAIR), own["b_value"]), (columns(layers, PAIR, steps), peer["biases"])]
    outs = [(act, (slots, half), BF)] * 8
    outs += [(pl.BlockSpec((None, 8, slots), lambda i, *s: (i, 0, 0)), (steps, 8, slots), F32)]
    if split:
        outs += [(whole(slots, width), (slots, width), BF)]
    kernel = functools.partial(attend_kernel, layer, count, split)
    return run(kernel, steps, scalars, ins, outs, [pltpu.VMEM((slots, slots), F32)], 32)


def normalize(r):
    mean = jnp.mean(r, axis=1, keepdims=True)
    c = r - mean
    rstd = lax.rsqrt(jnp.mean(c * c, axis=1, keepdims=True) + 1e-12)
    return c * rstd, rstd


def norm_back(dy, n, rstd, gain):
    gdy = dy * gain
    return (
        gdy - jnp.mean(gdy, axis=1, keepdims=True) - n * jnp.mean(gdy * n, axis=1, keepdims=True)
    ) * rstd


def colsum(v):
    return jnp.sum(v.astype(F32), axis=0, keepdims=True)


def norm_back_store(dy, n, rstd, gain, dr, low, sums):
    r = norm_back(dy, n, rstd, gain)
    lowv = r.astype(BF)
    dr[...] = r
    low[...] = lowv
    sums[...] = jnp.concatenate(
        [colsum(dy * n), colsum(dy), colsum(lowv), jnp.zeros((5, dy.shape[1]), F32)], axis=0
    )


def feed_kernel(layer, last, scalars, *refs):
    (x, co, cp, woo, wop, b_out, g1, s1, wuo, wup, wdo, wdp, buo, bup, b_down, g2, s2) = refs[:17]
    rest = list(refs[17:])
    cots = [rest.pop(0) for _ in range(2 if last else 0)]
    (n1, rstd1, hlow, acto, actp, gpo, gpp, y, a, b, c, h, acc) = rest
    step = pl.program_id(0)

    @pl.when(step == 0)
    def _():
        att = nt(beside(co, cp), beside(woo, wop)) + row_of(b_out, layer)
        n, rstd = normalize(x[...].astype(F32) + att)
        n1[...] = n
        rstd1[...] = rstd
        hv = n * row_of(g1, layer) + row_of(s1, layer)
        h[...] = hv
        hlow[...] = hv.astype(BF)
        acc[...] = jnp.zeros_like(acc)

    u = nn(hlow[...], beside(wuo, wup)) + both(buo, bup, layer)
    cdf = 0.5 * (1.0 + lax.erf(u * 0.7071067811865476))
    act = (u * cdf).astype(BF)
    slope = (cdf + u * (jnp.exp(u * u * -0.5) * 0.3989422804014327)).astype(BF)
    acto[...] = act[:, :CHUNK]
    actp[...] = act[:, CHUNK:]
    gpo[...] = slope[:, :CHUNK]
    gpp[...] = slope[:, CHUNK:]
    acc[...] += nt(act, beside(wdo, wdp))

    @pl.when(step == pl.num_programs(0) - 1)
    def _():
        n, rstd = normalize(h[...] + (acc[...] + row_of(b_down, layer)))
        y[...] = (n * row_of(g2, layer) + row_of(s2, layer)).astype(BF)
        if last:
            dy = jnp.concatenate([r[...] for r in cots], axis=0).astype(F32)
            norm_back_store(dy, n, rstd, row_of(g2, layer), a, b, c)
        else:
            a[...] = n
            b[...] = rstd


def feed(layer, scalars, x, ctx_own, ctx_peer, own, peer, cotangent):
    last = cotangent is not None
    layers, width, half = own["w_query"].shape
    slots = x.shape[0]
    ff = own["w_up"].shape[2]
    weight = layer_columns(layer, width, CHUNK)
    full = whole(slots, width)
    vec = whole(layers, width)
    act = columns(slots, CHUNK)
    part = whole(slots, half)
    projection = layer_whole(layer, width, half)
    ins = [(full, x), (part, ctx_own), (part, ctx_peer), (projection, own["w_out"]), (projection, peer["w_out"])]
    ins += [(vec, own[n]) for n in ("b_out", "first_gain", "first_shift")]
    for name in ("w_up", "w_down"):
        ins += [(weight, own[name]), (weight, peer[name])]
    ins += [(columns(layers, CHUNK), own["b_up"]), (columns(layers, CHUNK, 2 * half // CHUNK), peer["biases"])]
    ins += [(vec, own[n]) for n in ("b_down", "second_gain", "second_shift")]
    if last:
        ins += [(my_row(a), a) for a in cotangent]
    outs = [(full, (slots, width), F32), (whole(slots, 1), (slots, 1), F32), (full, (slots, width), BF)]
    outs += [(act, (slots, ff), BF)] * 4 + [(full, (slots, width), BF)]
    outs += [(full, (slots, width), F32)]
    if last:
        outs += [(full, (slots, width), BF), (whole(8, width), (8, width), F32)]
    else:
        outs += [(whole(slots, 1), (slots, 1), F32), (whole(8, 128), (8, 128), F32)]
    scratch = [pltpu.VMEM((slots, width), F32)] * 2
    return run(functools.partial(feed_kernel, layer, last), ff // CHUNK, scalars, ins, outs, scratch, 40)


def feed_back_kernel(layer, scalars, *refs):
    (dff, dr2, wdo, wdp, wuo, wup, gpo, gpp, n1, rstd1, g1, duo, dup, gbuo, gbup, dr1, datt, sums, acc) = refs
    step = pl.program_id(0)
    dact = nn(dff[...], beside(wdo, wdp))
    du = (dact * beside(gpo, gpp).astype(F32)).astype(BF)
    duo[...] = du[:, :CHUNK]
    dup[...] = du[:, CHUNK:]
    total = colsum(du)
    gbuo[...] = total[:, :CHUNK]
    gbup[...] = total[:, CHUNK:]
    part = nt(du, beside(wuo, wup))

    @pl.when(step == 0)
    def _():
        acc[...] = dr2[...] + part

    @pl.when(step > 0)
    def _():
        acc[...] += part

    @pl.when(step == pl.num_programs(0) - 1)
    def _():
        norm_back_store(acc[...], n1[...], rstd1[...], row_of(g1, layer), dr1, datt, sums)


def feed_back(layer, scalars, dff, dr2, own, peer, slope_own, slope_peer, n1, rstd1):
    slots, width = dff.shape
    ff = own["w_up"].shape[2]
    weight = layer_columns(layer, width, CHUNK)
    act = columns(slots, CHUNK)
    full = whole(slots, width)
    ins = [(full, dff), (full, dr2)]
    for name in ("w_down", "w_up"):
        ins += [(weight, own[name]), (weight, peer[name])]
    ins += [(act, slope_own), (act, slope_peer), (full, n1), (whole(slots, 1), rstd1)]
    ins += [(whole(*own["first_gain"].shape), own["first_gain"])]
    outs = [(act, (slots, ff), BF)] * 2 + [(columns(1, CHUNK), (1, ff), F32)] * 2
    outs += [(full, (slots, width), F32), (full, (slots, width), BF), (whole(8, width), (8, width), F32)]
    scratch = [pltpu.VMEM((slots, width), F32)]
    return run(functools.partial(feed_back_kernel, layer), ff // CHUNK, scalars, ins, outs, scratch, 36)


def attend_back_kernel(layer, count, scalars, *refs):
    (datt, dr1, woo, wop, wqo, wqp, wko, wkp, wvo, wvp, qo, qp, ko, kp, vo, vp, lse) = refs[:17]
    sums1, sums2, gbuo, gbup = refs[17:21]
    rest = list(refs[21:])
    n2, rstd2, gain = (rest.pop(0) for _ in range(3)) if layer else (None,) * 3
    dqo, dqp, dko, dkp, dvo, dvp, mine, theirs = rest[:8]
    bias = rest[-1]
    step = pl.program_id(0)
    slots, half = dqo.shape[0], woo.shape[1] * 3
    dx = rest[8]

    @pl.when(step == 0)
    def _():
        _, live = segments(scalars, count, slots, 0)
        segment, _ = segments(scalars, count, slots, 1)
        bias[...] = jnp.where(segment == live, 0.0, -1e9)
        rows = jnp.concatenate([sums1[0:3, :], sums2[0:3, :]], axis=0)
        for pack, gbu in ((mine, gbuo), (theirs, gbup)):
            width = pack.shape[1]
            pack[...] = jnp.concatenate(
                [rows, gbu[:, :width], gbu[:, width:], jnp.zeros((8, width), F32)], axis=0
            )

    dctx = nn(datt[...], beside(woo, wop)).astype(BF)
    first = lax.broadcasted_iota(jnp.int32, (1, PAIR), 1) < DH
    grads = []
    for pair, (qr, kr, vr, dqr, dkr, dvr, pack) in enumerate(
        ((qo, ko, vo, dqo, dko, dvo, mine), (qp, kp, vp, dqp, dkp, dvp, theirs))
    ):
        qq, kk, vv = qr[...], kr[...], vr[...]
        do = dctx[:, pair * PAIR : (pair + 1) * PAIR]
        dq_t, dk, dv = 0.0, 0.0, 0.0
        for head in range(2):
            sel = first if head == 0 else ~first
            qm = (jnp.where(sel, qq, jnp.zeros_like(qq)) * 0.125).astype(BF)
            km = (jnp.where(sel, kk, jnp.zeros_like(kk)) * 0.125).astype(BF)
            dom = jnp.where(sel, do, jnp.zeros_like(do))
            at = 2 * pair + head
            p = jnp.exp(nt(kk, qm) + bias[...] - lse[at : at + 1, :])
            dp = nt(vv, dom)
            delta = jnp.sum(p * dp, axis=0, keepdims=True)
            ds = (p * (dp - delta)).astype(BF)
            dv += nn(p.astype(BF), dom)
            dk += nn(ds, qm)
            dq_t += nn(km.T, ds)
        dq = dq_t.T.astype(BF)
        dk = dk.astype(BF)
        dv = dv.astype(BF)
        dqr[...] = dq
        dkr[...] = dk
        dvr[...] = dv
        pack[8:9, pl.ds(pl.multiple_of(step * PAIR, PAIR), PAIR)] = colsum(dq)
        pack[8:9, pl.ds(pl.multiple_of(step * PAIR + half_of(pack), PAIR), PAIR)] = colsum(dv)
        grads.append((dq, dk, dv))
    back = jnp.concatenate([g[i] for i in range(3) for g in grads], axis=1)
    part = nt(back, beside(wqo, wqp, wko, wkp, wvo, wvp))

    @pl.when(step == 0)
    def _():
        dx[...] = dr1[...] + part

    @pl.when(step > 0)
    def _():
        dx[...] += part

    if layer:
        dff, sums = rest[9:11]

        @pl.when(step == pl.num_programs(0) - 1)
        def _():
            norm_back_store(dx[...], n2[...], rstd2[...], row_of(gain, layer - 1), dx, dff, sums)


def half_of(pack):
    return pack.shape[1] // 2


def attend_back(layer, scalars, count, datt, dr1, own, peer, saved, lse, sums, below):
    slots, width = datt.shape
    half = own["w_query"].shape[2]
    steps = half // PAIR
    weight = layer_columns(layer, width, PAIR)
    act = columns(slots, PAIR)
    full = whole(slots, width)
    ins = [(full, datt), (full, dr1)]
    for name in ("w_out", "w_query", "w_key", "w_value"):
        ins += [(weight, own[name]), (weight, peer[name])]
    ins += [(act, a) for a in saved] + [(pl.BlockSpec((None, 8, slots), lambda i, *s: (i, 0, 0)), lse)]
    ins += [(whole(*a.shape), a) for a in sums]
    if layer:
        ins += [(whole(*a.shape), a) for a in below]
    outs = [(act, (slots, half), BF)] * 6 + [(whole(16, width), (16, width), F32)] * 2
    outs += [(full, (slots, width), F32)]
    if layer:
        outs += [(full, (slots, width), BF), (whole(8, width), (8, width), F32)]
    kernel = functools.partial(attend_back_kernel, layer, count)
    return run(kernel, steps, scalars, ins, outs, [pltpu.VMEM((slots, slots), F32)], 40)


def halves_of(value, bit, scalars, left, base):
    axis = left.index(bit)
    rows, width = value.shape
    cut = value.reshape(1 << axis, 2, rows >> (axis + 1), width)
    mine = (scalars[base] >> bit) & 1
    low, high = cut[:, 0].reshape(rows // 2, width), cut[:, 1].reshape(rows // 2, width)
    return jnp.where(mine == 0, low, high), jnp.where(mine == 0, high, low)


def weight_kernel(plan, left, scalars, *refs):
    step = pl.program_id(0)
    pieces = sum(len(p) for _, p in plan)
    operands, rest = refs[: 4 * pieces], refs[4 * pieces :]
    outs, (lt, right) = rest[:-2], rest[-2:]
    slots = operands[0].shape[0]
    n = 0
    for g, (bit, parts) in enumerate(plan):
        column = 0
        for start, steps, block, fresh in parts:
            lo, lp, ro, rp = operands[4 * n : 4 * n + 4]
            n += 1
            if fresh:

                @pl.when(step == start)
                def _(lo=lo, lp=lp):
                    lt[:, :slots] = lo[...].T
                    lt[:, slots:] = lp[...].T

            @pl.when((step >= start) & (step < start + steps))
            def _(ro=ro, rp=rp, block=block, start=start, column=column, g=g, bit=bit):
                right[:slots, :block] = ro[...]
                right[slots:, :block] = rp[...]
                value = nn(lt[...], right[:, :block])
                at = pl.ds(pl.multiple_of(column + (step - start) * block, 128), block)
                if bit is None:
                    outs[g][:, at] = value.astype(BF)
                else:
                    keep, send = halves_of(value, bit, scalars, left, 1)
                    outs[2 * g][:, at] = keep.astype(BF)
                    outs[2 * g + 1][:, at] = send.astype(BF)

            column += steps * block


def weight_grads(scalars, groups, size, block):
    bits = size.bit_length() - 1
    left = list(range(bits - 1, -1, -1))
    plan, ins, outs = [], [], []
    at = 0
    before = None
    slots, width = groups[0][1][0][0].shape
    split = (width // size) % 16 == 0
    for order, parts in groups:
        pieces, total = [], 0
        for lo, lp, ro, rp in parts:
            blk = min(block, ro.shape[1])
            steps = ro.shape[1] // blk
            pieces.append((at, steps, blk, lo is not before))
            before = lo
            spec = pl.BlockSpec((slots, blk), lambda i, *s, a=at, n=steps: (0, jnp.clip(i - a, 0, n - 1)))
            ins += [(whole(slots, width), lo), (whole(slots, width), lp), (spec, ro), (spec, rp)]
            at += steps
            total += ro.shape[1]
        plan.append((order[0] if split else None, pieces))
        rows = width // 2 if split else width
        outs += [(whole(rows, total), (rows, total), BF)] * (2 if split else 1)
    scratch = [pltpu.VMEM((width, 2 * slots), BF), pltpu.VMEM((2 * slots, block), BF)]
    made = run(functools.partial(weight_kernel, plan, left), at, scalars, ins, outs, scratch, 40)
    if split:
        return [Scatter(scalars, o, size, made[2 * g], made[2 * g + 1]) for g, (o, _) in enumerate(groups)]
    return [Scatter(scalars, o, size, None, made[g]) for g, (o, _) in enumerate(groups)]


def add_kernel(bit, left, scalars, keep, got, *outs):
    value = keep[...].astype(F32) + got[...].astype(F32)
    kept, send = halves_of(value, bit, scalars, left, 1)
    outs[0][...] = kept.astype(BF)
    outs[1][...] = send.astype(BF)


class Scatter:
    def __init__(self, scalars, order, size, keep, send):
        bits = size.bit_length() - 1
        self.scalars, self.size = scalars, size
        self.order = [b for b in order if b < bits] + list(range(4, bits))
        self.left = list(range(bits - 1, -1, -1))
        self.keep, self.value = keep, send
        if keep is None:
            self.part(send)

    def part(self, value):
        bit = self.order[0]
        axis = self.left.index(bit)
        rows, width = value.shape
        cut = value.reshape(1 << axis, 2, rows >> (axis + 1), width)
        mine = (self.scalars[1] >> bit) & 1
        self.keep = lax.dynamic_index_in_dim(cut, mine, 1, keepdims=False).reshape(rows // 2, width)
        self.value = lax.dynamic_index_in_dim(cut, 1 - mine, 1, keepdims=False).reshape(rows // 2, width)

    def launch(self):
        bit = self.order.pop(0)
        self.left.remove(bit)
        self.value = flip(self.value, bit, self.size)
        return self

    def land(self):
        rows, width = self.keep.shape
        if (rows >> len(self.order)) % 16:
            self.part((self.keep.astype(F32) + self.value.astype(F32)).astype(BF))
            return self
        block = width // 3
        full, less = columns(rows, block), columns(rows // 2, block)
        self.keep, self.value = run(
            functools.partial(add_kernel, self.order[0], list(self.left)), 3, self.scalars,
            [(full, self.keep), (full, self.value)], [(less, (rows // 2, width), BF)] * 2, [], 16,
        )
        return self


def gate(value, *scatters):
    out = lax.optimization_barrier((value, *[s.value for s in scatters]))
    for s, v in zip(scatters, out[1:], strict=True):
        s.value = v
    return out[0]


def last_kernel(count, scalars, *refs):
    ins, outs = refs[: 2 * count], refs[2 * count :]
    layers = outs[0].shape[0]
    at = 0
    for out in outs:
        column = 0
        while column < out.shape[2]:
            width = ins[at].shape[1]
            for layer in range(layers):
                keep, got = ins[at : at + 2]
                at += 2
                out[layer, :, column : column + width] = keep[...].astype(F32) + got[...].astype(F32)
            column += width


def last_sums(scalars, parts, widths):
    arrays = [a for pair in parts for a in pair]
    rows = arrays[0].shape[0]
    layers = 2
    return run(
        functools.partial(last_kernel, len(parts)), 1, scalars,
        [(whole(*a.shape), a) for a in arrays],
        [(whole(layers, rows, w), (layers, rows, w), F32) for w in widths], [], 24,
    )


def small_kernel(layers, scalars, mine, got, gbq, gbv, gbu, *vectors):
    width = mine.shape[1]
    for layer in range(layers):
        total = mine[16 * layer : 16 * layer + 16, :] + got[16 * layer : 16 * layer + 16, :]
        row = slice(layer, layer + 1)
        for i, out in enumerate(vectors):
            out[row, :] = total[i : i + 1, :]
        gbu[row, :width] = total[6:7, :]
        gbu[row, width:] = total[7:8, :]
        gbq[row, :] = total[8:9, : width // 2]
        gbv[row, :] = total[8:9, width // 2 :]


def swap(value):
    return lax.ppermute(value, "mp", [(0, 1), (1, 0)])


def flip(value, bit, size):
    return lax.ppermute(value, "dp", [(i, i ^ (1 << bit)) for i in range(size)])


NAMES = (
    "w_query", "b_query", "w_key", "w_value", "b_value", "w_out", "b_out", "first_gain", "first_shift",
    "w_up", "b_up", "w_down", "b_down", "second_gain", "second_shift",
)
XY, YX, ZX = (0, 1, 2, 3), (1, 0, 2, 3), (2, 3, 0, 1)


def shards(dp, tokens, lengths, cotangent, *given):
    held = dict(zip(NAMES, given, strict=True))
    layers, width, half = held["w_query"].shape
    ff = held["w_up"].shape[2]
    slots = 2 * tokens.shape[1]
    count = lengths.shape[1]
    me = lax.axis_index("mp")
    scalars = jnp.concatenate([me[None], lengths.reshape(-1)]).astype(jnp.int32)
    place = jnp.stack([me, lax.axis_index("dp")]).astype(jnp.int32)

    def give_row(mine, other):
        other = swap(other).astype(mine.dtype)
        return jnp.stack([jnp.where(me == 0, mine, other), jnp.where(me == 0, other, mine)])

    x = (tokens, swap(tokens))
    peer = {name: swap(held[name]) for name in ("w_query", "w_key", "w_value")}
    peer["biases"] = swap(jnp.concatenate([held["b_query"], held["b_value"], held["b_up"]], axis=1))
    for name in ("w_out", "w_up", "w_down"):
        peer[name] = swap(held[name])
    cot = (cotangent, swap(cotangent))

    kept = []
    for layer in range(layers):
        att = attend(layer, scalars, count, x, held, peer)
        x = att[9] if layer == 0 else x
        fed = feed(layer, scalars, x, att[6], att[7], held, peer, cot if layer == layers - 1 else None)
        kept.append((x, att, fed))
        x = fed[7]
    encoded = give_row(x[: slots // 2], x[slots // 2 :])

    groups = [None] * layers
    packs = [None] * layers
    dr2, dff, sums2 = kept[-1][2][8:11]
    for layer in reversed(range(layers)):
        x_in, att, fed = kept[layer]
        (ctx_own, ctx_peer, lse) = att[6:9]
        (n1, rstd1, hlow, act_own, act_peer, slope_own, slope_peer) = fed[:7]
        du_own, du_peer, gbu_own, gbu_peer, dr1, datt, sums1 = feed_back(
            layer, scalars, dff, dr2, held, peer, slope_own, slope_peer, n1, rstd1
        )
        (down,) = weight_grads(place, [(XY, [(dff, swap(dff), act_own, swap(act_peer))])], dp, 512)
        (up,) = weight_grads(
            place,
            [(YX, [(hlow, swap(hlow), du_own, swap(du_peer)), (datt, swap(datt), ctx_own, swap(ctx_peer))])],
            dp, 512,
        )
        if layer < layers - 1:
            for f in flying:
                f.land()
            datt = gate(datt, down, up, *flying)
            for f in flying:
                f.launch()
        else:
            datt = gate(datt, down, up)
        down.launch()
        up.launch()
        below = (*kept[layer - 1][2][8:10], held["second_gain"]) if layer else ()
        back = attend_back(
            layer, scalars, count, datt, dr1, held, peer, att[:6], lse, (sums1, sums2, gbu_own, gbu_peer), below
        )
        dqo, dqp, dko, dkp, dvo, dvp, mine, theirs = back[:8]
        packs[layer] = (mine, theirs)
        x_peer = swap(x_in)
        parts = [(x_in, x_peer, o, swap(p)) for o, p in ((dqo, dqp), (dko, dkp), (dvo, dvp))]
        if layer:
            rest = weight_grads(place, [(ZX, parts)], dp, 384)
            dr2, dff, sums2 = back[8:11]
            down.land()
            up.land()
            dff = gate(dff, down, up, *rest)
            flying = [down, up, *rest]
            for f in flying:
                f.launch()
        else:
            rest = weight_grads(place, [(o, [p]) for o, p in zip((XY, YX, ZX), parts, strict=True)], dp, 384)
            for f in rest:
                f.launch()
        groups[layer] = (down, up, rest)

    dx = back[8]
    token_grad = give_row(dx[: slots // 2], dx[slots // 2 :].astype(BF))

    total = jnp.concatenate([p[0] for p in packs], axis=0) + swap(jnp.concatenate([p[1] for p in packs], axis=0))
    everything = [groups[layer] for layer in reversed(range(layers))]
    while any(f.order for d, u, r in everything for f in (d, u, *r)):
        for d, u, r in everything:
            for f in (d, u, *r):
                if f.order:
                    f.land()
                    f.launch()
    bits = dp.bit_length() - 1
    for bit in range(bits - 1):
        total = total + flip(total, bit, dp)
    got = flip(total, bits - 1, dp)

    def pairs(pick):
        return [(f.keep, f.value) for f in (pick(groups[layer]) for layer in range(layers))]

    (gwd,) = last_sums(place, pairs(lambda g: g[0]), [ff])
    up = [(f.keep, f.value) for f in (groups[layer][1] for layer in range(layers))]
    uppers = [(k[:, :ff], v[:, :ff]) for k, v in up]
    outers = [(k[:, ff:], v[:, ff:]) for k, v in up]
    first = groups[0][2]
    later = groups[1][2][0]
    qkv = []
    for i in range(3):
        at = slice(i * half, (i + 1) * half)
        qkv += [(first[i].keep, first[i].value), (later.keep[:, at], later.value[:, at])]
    gwu, gwo = last_sums(place, uppers + outers, [ff, half])
    gwq, gwk, gwv = last_sums(place, qkv, [half] * 3)
    shapes = [half, half, ff] + [width] * 6
    gbq, gbv, gbu, gfg, gfs, gbo, gsg, gss, gbd = run(
        functools.partial(small_kernel, layers), 1, place,
        [(whole(*total.shape), total), (whole(*got.shape), got)],
        [(whole(layers, n), (layers, n), F32) for n in shapes], [], 16,
    )
    return (
        encoded, token_grad, gwq, gbq, gwk, gwv, gbv, gwo, gbo, gfg, gfs, gwu, gbu, gwd, gbd, gsg, gss,
    )


def solution(mesh):
    cols, mats, rep = P(None, "mp"), P(None, None, "mp"), P()
    placed = (
        P("dp", "mp", None), P("dp", None), P("dp", "mp", None),
        mats, cols, mats, mats, cols, mats, rep, rep, rep, mats, cols, mats, rep, rep, rep,
    )
    grads = P(None, "dp", "mp")
    return jax.shard_map(
        functools.partial(shards, mesh.shape["dp"]),
        mesh=mesh,
        in_specs=placed,
        out_specs=(
            P("dp", "mp", None), P("dp", "mp", None), grads, cols, grads, grads, cols,
            grads, rep, rep, rep, grads, cols, grads, rep, rep, rep,
        ),
        check_vma=False,
    )
```

```python
import functools

import jax
import jax.numpy as jnp
from jax import lax
from jax.experimental import pallas as pl
from jax.experimental.pallas import tpu as pltpu
from jax.sharding import PartitionSpec as P

DH = 64
QSLOT = 32
BF = jnp.bfloat16
F32 = jnp.float32
PAIR = 2 * DH
CHUNK = 256


def nn(left, right):
    return lax.dot_general(left, right, (((1,), (0,)), ((), ())), preferred_element_type=F32)


def nt(left, right):
    return lax.dot_general(left, right, (((1,), (1,)), ((), ())), preferred_element_type=F32)


def tn(left, right):
    return lax.dot_general(left, right, (((0,), (0,)), ((), ())), preferred_element_type=F32)


def beside(*refs):
    return jnp.concatenate([r[...] for r in refs], axis=1)


def whole(*shape):
    return pl.BlockSpec(shape, lambda i, *s: (0,) * len(shape))


def columns(rows, width, start=0):
    return pl.BlockSpec((rows, width), lambda i, *s: (0, start + i))


def layer_columns(layer, array, width):
    at = layer if array.shape[0] > 1 else 0
    return pl.BlockSpec((None, array.shape[1], width), lambda i, *s: (at, 0, i)), array


def layer_whole(layer, array):
    at = layer if array.shape[0] > 1 else 0
    return pl.BlockSpec((None, *array.shape[1:]), lambda i, *s: (at, 0, 0)), array


def my_row(array):
    return pl.BlockSpec((None, *array.shape[1:]), lambda i, s: (s[0], 0, 0))


def sds(shape, dtype):
    return jax.ShapeDtypeStruct(shape, dtype)


class Order:
    last = None
    pending = []


def run(kernel, grid, scalars, ins, outs, scratch, megabytes, pinned=False):
    shape = pltpu.HBM if pinned in (True, "out") else sds
    arrays = [a for _, a in ins]
    kept = range(len(arrays)) if pinned is True else pinned if isinstance(pinned, list) else ()
    for i in kept:
        arrays[i] = pltpu.with_memory_space_constraint(arrays[i], pltpu.HBM)
    extra = Order.pending + ([] if Order.last is None else [Order.last])
    Order.pending = []
    count = 1 + len(ins)

    def body(*refs):
        kernel(*refs[:count], *refs[count + len(extra) :])

    made = pl.pallas_call(
        body,
        grid_spec=pltpu.PrefetchScalarGridSpec(
            num_scalar_prefetch=1,
            grid=(grid,),
            in_specs=[b for b, _ in ins] + [pl.BlockSpec(memory_space=pl.ANY)] * len(extra),
            out_specs=[b for b, _, _ in outs],
            scratch_shapes=scratch,
        ),
        out_shape=[shape(dims, dtype) for _, dims, dtype in outs],
        compiler_params=pltpu.CompilerParams(vmem_limit_bytes=megabytes * 1024 * 1024),
        cost_estimate=pl.CostEstimate(flops=1000, transcendentals=0, bytes_accessed=1000),
    )(scalars, *arrays, *extra)
    Order.last = made[-1]
    return made


def row_of(ref, layer):
    return ref[layer : layer + 1, :].astype(F32)


def segments(scalars, count, slots, dim):
    shape = (slots, 1) if dim == 0 else (1, slots)
    slot = lax.broadcasted_iota(jnp.int32, shape, dim) + scalars[0] * (slots // 2)
    slot = jnp.where(slot >= slots, slot - slots, slot)
    base = 1 + scalars[0] * count
    shift = jnp.where(scalars[base + 1] > 0, QSLOT.bit_length() - 1, slots.bit_length() - 1)
    segment = lax.shift_right_logical(slot, jnp.broadcast_to(shift, shape))
    inside = slot - lax.shift_left(segment, jnp.broadcast_to(shift, shape))
    length = jnp.zeros(shape, jnp.int32)
    for k in range(count):
        length = jnp.where(segment == k, scalars[base + k], length)
    return segment, jnp.where(inside < length, segment, -1)


def attend_kernel(layer, count, split, scalars, *refs):
    refs = list(refs)
    xs = [refs.pop(0) for _ in range(2 if split else 1)]
    wqo, wqp, wko, wkp, wvo, wvp, bqo, bqp, bvo, bvp = refs[:10]
    qo, qp, ko, kp, vo, vp, co, cp, lse = refs[10:19]
    bias = refs[-1]
    x = refs[19] if split else xs[0]
    slots = qo.shape[0]

    @pl.when(pl.program_id(0) == 0)
    def _():
        segment, _ = segments(scalars, count, slots, 0)
        _, live = segments(scalars, count, slots, 1)
        bias[...] = jnp.where(segment == live, 0.0, -1e9)
        if split:
            x[...] = jnp.concatenate([r[...] for r in xs], axis=0)

    xv = x[...]
    q = (nn(xv, beside(wqo, wqp)) + both(bqo, bqp, layer)).astype(BF)
    k = nn(xv, beside(wko, wkp)).astype(BF)
    v = (nn(xv, beside(wvo, wvp)) + both(bvo, bvp, layer)).astype(BF)
    first = lax.broadcasted_iota(jnp.int32, (1, PAIR), 1) < DH
    lse[...] = jnp.zeros_like(lse)
    for pair, (qr, kr, vr, cr) in enumerate(((qo, ko, vo, co), (qp, kp, vp, cp))):
        at = slice(pair * PAIR, (pair + 1) * PAIR)
        qq, kk, vv = q[:, at], k[:, at], v[:, at]
        qr[...] = qq
        kr[...] = kk
        vr[...] = vv
        outs, peaks = [], []
        for head in range(2):
            mine = first if head == 0 else ~first
            qm = jnp.where(mine, qq, jnp.zeros_like(qq)) * 0.125
            s = nt(qm.astype(BF), kk) + bias[...]
            peak = jnp.max(s, axis=1, keepdims=True)
            e = jnp.exp(s - peak).astype(BF)
            outs.append(nn(e, jnp.where(mine, vv, jnp.ones_like(vv))))
            peaks.append(peak)
        total = pltpu.roll(jnp.where(first, outs[1], outs[0]), DH, 1)
        cr[...] = (jnp.where(first, outs[0], outs[1]) / total).astype(BF)
        logs = jnp.where(first, peaks[0], peaks[1]) + jnp.log(total)
        flat = logs.T
        lse[2 * pair : 2 * pair + 1, :] = flat[0:1, :]
        lse[2 * pair + 1 : 2 * pair + 2, :] = flat[DH : DH + 1, :]


def both(own, peer, layer):
    return jnp.concatenate([row_of(own, layer), row_of(peer, layer)], axis=1)


def attend(layer, scalars, count, x, own, peer):
    split = isinstance(x, tuple)
    layers, width, half = own["w_query"].shape
    slots = 2 * x[0].shape[1] if split else x.shape[0]
    steps = half // PAIR
    act = columns(slots, PAIR)
    ins = [(my_row(a), a) for a in x] if split else [(whole(slots, width), x)]
    for name in ("w_query", "w_key", "w_value"):
        ins += [layer_columns(layer, own[name], PAIR), layer_columns(layer, peer[name], PAIR)]
    ins += [(columns(layers, PAIR), own["b_query"]), (columns(layers, PAIR), peer["biases"])]
    ins += [(columns(layers, PAIR), own["b_value"]), (columns(layers, PAIR, steps), peer["biases"])]
    outs = [(act, (slots, half), BF)] * 8
    outs += [(pl.BlockSpec((None, 8, slots), lambda i, *s: (i, 0, 0)), (steps, 8, slots), F32)]
    if split:
        outs += [(whole(slots, width), (slots, width), BF)]
    kernel = functools.partial(attend_kernel, layer, count, split)
    return run(kernel, steps, scalars, ins, outs, [pltpu.VMEM((slots, slots), F32)], 32, True)


def normalize(r):
    mean = jnp.mean(r, axis=1, keepdims=True)
    c = r - mean
    rstd = lax.rsqrt(jnp.mean(c * c, axis=1, keepdims=True) + 1e-12)
    return c * rstd, rstd


def norm_back(dy, n, rstd, gain):
    gdy = dy * gain
    return (
        gdy - jnp.mean(gdy, axis=1, keepdims=True) - n * jnp.mean(gdy * n, axis=1, keepdims=True)
    ) * rstd


def colsum(v):
    return jnp.sum(v.astype(F32), axis=0, keepdims=True)


def norm_back_store(dy, n, rstd, gain, dr, low, sums):
    r = norm_back(dy, n, rstd, gain)
    lowv = r.astype(BF)
    dr[...] = r
    low[...] = lowv
    sums[...] = jnp.concatenate(
        [colsum(dy * n), colsum(dy), colsum(lowv), jnp.zeros((5, dy.shape[1]), F32)], axis=0
    )


def feed_kernel(layer, last, scalars, *refs):
    (x, co, cp, woo, wop, b_out, g1, s1, wuo, wup, wdo, wdp, buo, bup, b_down, g2, s2) = refs[:17]
    rest = list(refs[17:])
    cots = [rest.pop(0) for _ in range(2 if last else 0)]
    (n1, rstd1, hlow, acto, actp, gpo, gpp, y, a, b, c, h, acc) = rest
    step = pl.program_id(0)

    @pl.when(step == 0)
    def _():
        att = nt(beside(co, cp), beside(woo, wop)) + row_of(b_out, layer)
        n, rstd = normalize(x[...].astype(F32) + att)
        n1[...] = n
        rstd1[...] = rstd
        hv = n * row_of(g1, layer) + row_of(s1, layer)
        h[...] = hv
        hlow[...] = hv.astype(BF)
        acc[...] = jnp.zeros_like(acc)

    u = nn(hlow[...], beside(wuo, wup)) + both(buo, bup, layer)
    cdf = 0.5 * (1.0 + lax.erf(u * 0.7071067811865476))
    act = (u * cdf).astype(BF)
    slope = (cdf + u * (jnp.exp(u * u * -0.5) * 0.3989422804014327)).astype(BF)
    acto[...] = act[:, :CHUNK]
    actp[...] = act[:, CHUNK:]
    gpo[...] = slope[:, :CHUNK]
    gpp[...] = slope[:, CHUNK:]
    acc[...] += nt(act, beside(wdo, wdp))

    @pl.when(step == pl.num_programs(0) - 1)
    def _():
        n, rstd = normalize(h[...] + (acc[...] + row_of(b_down, layer)))
        result = (n * row_of(g2, layer) + row_of(s2, layer)).astype(BF)
        if last:
            y[0, :, :] = result[: result.shape[0] // 2]
            y[1, :, :] = result[result.shape[0] // 2 :]
        else:
            y[...] = result
        if last:
            dy = jnp.concatenate([r[...] for r in cots], axis=0).astype(F32)
            norm_back_store(dy, n, rstd, row_of(g2, layer), a, b, c)
        else:
            a[...] = n
            b[...] = rstd


def feed(layer, scalars, x, ctx_own, ctx_peer, own, peer, cotangent):
    last = cotangent is not None
    layers, width, half = own["w_query"].shape
    slots = x.shape[0]
    ff = own["w_up"].shape[2]
    full = whole(slots, width)
    vec = whole(layers, width)
    act = columns(slots, CHUNK)
    part = whole(slots, half)
    ins = [(full, x), (part, ctx_own), (part, ctx_peer), layer_whole(layer, own["w_out"]), layer_whole(layer, peer["w_out"])]
    ins += [(vec, own[n]) for n in ("b_out", "first_gain", "first_shift")]
    for name in ("w_up", "w_down"):
        ins += [layer_columns(layer, own[name], CHUNK), layer_columns(layer, peer[name], CHUNK)]
    ins += [(columns(layers, CHUNK), own["b_up"]), (columns(layers, CHUNK, 2 * half // CHUNK), peer["biases"])]
    ins += [(vec, own[n]) for n in ("b_down", "second_gain", "second_shift")]
    if last:
        ins += [(my_row(a), a) for a in cotangent]
    outs = [(full, (slots, width), F32), (whole(slots, 1), (slots, 1), F32), (full, (slots, width), BF)]
    outs += [(act, (slots, ff), BF)] * 4
    halves = (2, slots // 2, width)
    outs += [(whole(*halves), halves, BF) if last else (full, (slots, width), BF)]
    outs += [(full, (slots, width), F32)]
    if last:
        outs += [(full, (slots, width), BF), (whole(8, width), (8, width), F32)]
    else:
        outs += [(whole(slots, 1), (slots, 1), F32), (whole(8, 128), (8, 128), F32)]
    scratch = [pltpu.VMEM((slots, width), F32)] * 2
    return run(functools.partial(feed_kernel, layer, last), ff // CHUNK, scalars, ins, outs, scratch, 40, True)


def feed_back_kernel(layer, scalars, *refs):
    (dff, dr2, wdo, wdp, wuo, wup, gpo, gpp, n1, rstd1, g1) = refs[:11]
    (gbuo, gbup, dr1, datt, sums, acc) = refs[-6:]
    pieces = refs[11:-6]
    step = pl.program_id(0)
    dact = nn(dff[...], beside(wdo, wdp))
    du = (dact * beside(gpo, gpp).astype(F32)).astype(BF)
    for p in range(len(pieces) // 2):

        @pl.when(step // 2 == p)
        def _(p=p):
            pieces[2 * p][...] = du[:, :CHUNK]
            pieces[2 * p + 1][...] = du[:, CHUNK:]

    total = colsum(du)
    gbuo[...] = total[:, :CHUNK]
    gbup[...] = total[:, CHUNK:]
    part = nt(du, beside(wuo, wup))

    @pl.when(step == 0)
    def _():
        acc[...] = dr2[...] + part

    @pl.when(step > 0)
    def _():
        acc[...] += part

    @pl.when(step == pl.num_programs(0) - 1)
    def _():
        norm_back_store(acc[...], n1[...], rstd1[...], row_of(g1, layer), dr1, datt, sums)


def feed_back(layer, scalars, dff, dr2, own, peer, slope_own, slope_peer, n1, rstd1):
    slots, width = dff.shape
    ff = own["w_up"].shape[2]
    act = columns(slots, CHUNK)
    full = whole(slots, width)
    ins = [(full, dff), (full, dr2)]
    for name in ("w_down", "w_up"):
        ins += [layer_columns(layer, own[name], CHUNK), layer_columns(layer, peer[name], CHUNK)]
    ins += [(act, slope_own), (act, slope_peer), (full, n1), (whole(slots, 1), rstd1)]
    ins += [(whole(*own["first_gain"].shape), own["first_gain"])]
    outs = []
    for p in range(ff // CHUNK // 2):
        piece = pl.BlockSpec((slots, CHUNK), lambda i, *s, p=p: (0, jnp.clip(i - 2 * p, 0, 1)))
        outs += [(piece, (slots, 2 * CHUNK), BF)] * 2
    outs += [(columns(1, CHUNK), (1, ff), F32)] * 2
    outs += [(full, (slots, width), F32), (full, (slots, width), BF), (whole(8, width), (8, width), F32)]
    scratch = [pltpu.VMEM((slots, width), F32)]
    return run(functools.partial(feed_back_kernel, layer), ff // CHUNK, scalars, ins, outs, scratch, 36, True)


def attend_back_kernel(layer, count, above, scalars, *refs):
    (datt, dr1, woo, wop, wqo, wqp, wko, wkp, wvo, wvp, qo, qp, ko, kp, vo, vp, lse) = refs[:17]
    sums1, sums2, gbuo, gbup = refs[17:21]
    rest = list(refs[21:])
    upper = [rest.pop(0) for _ in range(2)] if above else None
    n2, rstd2, gain = (rest.pop(0) for _ in range(3)) if layer else (None,) * 3
    dqo, dqp, dko, dkp, dvo, dvp, mine, theirs = rest[:8]
    bias = rest[-1]
    step = pl.program_id(0)
    slots, half = dqo.shape[0], woo.shape[1] * 3
    dx = rest[8]

    @pl.when(step == 0)
    def _():
        _, live = segments(scalars, count, slots, 0)
        segment, _ = segments(scalars, count, slots, 1)
        bias[...] = jnp.where(segment == live, 0.0, -1e9)
        rows = jnp.concatenate([sums1[0:3, :], sums2[0:3, :]], axis=0)
        for i, (pack, gbu) in enumerate(((mine, gbuo), (theirs, gbup))):
            width = pack.shape[1]
            pack[:16, :] = jnp.concatenate(
                [rows, gbu[:, :width], gbu[:, width:], jnp.zeros((8, width), F32)], axis=0
            )
            if above:
                pack[16:, :] = upper[i][...]

    dctx = nn(datt[...], beside(woo, wop)).astype(BF)
    first = lax.broadcasted_iota(jnp.int32, (1, PAIR), 1) < DH
    grads = []
    for pair, (qr, kr, vr, dqr, dkr, dvr, pack) in enumerate(
        ((qo, ko, vo, dqo, dko, dvo, mine), (qp, kp, vp, dqp, dkp, dvp, theirs))
    ):
        qq, kk, vv = qr[...], kr[...], vr[...]
        do = dctx[:, pair * PAIR : (pair + 1) * PAIR]
        dq_t, dk, dv = 0.0, 0.0, 0.0
        for head in range(2):
            sel = first if head == 0 else ~first
            qm = (jnp.where(sel, qq, jnp.zeros_like(qq)) * 0.125).astype(BF)
            km = (jnp.where(sel, kk, jnp.zeros_like(kk)) * 0.125).astype(BF)
            dom = jnp.where(sel, do, jnp.zeros_like(do))
            at = 2 * pair + head
            p = jnp.exp(nt(kk, qm) + bias[...] - lse[at : at + 1, :])
            dp = nt(vv, dom)
            delta = jnp.sum(p * dp, axis=0, keepdims=True)
            ds = (p * (dp - delta)).astype(BF)
            dv += nn(p.astype(BF), dom)
            dk += nn(ds, qm)
            dq_t += nn(km.T, ds)
        dq = dq_t.T.astype(BF)
        dk = dk.astype(BF)
        dv = dv.astype(BF)
        dqr[...] = dq
        dkr[...] = dk
        dvr[...] = dv
        pack[8:9, pl.ds(pl.multiple_of(step * PAIR, PAIR), PAIR)] = colsum(dq)
        pack[8:9, pl.ds(pl.multiple_of(step * PAIR + half_of(pack), PAIR), PAIR)] = colsum(dv)
        grads.append((dq, dk, dv))
    back = jnp.concatenate([g[i] for i in range(3) for g in grads], axis=1)
    part = nt(back, beside(wqo, wqp, wko, wkp, wvo, wvp))

    @pl.when(step == 0)
    def _():
        dx[...] = dr1[...] + part

    @pl.when(step > 0)
    def _():
        dx[...] += part

    if layer:
        dff, sums = rest[9:11]

        @pl.when(step == pl.num_programs(0) - 1)
        def _():
            norm_back_store(dx[...], n2[...], rstd2[...], row_of(gain, layer - 1), dx, dff, sums)

    else:

        @pl.when(step == pl.num_programs(0) - 1)
        def _():
            rest[9][...] = dx[...][slots // 2 :, :].astype(BF)


def half_of(pack):
    return pack.shape[1] // 2


def attend_back(layer, scalars, count, datt, dr1, own, peer, saved, lse, sums, above, below):
    slots, width = datt.shape
    half = own["w_query"].shape[2]
    steps = half // PAIR
    act = columns(slots, PAIR)
    full = whole(slots, width)
    ins = [(full, datt), (full, dr1)]
    for name in ("w_out", "w_query", "w_key", "w_value"):
        ins += [layer_columns(layer, own[name], PAIR), layer_columns(layer, peer[name], PAIR)]
    ins += [(act, a) for a in saved] + [(pl.BlockSpec((None, 8, slots), lambda i, *s: (i, 0, 0)), lse)]
    ins += [(whole(*a.shape), a) for a in (*sums, *above, *below)]
    packed = (16 * (own["w_query"].shape[0] - layer), width)
    outs = [(act, (slots, half), BF)] * 6 + [(whole(*packed), packed, F32)] * 2
    outs += [(full, (slots, width), F32)]
    if layer:
        outs += [(full, (slots, width), BF), (whole(8, width), (8, width), F32)]
    else:
        outs += [(whole(slots // 2, width), (slots // 2, width), BF)]
    kernel = functools.partial(attend_back_kernel, layer, count, bool(above))
    return run(kernel, steps, scalars, ins, outs, [pltpu.VMEM((slots, slots), F32)], 40, True)


def halves_of(value, bit, scalars, left, base):
    axis = left.index(bit)
    rows, width = value.shape
    cut = value.reshape(1 << axis, 2, rows >> (axis + 1), width)
    mine = (scalars[base] >> bit) & 1
    low, high = cut[:, 0].reshape(rows // 2, width), cut[:, 1].reshape(rows // 2, width)
    return jnp.where(mine == 0, low, high), jnp.where(mine == 0, high, low)


def weight_kernel(plan, left, scalars, *refs):
    step = pl.program_id(0)
    pieces = sum(len(p) for _, p in plan)
    operands, rest = refs[: 4 * pieces], refs[4 * pieces :]
    outs, (lt, right) = rest[:-2], rest[-2:]
    slots = operands[0].shape[0]
    n = 0
    for g, (bit, parts) in enumerate(plan):
        column = 0
        for start, steps, block, fresh in parts:
            lo, lp, ro, rp = operands[4 * n : 4 * n + 4]
            n += 1
            if fresh:

                @pl.when(step == start)
                def _(lo=lo, lp=lp):
                    lt[:, :slots] = lo[...].T
                    lt[:, slots:] = lp[...].T

            @pl.when((step >= start) & (step < start + steps))
            def _(ro=ro, rp=rp, block=block, start=start, column=column, g=g, bit=bit):
                right[:slots, :block] = ro[...]
                right[slots:, :block] = rp[...]
                value = nn(lt[...], right[:, :block])
                at = pl.ds(pl.multiple_of(column + (step - start) * block, 128), block)
                if bit is None:
                    outs[g][:, at] = value.astype(BF)
                else:
                    keep, send = halves_of(value, bit, scalars, left, 1)
                    outs[2 * g][:, at] = keep.astype(BF)
                    outs[2 * g + 1][:, at] = send.astype(BF)

            column += steps * block


def weight_grads(scalars, groups, size, block):
    bits = size.bit_length() - 1
    left = list(range(bits - 1, -1, -1))
    plan, ins, outs, pins = [], [], [], []
    at = 0
    before = None
    slots, width = groups[0][1][0][0].shape
    split = (width // size) % 16 == 0
    for order, parts in groups:
        pieces, total = [], 0
        for lo, lp, ro, rp in parts:
            blk = min(block, ro.shape[1])
            steps = ro.shape[1] // blk
            pieces.append((at, steps, blk, lo is not before))
            before = lo
            spec = pl.BlockSpec((slots, blk), lambda i, *s, a=at, n=steps: (0, jnp.clip(i - a, 0, n - 1)))
            pins += [len(ins), len(ins) + 2]
            ins += [(whole(slots, width), lo), (whole(slots, width), lp), (spec, ro), (spec, rp)]
            at += steps
            total += ro.shape[1]
        plan.append((order[0] if split else None, pieces))
        rows = width // 2 if split else width
        outs += [(whole(rows, total), (rows, total), BF)] * (2 if split else 1)
    scratch = [pltpu.VMEM((width, 2 * slots), BF), pltpu.VMEM((2 * slots, block), BF)]
    made = run(functools.partial(weight_kernel, plan, left), at, scalars, ins, outs, scratch, 40, pins)
    if split:
        return [Scatter(scalars, o, size, made[2 * g], made[2 * g + 1]) for g, (o, _) in enumerate(groups)]
    return [Scatter(scalars, o, size, None, made[g]) for g, (o, _) in enumerate(groups)]


def add_kernel(plan, scalars, *refs):
    ins, outs = refs[: 2 * len(plan)], refs[2 * len(plan) :]
    for i, (bit, left) in enumerate(plan):
        value = ins[2 * i][...].astype(F32) + ins[2 * i + 1][...].astype(F32)
        if bit is None:
            outs[2 * i][...] = value
        else:
            kept, send = halves_of(value, bit, scalars, left, 1)
            outs[2 * i][...] = kept.astype(BF)
            outs[2 * i + 1][...] = send.astype(BF)


def land(*scatters):
    if not scatters:
        return
    unit = scatters[0].keep.shape[0] >> len(scatters[0].order)
    if unit % 16:
        for f in scatters:
            f.part((f.keep.astype(F32) + f.value.astype(F32)).astype(BF))
        return
    steps = 3 if max(f.keep.size for f in scatters) > 300000 else 1
    ins, outs, plan = [], [], []
    for f in scatters:
        rows, width = f.keep.shape
        block = columns(rows, width // steps)
        ins += [(block, f.keep), (block, f.value)]
        outs += [(columns(rows // 2, width // steps), (rows // 2, width), BF)] * 2
        plan.append((f.order[0], list(f.left)))
    made = run(functools.partial(add_kernel, plan), steps, scatters[0].scalars, ins, outs, [], 32)
    for i, f in enumerate(scatters):
        f.keep, f.value = made[2 * i : 2 * i + 2]


class Scatter:
    def __init__(self, scalars, order, size, keep, send):
        bits = size.bit_length() - 1
        self.scalars, self.size = scalars, size
        self.order = [b for b in order if b < bits] + list(range(4, bits))
        self.left = list(range(bits - 1, -1, -1))
        self.keep, self.value = keep, send
        if keep is None:
            self.part(send)

    def part(self, value):
        bit = self.order[0]
        axis = self.left.index(bit)
        rows, width = value.shape
        cut = value.reshape(1 << axis, 2, rows >> (axis + 1), width)
        mine = (self.scalars[1] >> bit) & 1
        self.keep = lax.dynamic_index_in_dim(cut, mine, 1, keepdims=False).reshape(rows // 2, width)
        self.value = lax.dynamic_index_in_dim(cut, 1 - mine, 1, keepdims=False).reshape(rows // 2, width)

    def launch(self):
        bit = self.order.pop(0)
        self.left.remove(bit)
        self.value = flip(self.value, bit, self.size)
        return self


def last_kernel(count, scalars, *refs):
    ins, outs = refs[: 2 * count], refs[2 * count :]
    layers = outs[0].shape[0]
    at = 0
    for out in outs:
        column = 0
        while column < out.shape[2]:
            width = ins[at].shape[1]
            for layer in range(layers):
                keep, got = ins[at : at + 2]
                at += 2
                out[layer, :, column : column + width] = keep[...].astype(F32) + got[...].astype(F32)
            column += width


def last_sums(scalars, parts, widths):
    arrays = [a for pair in parts for a in pair]
    rows = arrays[0].shape[0]
    layers = 2
    return run(
        functools.partial(last_kernel, len(parts)), 1, scalars,
        [(whole(*a.shape), a) for a in arrays],
        [(whole(layers, rows, w), (layers, rows, w), F32) for w in widths], [], 24, "out",
    )


def sum_kernel(scalars, left, right, out):
    out[...] = left[...] + right[...]


def small_kernel(layers, scalars, mine, got, gbq, gbv, gbu, *vectors):
    width = mine.shape[1]
    for layer in range(layers):
        total = mine[16 * layer : 16 * layer + 16, :] + got[16 * layer : 16 * layer + 16, :]
        row = slice(layer, layer + 1)
        for i, out in enumerate(vectors):
            out[row, :] = total[i : i + 1, :]
        gbu[row, :width] = total[6:7, :]
        gbu[row, width:] = total[7:8, :]
        gbq[row, :] = total[8:9, : width // 2]
        gbv[row, :] = total[8:9, width // 2 :]


def swap(value):
    return lax.ppermute(value, "mp", [(0, 1), (1, 0)])


def flip(value, bit, size):
    return lax.ppermute(value, "dp", [(i, i ^ (1 << bit)) for i in range(size)])


NAMES = (
    "w_query", "b_query", "w_key", "w_value", "b_value", "w_out", "b_out", "first_gain", "first_shift",
    "w_up", "b_up", "w_down", "b_down", "second_gain", "second_shift",
)
XY, YX, ZX = (0, 1, 2, 3), (1, 0, 2, 3), (2, 3, 0, 1)


def shards(dp, tokens, lengths, cotangent, *given):
    held = dict(zip(NAMES, given, strict=True))
    layers, width, half = held["w_query"].shape
    ff = held["w_up"].shape[2]
    slots = 2 * tokens.shape[1]
    count = lengths.shape[1]
    me = lax.axis_index("mp")
    scalars = jnp.concatenate([me[None], lengths.reshape(-1)]).astype(jnp.int32)
    place = jnp.stack([me, lax.axis_index("dp")]).astype(jnp.int32)

    def give_row(mine, other):
        other = swap(other).astype(mine.dtype)
        return jnp.stack([jnp.where(me == 0, mine, other), jnp.where(me == 0, other, mine)])

    Order.last, Order.pending = None, []
    biases = swap(jnp.concatenate([held["b_query"], held["b_value"], held["b_up"]], axis=1))
    x = (tokens, swap(tokens))
    early = {n: swap(held[n]) for n in ("w_query", "w_key", "w_value")}
    names = ("w_out", "w_up", "w_down")
    pieces, early, biases, x = lax.optimization_barrier(([held[n][:1] for n in names], early, biases, x))
    first = {n: swap(p) for n, p in zip(names, pieces, strict=True)}
    pieces, cot, first = lax.optimization_barrier(([held[n] for n in names], cotangent, first))
    later = {n: swap(p) for n, p in zip(names, pieces, strict=True)}
    cot = (cot, swap(cot))
    peers = [{"biases": biases, **early, **(later if layer else first)} for layer in range(layers)]

    kept = []
    for layer in range(layers):
        att = attend(layer, scalars, count, x, held, peers[layer])
        x = att[9] if layer == 0 else x
        fed = feed(
            layer, scalars, x, att[6], att[7], held, peers[layer], cot if layer == layers - 1 else None
        )
        kept.append((x, att, fed))
        x = fed[7]

    groups = [None] * layers
    dr2, dff, sums2 = kept[-1][2][8:11]

    def step(*scatters):
        scatters = [f for f in scatters if f.order]
        land(*scatters)
        for f in scatters:
            f.launch()

    flying, waiting, pack = [], None, ()
    for layer in reversed(range(layers)):
        x_in, att, fed = kept[layer]
        (ctx_own, ctx_peer, lse) = att[6:9]
        (n1, rstd1, hlow, act_own, act_peer, slope_own, slope_peer) = fed[:7]
        dff_peer = swap(dff)
        act_peer = swap(act_peer)
        if not flying:
            (down,) = weight_grads(place, [(XY, [(dff, dff_peer, act_own, act_peer)])], dp, 512)
            down.launch()
        *du, gbu_own, gbu_peer, dr1, datt, sums1 = feed_back(
            layer, scalars, dff, dr2, held, peers[layer], slope_own, slope_peer, n1, rstd1
        )
        h_peer = swap(hlow)
        if flying:
            step(flying[1])
            (down,) = weight_grads(place, [(XY, [(dff, dff_peer, act_own, act_peer)])], dp, 512)
            down.launch()
            (waiting,) = weight_grads(place, [(ZX, waiting)], dp, 384)
            waiting.launch()
        (up,) = weight_grads(
            place,
            [(YX, [(hlow, h_peer, du[2 * p], swap(du[2 * p + 1])) for p in range(len(du) // 2)])],
            dp, 512,
        )
        up.launch()
        step(*flying[:1])
        below = (*kept[layer - 1][2][8:10], held["second_gain"]) if layer else ()
        back = attend_back(
            layer, scalars, count, datt, dr1, held, peers[layer], att[:6], lse,
            (sums1, sums2, gbu_own, gbu_peer), pack, below,
        )
        dqo, dqp, dko, dkp, dvo, dvp, *pack = back[:8]
        x_peer = swap(x_in)
        parts = [(datt, swap(datt), ctx_own, swap(ctx_peer))]
        parts += [(x_in, x_peer, o, swap(p)) for o, p in ((dqo, dqp), (dko, dkp), (dvo, dvp))]
        step(down)
        if layer:
            dr2, dff, sums2 = back[8:11]
            flying = [down, up]
            waiting = parts
        else:
            step(flying[1], waiting)
            rest = weight_grads(place, [(XY, parts[:2]), (YX, parts[2:])], dp, 384)
            for f in rest:
                f.launch()
        groups[layer] = [down, up, None]
    groups[0][2] = rest
    groups[1][2] = [waiting]

    dx = back[8]
    encoded = give_row(x[0], x[1])
    token_grad = give_row(dx[: slots // 2], back[9])

    bits = dp.bit_length() - 1
    left = list(range(bits - 1, -1, -1))
    total, got = pack[0], swap(pack[1])

    def small_step(total, got):
        if not left:
            return total, got
        whole_one = whole(*total.shape)
        (total,) = run(
            sum_kernel, 1, place, [(whole_one, total), (whole_one, got)], [(whole_one, total.shape, F32)], [], 8
        )
        return total, flip(total, left.pop(0), dp)

    down, up, rest = groups[0]
    step(up)
    total, got = small_step(total, got)
    flying = [*groups[1][:2], *groups[1][2]]
    step(*flying)
    while left or any(f.order for f in (down, up, *flying, *rest)):
        step(*rest)
        total, got = small_step(total, got)
        step(down, up)
        step(*flying)

    def pairs(pick):
        return [(f.keep, f.value) for f in (pick(groups[layer]) for layer in range(layers))]

    (gwd,) = last_sums(place, pairs(lambda g: g[0]), [ff])
    (gwu,) = last_sums(place, pairs(lambda g: g[1]), [ff])
    tail = []
    for i in range(4):
        for layer in range(layers):
            per = 4 // len(groups[layer][2])
            f = groups[layer][2][i // per]
            at = slice(i % per * half, (i % per + 1) * half)
            tail.append((f.keep[:, at], f.value[:, at]))
    gwo, gwq, gwk, gwv = last_sums(place, tail, [half] * 4)
    shapes = [half, half, ff] + [width] * 6
    gbq, gbv, gbu, gfg, gfs, gbo, gsg, gss, gbd = run(
        functools.partial(small_kernel, layers), 1, place,
        [(whole(*total.shape), total), (whole(*got.shape), got)],
        [(whole(layers, n), (layers, n), F32) for n in shapes], [], 16, "out",
    )
    return (
        encoded, token_grad, gwq, gbq, gwk, gwv, gbv, gwo, gbo, gfg, gfs, gwu, gbu, gwd, gbd, gsg, gss,
    )


def solution(mesh):
    cols, mats, rep = P(None, "mp"), P(None, None, "mp"), P()
    placed = (
        P("dp", "mp", None), P("dp", None), P("dp", "mp", None),
        mats, cols, mats, mats, cols, mats, rep, rep, rep, mats, cols, mats, rep, rep, rep,
    )
    grads = P(None, "dp", "mp")
    return jax.shard_map(
        functools.partial(shards, mesh.shape["dp"]),
        mesh=mesh,
        in_specs=placed,
        out_specs=(
            P("dp", "mp", None), P("dp", "mp", None), grads, cols, grads, grads, cols,
            grads, rep, rep, rep, grads, cols, grads, rep, rep, rep,
        ),
        check_vma=False,
    )
```

```python
import functools

import jax
import jax.numpy as jnp
from jax import lax
from jax.experimental import pallas as pl
from jax.experimental.pallas import tpu as pltpu
from jax.sharding import PartitionSpec as P

DH = 64
QSLOT = 32
BF = jnp.bfloat16
F32 = jnp.float32
PAIR = 2 * DH
CHUNK = 512


def nn(left, right):
    return lax.dot_general(left, right, (((1,), (0,)), ((), ())), preferred_element_type=F32)


def nt(left, right):
    return lax.dot_general(left, right, (((1,), (1,)), ((), ())), preferred_element_type=F32)


def tn(left, right):
    return lax.dot_general(left, right, (((0,), (0,)), ((), ())), preferred_element_type=F32)


def beside(*refs):
    return jnp.concatenate([r[...] for r in refs], axis=1)


def whole(*shape):
    return pl.BlockSpec(shape, lambda i, *s: (0,) * len(shape))


def columns(rows, width, start=0):
    return pl.BlockSpec((rows, width), lambda i, *s: (0, start + i))


def layer_columns(layer, array, width):
    at = layer if array.shape[0] > 1 else 0
    return pl.BlockSpec((None, array.shape[1], width), lambda i, *s: (at, 0, i)), array


def layer_whole(layer, array):
    at = layer if array.shape[0] > 1 else 0
    return pl.BlockSpec((None, *array.shape[1:]), lambda i, *s: (at, 0, 0)), array


def my_row(array):
    return pl.BlockSpec((None, *array.shape[1:]), lambda i, s: (s[0], 0, 0))


def sds(shape, dtype):
    return jax.ShapeDtypeStruct(shape, dtype)


class Order:
    last = None
    also = ()


def run(kernel, grid, scalars, ins, outs, scratch, megabytes, pinned=False, micros=0.05):
    shape = pltpu.HBM if pinned in (True, "out") else sds
    arrays = [a for _, a in ins]
    kept = range(len(arrays)) if pinned is True else pinned if isinstance(pinned, list) else ()
    for i in kept:
        arrays[i] = pltpu.with_memory_space_constraint(arrays[i], pltpu.HBM)
    extra = [pltpu.with_memory_space_constraint(a, pltpu.HBM) for a in Order.also]
    extra += [] if Order.last is None else [Order.last]
    Order.also = ()
    count = 1 + len(ins)

    def body(*refs):
        kernel(*refs[:count], *refs[count + len(extra) :])

    made = pl.pallas_call(
        body,
        grid_spec=pltpu.PrefetchScalarGridSpec(
            num_scalar_prefetch=1,
            grid=(grid,),
            in_specs=[b for b, _ in ins] + [pl.BlockSpec(memory_space=pl.ANY)] * len(extra),
            out_specs=[b for b, _, _ in outs],
            scratch_shapes=scratch,
        ),
        out_shape=[shape(dims, dtype) for _, dims, dtype in outs],
        compiler_params=pltpu.CompilerParams(vmem_limit_bytes=megabytes * 1024 * 1024),
        cost_estimate=pl.CostEstimate(flops=1000 + int(1e9 * micros), transcendentals=0, bytes_accessed=1000),
    )(scalars, *arrays, *extra)
    Order.last = made[-1]
    if shape is pltpu.HBM:
        Order.last = pltpu.with_memory_space_constraint(made[-1], pltpu.HBM)
    return made


def row_of(ref, layer):
    return ref[layer : layer + 1, :].astype(F32)


def segments(scalars, count, slots, dim):
    shape = (slots, 1) if dim == 0 else (1, slots)
    slot = lax.broadcasted_iota(jnp.int32, shape, dim) + scalars[0] * (slots // 2)
    slot = jnp.where(slot >= slots, slot - slots, slot)
    base = 1 + scalars[0] * count
    shift = jnp.where(scalars[base + 1] > 0, QSLOT.bit_length() - 1, slots.bit_length() - 1)
    segment = lax.shift_right_logical(slot, jnp.broadcast_to(shift, shape))
    inside = slot - lax.shift_left(segment, jnp.broadcast_to(shift, shape))
    length = jnp.zeros(shape, jnp.int32)
    for k in range(count):
        length = jnp.where(segment == k, scalars[base + k], length)
    return segment, jnp.where(inside < length, segment, -1)


def attend_kernel(layer, count, split, scalars, *refs):
    refs = list(refs)
    xs = [refs.pop(0) for _ in range(2 if split else 1)]
    qkv, co, cp, lse = refs[10:14]
    bias = refs[-1]
    x = refs[14] if split else xs[0]
    slots = co.shape[0]

    @pl.when(pl.program_id(0) == 0)
    def _():
        segment, _ = segments(scalars, count, slots, 0)
        _, live = segments(scalars, count, slots, 1)
        bias[...] = jnp.where(segment == live, 0.0, -1e9)
        if split:
            x[...] = jnp.concatenate([r[...] for r in xs], axis=0)

    attend_step(layer, x[...], refs[:10], qkv, (co, cp), lse, bias, 0)


def attend_step(layer, xv, operands, qkv, ctx, lse, bias, column):
    wqo, wqp, wko, wkp, wvo, wvp, bqo, bqp, bvo, bvp = operands
    q = (nn(xv, beside(wqo, wqp)) + both(bqo, bqp, layer)).astype(BF)
    k = nn(xv, beside(wko, wkp)).astype(BF)
    v = (nn(xv, beside(wvo, wvp)) + both(bvo, bvp, layer)).astype(BF)
    first = lax.broadcasted_iota(jnp.int32, (1, PAIR), 1) < DH
    lse[...] = jnp.zeros_like(lse)
    for pair, cr in enumerate(ctx):
        at = slice(pair * PAIR, (pair + 1) * PAIR)
        qq, kk, vv = q[:, at], k[:, at], v[:, at]
        for i, part in enumerate((qq, kk, vv)):
            qkv[2 * i + pair, :, :] = part
        outs, peaks = [], []
        for head in range(2):
            mine = first if head == 0 else ~first
            qm = jnp.where(mine, qq, jnp.zeros_like(qq)) * 0.125
            s = nt(qm.astype(BF), kk) + bias[...]
            peak = jnp.max(s, axis=1, keepdims=True)
            e = jnp.exp(s - peak).astype(BF)
            outs.append(nn(e, jnp.where(mine, vv, jnp.ones_like(vv))))
            peaks.append(peak)
        total = pltpu.roll(jnp.where(first, outs[1], outs[0]), DH, 1)
        cr[:, pl.ds(column, PAIR)] = (jnp.where(first, outs[0], outs[1]) / total).astype(BF)
        logs = jnp.where(first, peaks[0], peaks[1]) + jnp.log(total)
        flat = logs.T
        lse[2 * pair : 2 * pair + 1, :] = flat[0:1, :]
        lse[2 * pair + 1 : 2 * pair + 2, :] = flat[DH : DH + 1, :]


def triple(count, slots):
    return pl.BlockSpec((count, slots, PAIR), lambda i, *s: (0, 0, i))


def both(own, peer, layer):
    return jnp.concatenate([row_of(own, layer), row_of(peer, layer)], axis=1)


def attend(layer, scalars, count, x, own, peer):
    split = isinstance(x, tuple)
    layers, width, half = own["w_query"].shape
    slots = 2 * x[0].shape[1] if split else x.shape[0]
    steps = half // PAIR
    act = columns(slots, PAIR)
    ins = [(my_row(a), a) for a in x] if split else [(whole(slots, width), x)]
    for name in ("w_query", "w_key", "w_value"):
        ins += [layer_columns(layer, own[name], PAIR), layer_columns(layer, peer[name], PAIR)]
    ins += [(columns(layers, PAIR), own["b_query"]), (columns(layers, PAIR, 4 * steps), peer["biases"])]
    ins += [(columns(layers, PAIR), own["b_value"]), (columns(layers, PAIR, 5 * steps), peer["biases"])]
    outs = [(triple(6, slots), (6, slots, half), BF)] + [(act, (slots, half), BF)] * 2
    outs += [(pl.BlockSpec((None, 8, slots), lambda i, *s: (i, 0, 0)), (steps, 8, slots), F32)]
    if split:
        outs += [(whole(slots, width), (slots, width), BF)]
    kernel = functools.partial(attend_kernel, layer, count, split)
    return run(kernel, steps, scalars, ins, outs, [pltpu.VMEM((slots, slots), F32)], 32, True)


def normalize(r):
    mean = jnp.mean(r, axis=1, keepdims=True)
    c = r - mean
    rstd = lax.rsqrt(jnp.mean(c * c, axis=1, keepdims=True) + 1e-12)
    return c * rstd, rstd


def norm_back(dy, n, rstd, gain):
    gdy = dy * gain
    return (
        gdy - jnp.mean(gdy, axis=1, keepdims=True) - n * jnp.mean(gdy * n, axis=1, keepdims=True)
    ) * rstd


def colsum(v):
    return jnp.sum(v.astype(F32), axis=0, keepdims=True)


def norm_back_store(dy, n, rstd, gain, low, sums):
    lowv = norm_back(dy, n, rstd, gain).astype(BF)
    low[:, :] = lowv
    sums[...] = jnp.concatenate(
        [colsum(dy * n), colsum(dy), colsum(lowv), jnp.zeros((5, dy.shape[1]), F32)], axis=0
    )


def gelu_step(low, up, up_bias):
    u = nn(low, up) + up_bias
    cdf = 0.5 * (1.0 + lax.erf(u * 0.7071067811865476))
    act = (u * cdf).astype(BF)
    return act, (cdf + u * (jnp.exp(u * u * -0.5) * 0.3989422804014327)).astype(BF)


def first_norm(layer, x, ctx, projection, b_out, g1, s1):
    n, rstd = normalize(x.astype(F32) + (nt(ctx, projection) + row_of(b_out, layer)))
    return n, rstd, n * row_of(g1, layer) + row_of(s1, layer)


def feed_kernel(layer, scalars, *refs):
    (x, co, cp, woo, wop, b_out, g1, s1, wuo, wup, wdo, wdp, buo, bup, b_down, g2, s2) = refs[:17]
    (n1, rstd1, hlow, acto, actp, gp, y, n2, rstd2, h, acc) = refs[17:]
    step = pl.program_id(0)

    @pl.when(step == 0)
    def _():
        n, rstd, hv = first_norm(layer, x[...], beside(co, cp), beside(woo, wop), b_out, g1, s1)
        n1[...] = n.astype(BF)
        rstd1[...] = rstd
        h[...] = hv
        hlow[...] = hv.astype(BF)
        acc[...] = jnp.zeros_like(acc)

    act, slope = gelu_step(hlow[...], beside(wuo, wup), both(buo, bup, layer))
    acto[...] = act[:, :CHUNK]
    actp[...] = act[:, CHUNK:]
    gp[0, :, :] = slope[:, :CHUNK]
    gp[1, :, :] = slope[:, CHUNK:]
    acc[...] += nt(act, beside(wdo, wdp))

    @pl.when(step == pl.num_programs(0) - 1)
    def _():
        n, rstd = normalize(h[...] + (acc[...] + row_of(b_down, layer)))
        y[...] = (n * row_of(g2, layer) + row_of(s2, layer)).astype(BF)
        n2[...] = n.astype(BF)
        rstd2[...] = rstd


def feed(layer, scalars, x, ctx_own, ctx_peer, own, peer):
    layers, width, half = own["w_query"].shape
    slots = x.shape[0]
    ff = own["w_up"].shape[2]
    full = whole(slots, width)
    one = whole(slots, 1)
    vec = whole(layers, width)
    act = columns(slots, CHUNK)
    part = whole(slots, half)
    ins = [(full, x), (part, ctx_own), (part, ctx_peer), layer_whole(layer, own["w_out"]), layer_whole(layer, peer["w_out"])]
    ins += [(vec, own[n]) for n in ("b_out", "first_gain", "first_shift")]
    for name in ("w_up", "w_down"):
        ins += [layer_columns(layer, own[name], CHUNK), layer_columns(layer, peer[name], CHUNK)]
    ins += [(columns(layers, CHUNK), own["b_up"]), (columns(layers, CHUNK), peer["biases"])]
    ins += [(vec, own[n]) for n in ("b_down", "second_gain", "second_shift")]
    outs = [(full, (slots, width), BF), (one, (slots, 1), F32), (full, (slots, width), BF)]
    outs += [(act, (slots, ff), BF)] * 2
    outs += [(pl.BlockSpec((2, slots, CHUNK), lambda i, *s: (0, 0, i)), (2, slots, ff), BF)]
    outs += [(full, (slots, width), BF), (full, (slots, width), BF), (one, (slots, 1), F32)]
    scratch = [pltpu.VMEM((slots, width), F32)] * 2
    return run(functools.partial(feed_kernel, layer), ff // CHUNK, scalars, ins, outs, scratch, 40, True)


class Loads:
    def __init__(self, sources, targets, sems):
        self.copies = [pltpu.make_async_copy(s, t, sems.at[i]) for i, (s, t) in enumerate(zip(sources, targets))]

    def start(self):
        for c in self.copies:
            c.start()

    def wait(self):
        for c in self.copies:
            c.wait()


def layer_of(ref, layer):
    return ref.at[layer if ref.shape[0] > 1 else 0]


def slope_step(chunk, low, gp, down, up, duo, dup, gbuo, gbup):
    du = (nn(low, down) * gp.astype(F32)).astype(BF)
    duo[...] = du[:, :CHUNK]
    dup[...] = du[:, CHUNK:]
    total = colsum(du)
    gbuo[:, chunk] = total[:, :CHUNK]
    gbup[:, chunk] = total[:, CHUNK:]
    return nt(du, up)


def columns_of(refs, chunk):
    return jnp.concatenate([r[:, chunk] for r in refs], axis=1)


def turn_kernel(layer, count, scalars, *refs):
    x, attention, weights, rest = refs[0], refs[1:11], refs[11:17], list(refs[17:])
    (b_out, g1, s1, buo, bup, b_down, g2, s2, cot_a, cot_b) = rest[:10]
    (qkv, co, cp, lse, hlow, acto, actp, y, gbuo, gbup, sums2, duo, dup, both_low, sums1) = rest[10:25]
    (bias, woo, wop, wuo, wup, wdo, wdp, gp, h, acc, n1, rstd1, sems) = rest[25:]
    dff, datt = both_low.at[0], both_low.at[1]
    step = pl.program_id(0)
    slots = co.shape[0]
    attending = co.shape[1] // PAIR
    feeding = gp.shape[2] // CHUNK
    loads = Loads([layer_of(w, layer) for w in weights], (woo, wop, wuo, wup, wdo, wdp), sems)

    @pl.when(step == 0)
    def _():
        loads.start()
        segment, _ = segments(scalars, count, slots, 0)
        _, live = segments(scalars, count, slots, 1)
        bias[...] = jnp.where(segment == live, 0.0, -1e9)

    @pl.when(step < attending)
    def _():
        attend_step(layer, x[...], attention, qkv, (co, cp), lse, bias, pl.multiple_of(step * PAIR, PAIR))

    @pl.when(step == attending)
    def _():
        loads.wait()
        n, rstd, hv = first_norm(layer, x[...], beside(co, cp), beside(woo, wop), b_out, g1, s1)
        n1[...] = n
        rstd1[...] = rstd
        h[...] = hv
        hlow[...] = hv.astype(BF)
        acc[...] = jnp.zeros_like(acc)

    @pl.when((step >= attending) & (step < attending + feeding))
    def _():
        chunk = pl.ds(pl.multiple_of((step - attending) * CHUNK, CHUNK), CHUNK)
        up_bias = jnp.concatenate([r[layer : layer + 1, chunk].astype(F32) for r in (buo, bup)], axis=1)
        act, slope = gelu_step(hlow[...], columns_of((wuo, wup), chunk), up_bias)
        acto[...] = act[:, :CHUNK]
        actp[...] = act[:, CHUNK:]
        gp[0, :, chunk] = slope[:, :CHUNK]
        gp[1, :, chunk] = slope[:, CHUNK:]
        acc[...] += nt(act, columns_of((wdo, wdp), chunk))

    @pl.when(step == attending + feeding - 1)
    def _():
        n, rstd = normalize(h[...] + (acc[...] + row_of(b_down, layer)))
        result = (n * row_of(g2, layer) + row_of(s2, layer)).astype(BF)
        y[0, :, :] = result[: slots // 2]
        y[1, :, :] = result[slots // 2 :]
        dy = jnp.concatenate([cot_a[...], cot_b[...]], axis=0).astype(F32)
        norm_back_store(dy, n, rstd, row_of(g2, layer), dff, sums2)
        acc[...] = dff[...].astype(F32)

    @pl.when(step >= attending + feeding)
    def _():
        chunk = pl.ds(pl.multiple_of((step - attending - feeding) * CHUNK, CHUNK), CHUNK)
        slope = jnp.concatenate([gp[0, :, chunk], gp[1, :, chunk]], axis=1)
        acc[...] += slope_step(
            chunk, dff[...], slope, columns_of((wdo, wdp), chunk), columns_of((wuo, wup), chunk),
            duo, dup, gbuo, gbup,
        )

    @pl.when(step == pl.num_programs(0) - 1)
    def _():
        norm_back_store(acc[...], n1[...], rstd1[...], row_of(g1, layer), datt, sums1)


def turn(layer, scalars, count, x, own, peer, cotangent):
    layers, width, half = own["w_query"].shape
    slots, ff = x.shape[0], own["w_up"].shape[2]
    attending, feeding = half // PAIR, ff // CHUNK

    def early(rows, start=0):
        return pl.BlockSpec((rows, PAIR), lambda i, *s: (0, start + jnp.clip(i, 0, attending - 1)))

    def early_weight(array):
        at = layer if array.shape[0] > 1 else 0
        return pl.BlockSpec((None, width, PAIR), lambda i, *s: (at, 0, jnp.clip(i, 0, attending - 1))), array

    full, vec = whole(slots, width), whole(layers, width)
    anywhere = pl.BlockSpec(memory_space=pl.ANY)
    ins = [(full, x)]
    for name in ("w_query", "w_key", "w_value"):
        ins += [early_weight(own[name]), early_weight(peer[name])]
    ins += [(early(layers), own["b_query"]), (early(layers, 4 * attending), peer["biases"])]
    ins += [(early(layers), own["b_value"]), (early(layers, 5 * attending), peer["biases"])]
    for name in ("w_out", "w_up", "w_down"):
        ins += [(anywhere, own[name]), (anywhere, peer[name])]
    ins += [(vec, own[n]) for n in ("b_out", "first_gain", "first_shift")]
    ins += [(whole(*a.shape), a) for a in (own["b_up"], peer["biases"])]
    ins += [(vec, own[n]) for n in ("b_down", "second_gain", "second_shift")]
    ins += [(my_row(a), a) for a in cotangent]
    late = pl.BlockSpec((slots, CHUNK), lambda i, *s: (0, jnp.clip(i - attending, 0, feeding - 1)))
    halves = (2, slots // 2, width)
    outs = [
        (pl.BlockSpec((6, slots, PAIR), lambda i, *s: (0, 0, jnp.clip(i, 0, attending - 1))), (6, slots, half), BF)
    ]
    outs += [(whole(slots, half), (slots, half), BF)] * 2
    outs += [
        (pl.BlockSpec((None, 8, slots), lambda i, *s: (jnp.clip(i, 0, attending - 1), 0, 0)), (attending, 8, slots), F32)
    ]
    outs += [(full, (slots, width), BF)] + [(late, (slots, ff), BF)] * 2 + [(whole(*halves), halves, BF)]
    outs += [(whole(1, ff), (1, ff), F32)] * 2 + [(whole(8, width), (8, width), F32)]
    latest = pl.BlockSpec((slots, CHUNK), lambda i, *s: (0, jnp.clip(i - attending - feeding, 0, feeding - 1)))
    outs += [(latest, (slots, ff), BF)] * 2
    outs += [(whole(2, slots, width), (2, slots, width), BF), (whole(8, width), (8, width), F32)]
    scratch = [pltpu.VMEM((slots, slots), F32)] + [pltpu.VMEM((width, half), BF)] * 2
    scratch += [pltpu.VMEM((width, ff), BF)] * 4 + [pltpu.VMEM((2, slots, ff), BF)]
    scratch += [pltpu.VMEM((slots, width), F32)] * 3 + [pltpu.VMEM((slots, 1), F32), pltpu.SemaphoreType.DMA((6,))]
    kernel = functools.partial(turn_kernel, layer, count)
    return run(kernel, attending + 2 * feeding, scalars, ins, outs, scratch, 56, True)


def attend_back_kernel(layer, count, above, scalars, *refs):
    rest = list(refs)

    def take(n):
        return [rest.pop(0) for _ in range(n)]

    datt, woo, wop, wqo, wqp, wko, wkp, wvo, wvp, qkv, lse, sums1, sums2, gbuo, gbup = take(15)
    upper = take(2) if above else None
    if layer:
        n2, rstd2, gain2, n1, rstd1, gain1 = take(6)
        sources = take(5)
    ours, others, mine, theirs = take(4)
    if layer:
        below2, duo, dup, below_gbuo, below_gbup, both_low, below1 = take(7)
        dff, below_datt = both_low.at[0], both_low.at[1]
    else:
        dx_own, dx_peer = take(2)
    dx, bias = take(2)
    step = pl.program_id(0)
    slots = datt.shape[0]
    attending = down_steps(mine)
    if layer:
        wuo, wup, wdo, wdp, gp, sems = take(6)
        loads = Loads(
            [*[layer_of(w, layer - 1) for w in sources[:4]], sources[4]], (wuo, wup, wdo, wdp, gp), sems
        )

    @pl.when(step == 0)
    def _():
        if layer:
            loads.start()
        _, live = segments(scalars, count, slots, 0)
        segment, _ = segments(scalars, count, slots, 1)
        bias[...] = jnp.where(segment == live, 0.0, -1e9)
        rows = jnp.concatenate([sums1[0:3, :], sums2[0:3, :]], axis=0)
        for i, (pack, gbu) in enumerate(((mine, gbuo), (theirs, gbup))):
            width = pack.shape[1]
            pack[:16, :] = jnp.concatenate(
                [rows, gbu[:, :width], gbu[:, width:], jnp.zeros((8, width), F32)], axis=0
            )
            if above:
                pack[16:, :] = upper[i][...]
        dx[...] = datt[...].astype(F32)

    @pl.when(step < attending)
    def _():
        dctx = nn(datt[...], beside(woo, wop)).astype(BF)
        first = lax.broadcasted_iota(jnp.int32, (1, PAIR), 1) < DH
        grads = []
        for pair, pack in enumerate((mine, theirs)):
            qq, kk, vv = (qkv[2 * i + pair, :, :] for i in range(3))
            do = dctx[:, pair * PAIR : (pair + 1) * PAIR]
            dq_t, dk, dv = 0.0, 0.0, 0.0
            for head in range(2):
                sel = first if head == 0 else ~first
                qm = (jnp.where(sel, qq, jnp.zeros_like(qq)) * 0.125).astype(BF)
                km = (jnp.where(sel, kk, jnp.zeros_like(kk)) * 0.125).astype(BF)
                dom = jnp.where(sel, do, jnp.zeros_like(do))
                at = 2 * pair + head
                p = jnp.exp(nt(kk, qm) + bias[...] - lse[at : at + 1, :])
                dp = nt(vv, dom)
                delta = jnp.sum(p * dp, axis=0, keepdims=True)
                ds = (p * (dp - delta)).astype(BF)
                dv += nn(p.astype(BF), dom)
                dk += nn(ds, qm)
                dq_t += nn(km.T, ds)
            dq = dq_t.T.astype(BF)
            dk = dk.astype(BF)
            dv = dv.astype(BF)
            for i, part in enumerate((dq, dk, dv)):
                (others if pair else ours)[i, :, :] = part
            pack[8:9, pl.ds(pl.multiple_of(step * PAIR, PAIR), PAIR)] = colsum(dq)
            pack[8:9, pl.ds(pl.multiple_of((step + attending) * PAIR, PAIR), PAIR)] = colsum(dv)
            grads.append((dq, dk, dv))
        back = jnp.concatenate([g[i] for i in range(3) for g in grads], axis=1)
        dx[...] += nt(back, beside(wqo, wqp, wko, wkp, wvo, wvp))

    if not layer:

        @pl.when(step == attending - 1)
        def _():
            dx_own[...] = dx[: slots // 2, :]
            dx_peer[...] = dx[slots // 2 :, :].astype(BF)

        return

    @pl.when(step == attending)
    def _():
        loads.wait()
        norm_back_store(dx[...], n2[...].astype(F32), rstd2[...], row_of(gain2, layer - 1), dff, below2)
        dx[...] = dff[...].astype(F32)

    @pl.when(step >= attending)
    def _():
        chunk = pl.ds(pl.multiple_of((step - attending) * CHUNK, CHUNK), CHUNK)
        slope = jnp.concatenate([gp[0, :, chunk], gp[1, :, chunk]], axis=1)
        dx[...] += slope_step(
            chunk, dff[...], slope, columns_of((wdo, wdp), chunk), columns_of((wuo, wup), chunk),
            duo, dup, below_gbuo, below_gbup,
        )

    @pl.when(step == pl.num_programs(0) - 1)
    def _():
        norm_back_store(dx[...], n1[...].astype(F32), rstd1[...], row_of(gain1, layer - 1), below_datt, below1)


def down_steps(pack):
    return pack.shape[1] // 2 // PAIR


def attend_back(layer, scalars, count, lows, own, peer, saved, lse, sums, above, below):
    lows, pick = lows
    slots, width = lows.shape[1:]
    layers, _, half = own["w_query"].shape
    ff = own["w_up"].shape[2]
    attending, feeding = half // PAIR, ff // CHUNK if layer else 0

    def at(i):
        return jnp.clip(i, 0, attending - 1)

    def early_weight(array):
        k = layer if array.shape[0] > 1 else 0
        return pl.BlockSpec((None, width, PAIR), lambda i, *s: (k, 0, at(i))), array

    def stack(n):
        return pl.BlockSpec((n, slots, PAIR), lambda i, *s: (0, 0, at(i)))

    full, one = whole(slots, width), whole(slots, 1)
    vec = whole(layers, width)
    ins = [(pl.BlockSpec((None, slots, width), lambda i, *s: (pick, 0, 0)), lows)]
    for name in ("w_out", "w_query", "w_key", "w_value"):
        ins += [early_weight(own[name]), early_weight(peer[name])]
    ins += [(stack(6), saved), (pl.BlockSpec((None, 8, slots), lambda i, *s: (at(i), 0, 0)), lse)]
    ins += [(whole(*a.shape), a) for a in (*sums, *above)]
    packed = (16 * (layers - layer), width)
    outs = [(stack(3), (3, slots, half), BF)] * 2
    outs += [(whole(*packed), packed, F32)] * 2
    scratch = [pltpu.VMEM((slots, width), F32), pltpu.VMEM((slots, slots), F32)]
    row = (whole(8, width), (8, width), F32)
    if layer:
        n1, rstd1, slope, n2, rstd2, lower = below
        ins += [(full, n2), (one, rstd2), (vec, own["second_gain"]), (full, n1), (one, rstd1), (vec, own["first_gain"])]
        anywhere = pl.BlockSpec(memory_space=pl.ANY)
        ins += [(anywhere, a) for a in (own["w_up"], lower["w_up"], own["w_down"], lower["w_down"], slope)]
        latest = pl.BlockSpec((slots, CHUNK), lambda i, *s: (0, jnp.clip(i - attending, 0, feeding - 1)))
        outs += [row] + [(latest, (slots, ff), BF)] * 2
        outs += [(whole(1, ff), (1, ff), F32)] * 2 + [(whole(2, slots, width), (2, slots, width), BF), row]
        scratch += [pltpu.VMEM((width, ff), BF)] * 4 + [pltpu.VMEM((2, slots, ff), BF), pltpu.SemaphoreType.DMA((5,))]
    else:
        outs += [(whole(slots // 2, width), (slots // 2, width), t) for t in (F32, BF)]
    kernel = functools.partial(attend_back_kernel, layer, count, bool(above))
    return run(kernel, attending + feeding, scalars, ins, outs, scratch, 52, True)


def halves_of(value, bit, scalars, left, base):
    axis = left.index(bit)
    rows, width = value.shape
    cut = value.reshape(1 << axis, 2, rows >> (axis + 1), width)
    mine = (scalars[base] >> bit) & 1
    low, high = cut[:, 0].reshape(rows // 2, width), cut[:, 1].reshape(rows // 2, width)
    return jnp.where(mine == 0, low, high), jnp.where(mine == 0, high, low)


def weight_kernel(plan, lefts, left, scalars, *refs):
    step = pl.program_id(0)
    pieces = sum(len(p) for _, p in plan)
    sides, operands = refs[: 2 * lefts], refs[2 * lefts : 2 * lefts + 2 * pieces]
    outs, (lt, right) = refs[2 * lefts + 2 * pieces : -2], refs[-2:]
    slots = sides[0].shape[0]
    n = 0
    for g, (bit, parts) in enumerate(plan):
        column = 0
        for start, steps, block, side, fresh in parts:
            ro, rp = operands[2 * n : 2 * n + 2]
            n += 1
            if fresh:

                @pl.when(step == start)
                def _(side=side):
                    lt[:, :slots] = sides[2 * side][...].T
                    lt[:, slots:] = sides[2 * side + 1][...].T

            @pl.when((step >= start) & (step < start + steps))
            def _(ro=ro, rp=rp, block=block, start=start, column=column, g=g, bit=bit):
                right[:slots, :block] = ro[...]
                right[slots:, :block] = rp[...]
                value = nn(lt[...], right[:, :block])
                at = pl.ds(pl.multiple_of(column + (step - start) * block, 128), block)
                if bit is None:
                    outs[g][:, at] = value.astype(BF)
                else:
                    keep, send = halves_of(value, bit, scalars, left, 1)
                    outs[2 * g][:, at] = keep.astype(BF)
                    outs[2 * g + 1][:, at] = send.astype(BF)

            column += steps * block


def weight_grads(scalars, groups, size, block):
    bits = size.bit_length() - 1
    left = list(range(bits - 1, -1, -1))
    plan, ins, outs, wide, sides = [], [], [], [], {}
    at = 0

    def parted(operand):
        return operand if isinstance(operand, tuple) else (operand, None)

    def side_spec(pick):
        if pick is None:
            return pl.BlockSpec((slots, width), lambda i, *s: (0, 0), pipeline_mode=pl.Buffered(1))
        return pl.BlockSpec((None, slots, width), lambda i, *s: (pick, 0, 0), pipeline_mode=pl.Buffered(1))

    slots, width = parted(groups[0][1][0][0])[0].shape[-2:]
    split = (width // size) % 16 == 0
    before = None
    for order, parts in groups:
        pieces, total = [], 0
        for lo, lp, ro, rp, *window in parts:
            (lo, pick), (lp, _) = parted(lo), parted(lp)
            key = (id(lo), pick)
            if key not in sides:
                sides[key] = len(sides)
                wide += [(side_spec(pick), lo), (side_spec(pick), lp)]
            (ro, pick), (rp, _) = parted(ro), parted(rp)
            units = rp.shape[-1]
            blk, skip, steps = window or (min(block, units), 0, units // min(block, units))
            pieces.append((at, steps, blk, sides[key], sides[key] != before))
            before = sides[key]

            def spec(i, *s, a=at, n=steps, k=pick, skip=skip):
                place = jnp.clip(i - a, 0, n - 1) + skip
                return (0, place) if k is None else (k, 0, place)

            shape = (slots, blk) if pick is None else (None, slots, blk)
            ins += [(pl.BlockSpec(shape, spec), ro), (pl.BlockSpec(shape, spec), rp)]
            at += steps
            total += steps * blk
        plan.append((order[0] if split else None, pieces))
        rows = width // 2 if split else width
        outs += [(whole(rows, total), (rows, total), BF)] * (2 if split else 1)
    pins = [*range(len(wide) + len(ins))]
    scratch = [pltpu.VMEM((width, 2 * slots), BF), pltpu.VMEM((2 * slots, block), BF)]
    kernel = functools.partial(weight_kernel, plan, len(sides), left)
    made = run(kernel, at, scalars, [*wide, *ins], outs, scratch, 36, pins)
    if split:
        return [Scatter(scalars, o, size, made[2 * g], made[2 * g + 1]) for g, (o, _) in enumerate(groups)]
    return [Scatter(scalars, o, size, None, made[g]) for g, (o, _) in enumerate(groups)]


def add_kernel(plan, scalars, *refs):
    ins, outs = refs[: 2 * len(plan)], refs[2 * len(plan) :]
    for i, (bit, left) in enumerate(plan):
        value = ins[2 * i][...].astype(F32) + ins[2 * i + 1][...].astype(F32)
        if bit is None:
            outs[2 * i][...] = value
        else:
            kept, send = halves_of(value, bit, scalars, left, 1)
            outs[2 * i][...] = kept.astype(BF)
            outs[2 * i + 1][...] = send.astype(BF)


def merge_kernel(bit, left, scalars, *refs):
    ins, (keep, send) = refs[:-2], refs[-2:]
    at = 0
    for i in range(len(ins) // 2):
        value = ins[2 * i][...].astype(F32) + ins[2 * i + 1][...].astype(F32)
        kept, sent = halves_of(value, bit, scalars, left, 1)
        width = value.shape[1]
        keep[:, at : at + width] = kept.astype(BF)
        send[:, at : at + width] = sent.astype(BF)
        at += width


def land(*scatters, merge=False, micros=0.05):
    if not scatters:
        return None
    unit = scatters[0].keep.shape[0] >> len(scatters[0].order)
    if unit % 16:
        for f in scatters:
            f.part((f.keep.astype(F32) + f.value.astype(F32)).astype(BF))
        if merge:
            first = scatters[0]
            first.keep = jnp.concatenate([f.keep for f in scatters], axis=1)
            first.value = jnp.concatenate([f.value for f in scatters], axis=1)
            return first
        return None
    if merge:
        first = scatters[0]
        rows, total = first.keep.shape[0] // 2, sum(f.keep.shape[1] for f in scatters)
        ins = [(whole(*a.shape), a) for f in scatters for a in (f.keep, f.value)]
        kernel = functools.partial(merge_kernel, first.order[0], list(first.left))
        both_out = [(whole(rows, total), (rows, total), BF)] * 2
        first.keep, first.value = run(kernel, 1, first.scalars, ins, both_out, [], 32)
        return first
    steps = 1
    if max(f.keep.size for f in scatters) > 300000:
        steps = next(n for n in (3, 2, 1) if not any(f.keep.shape[1] % (128 * n) for f in scatters))
    ins, outs, plan = [], [], []
    for f in scatters:
        rows, width = f.keep.shape
        block = columns(rows, width // steps)
        ins += [(block, f.keep), (block, f.value)]
        outs += [(columns(rows // 2, width // steps), (rows // 2, width), BF)] * 2
        plan.append((f.order[0], list(f.left)))
    made = run(functools.partial(add_kernel, plan), steps, scatters[0].scalars, ins, outs, [], 32, micros=micros)
    for i, f in enumerate(scatters):
        f.keep, f.value = made[2 * i : 2 * i + 2]
    return None


class Scatter:
    def __init__(self, scalars, order, size, keep, send):
        bits = size.bit_length() - 1
        self.scalars, self.size = scalars, size
        self.order = [b for b in order if b < bits] + list(range(4, bits))
        self.left = list(range(bits - 1, -1, -1))
        self.keep, self.value = keep, send
        if keep is None:
            self.part(send)

    def part(self, value):
        bit = self.order[0]
        axis = self.left.index(bit)
        rows, width = value.shape
        cut = value.reshape(1 << axis, 2, rows >> (axis + 1), width)
        mine = (self.scalars[1] >> bit) & 1
        self.keep = lax.dynamic_index_in_dim(cut, mine, 1, keepdims=False).reshape(rows // 2, width)
        self.value = lax.dynamic_index_in_dim(cut, 1 - mine, 1, keepdims=False).reshape(rows // 2, width)

    def launch(self):
        bit = self.order.pop(0)
        self.left.remove(bit)
        self.value = flip(self.value, bit, self.size)
        return self


def settle_kernel(scalars, keep, got, out):
    out[...] = keep[...].astype(F32) + got[...].astype(F32)


def settle(scatter):
    rows, width = scatter.keep.shape
    block = whole(rows, width)
    (scatter.keep,) = run(
        settle_kernel, 1, scatter.scalars, [(block, scatter.keep), (block, scatter.value)],
        [(block, (rows, width), F32)], [], 16,
    )
    scatter.value = None


def last_kernel(plan, count, scalars, *refs):
    pairs, outs = [], list(refs)
    for n in count:
        pairs.append([outs.pop(0) for _ in range(n)])
    for out, layers in zip(outs, plan, strict=True):
        for layer, (i, at) in enumerate(layers):
            cut = slice(at, at + out.shape[2])
            parts = [r[:, cut].astype(F32) for r in pairs[i]]
            out[layer, :, :] = sum(parts[1:], parts[0])


def last_sums(scalars, scatters, plan, widths):
    rows, layers = scatters[0].keep.shape[0], len(plan[0])
    return run(
        functools.partial(last_kernel, plan, [1 if f.value is None else 2 for f in scatters]), 1, scalars,
        [(whole(*a.shape), a) for f in scatters for a in (f.keep, f.value) if a is not None],
        [(whole(layers, rows, w), (layers, rows, w), F32) for w in widths], [], 24, "out",
    )


def sum_kernel(scalars, left, right, out):
    out[...] = left[...] + right[...]


def small_kernel(layers, scalars, mine, got, gbq, gbv, gbu, *vectors):
    width = mine.shape[1]
    for layer in range(layers):
        total = mine[16 * layer : 16 * layer + 16, :] + got[16 * layer : 16 * layer + 16, :]
        row = slice(layer, layer + 1)
        for i, out in enumerate(vectors):
            out[row, :] = total[i : i + 1, :]
        gbu[row, :width] = total[6:7, :]
        gbu[row, width:] = total[7:8, :]
        gbq[row, :] = total[8:9, : width // 2]
        gbv[row, :] = total[8:9, width // 2 :]


def swap(value):
    return lax.ppermute(value, "mp", [(0, 1), (1, 0)])


def flip(value, bit, size):
    return lax.ppermute(value, "dp", [(i, i ^ (1 << bit)) for i in range(size)])


NAMES = (
    "w_query", "b_query", "w_key", "w_value", "b_value", "w_out", "b_out", "first_gain", "first_shift",
    "w_up", "b_up", "w_down", "b_down", "second_gain", "second_shift",
)
XY, YX = (0, 1, 2, 3), (1, 0, 2, 3)
TURNS = (0, 1, 2, 3), (1, 2, 0, 3), (2, 0, 1, 3)


def shards(dp, tokens, lengths, cotangent, *given):
    held = dict(zip(NAMES, given, strict=True))
    layers, width, half = held["w_query"].shape
    ff = held["w_up"].shape[2]
    slots = 2 * tokens.shape[1]
    count = lengths.shape[1]
    me = lax.axis_index("mp")
    scalars = jnp.concatenate([me[None], lengths.reshape(-1)]).astype(jnp.int32)
    place = jnp.stack([me, lax.axis_index("dp")]).astype(jnp.int32)

    def give_row(mine, other):
        other = swap(other).astype(mine.dtype)
        return jnp.stack([jnp.where(me == 0, mine, other), jnp.where(me == 0, other, mine)])

    Order.last, Order.also = None, ()
    biases = swap(jnp.concatenate([held["b_up"], held["b_query"], held["b_value"]], axis=1))
    x = (tokens, swap(tokens))
    early = {n: swap(held[n]) for n in ("w_query", "w_key", "w_value")}
    names = ("w_out", "w_up", "w_down")
    pieces, early, biases, x = lax.optimization_barrier(([held[n][:1] for n in names], early, biases, x))
    first = {n: swap(p) for n, p in zip(names, pieces, strict=True)}
    peers = [{"biases": biases, **early, **first} for _ in range(layers)]

    def last_wave(after):
        pieces, cot, fresh, after = lax.optimization_barrier(([held[n] for n in names], cotangent, first, after))
        later = {n: swap(p) for n, p in zip(names, pieces, strict=True)}
        for layer in range(layers):
            peers[layer].update(later if layer else fresh)
        return (cot, swap(cot)), after

    kept = []
    for layer in range(layers - 1):
        made = attend(layer, scalars, count, x, held, peers[layer])
        if layer == 0:
            x = made[4]
            cot, x = last_wave(x)
        fed = feed(layer, scalars, x, made[1], made[2], held, peers[layer])
        kept.append((x, made[:4], fed))
        x = fed[6]
    made = turn(layers - 1, scalars, count, x, held, peers[-1], cot)
    kept.append((x, made[:4], (None, None, *made[4:7])))
    y, gbu_own, gbu_peer, sums2, du_own, du_peer, lows, sums1 = made[7:]

    def step(*scatters, micros=0.05):
        land(*scatters, micros=micros)
        for f in scatters:
            f.launch()

    def step_as_one(*scatters):
        return land(*scatters, merge=True).launch()

    pack, flying, above = (), [], None
    theirs_of = [[swap(a) for a in (x, att[2], fed[2], fed[4])] for x, att, fed in kept]
    Order.also = [a for arrays in theirs_of[:-1] for a in arrays]
    for layer in reversed(range(layers)):
        x_in, (qkv, ctx_own, _, lse), fed = kept[layer]
        hlow, act_own = fed[2:4]
        x_peer, ctx_peer, h_peer, act_peer = theirs_of[layer]
        lows_peer, du_theirs = swap(lows), swap(du_peer)
        ahead = [((lows, 0), (lows_peer, 0), act_own, act_peer)], [(hlow, h_peer, du_own, du_theirs)]
        if not flying:
            (down,) = weight_grads(place, [(XY, ahead[0])], dp, 512)
            (up,) = weight_grads(place, [(YX, ahead[1])], dp, 512)
            down.launch()
            up.launch()
        else:
            group = weight_grads(place, list(zip(TURNS, ahead)), dp, 512)
            for f in group:
                f.launch()
            high = step_as_one(*flying)
            group += weight_grads(place, [(TURNS[2], above)], dp, 384)
            group[2].launch()
        Order.also = [x_peer, ctx_peer]
        sums = (sums1, sums2, gbu_own, gbu_peer)
        below = ()
        if layer:
            n1, rstd1, _, _, _, slope, _, n2, rstd2 = kept[layer - 1][2]
            below = (n1, rstd1, slope, n2, rstd2, peers[layer - 1])
        back = attend_back(
            layer, scalars, count, (lows, 1), held, peers[layer], qkv, lse, sums, pack, below
        )
        ours, others, mine, theirs = back[:4]
        pack = (mine, theirs)
        others = swap(others)
        above = [((lows, 1), (lows_peer, 1), ctx_own, ctx_peer)]
        above += [(x_in, x_peer, (ours, i), (others, i)) for i in range(3)]
        if not layer:
            step(high, micros=12)
            step(*group, micros=8)
        if layer:
            step(down, up, micros=8)
            sums2, du_own, du_peer, gbu_own, gbu_peer, lows, sums1 = back[4:]
            flying = [down, up]
    encoded = give_row(y[0], y[1])
    bits = dp.bit_length() - 1
    left = list(range(bits - 1, -1, -1))
    total, got = mine, swap(theirs)

    def small_step(total, got):
        whole_one = whole(*total.shape)
        (total,) = run(
            sum_kernel, 1, place, [(whole_one, total), (whole_one, got)], [(whole_one, total.shape, F32)], [], 8
        )
        return total, flip(total, left.pop(0), dp)

    outer, query, key, value = above
    third = half // 3
    last = weight_grads(
        place,
        list(
            zip(
                TURNS,
                (
                    [outer, (*query, third, 0, 1)],
                    [(*query, third, 1, 2), (*key, third, 0, 2)],
                    [(*key, third, 2, 1), value],
                ),
            )
        ),
        dp, half,
    )
    for f in last:
        f.launch()
    total, got = small_step(total, got)
    token_grad = give_row(back[4], back[5])
    step(*group)
    step(*last)
    total, got = small_step(total, got)
    middle = step_as_one(*group)
    step(*last)
    while high.order:
        step(high)
    settle(high)
    total, got = small_step(total, got)
    low = step_as_one(*last)
    total, got = small_step(total, got)
    rest = [middle, low]
    while any(f.order for f in rest) or left:
        for f in rest:
            if f.order:
                step(f)
        if left:
            total, got = small_step(total, got)

    gwd, gwu = last_sums(place, [middle, high], [[(0, 0), (1, 0)], [(0, ff), (1, ff)]], [ff, ff])
    gwo, gwq, gwk, gwv = last_sums(
        place, [low, middle], [[(0, i * half), (1, 2 * ff + i * half)] for i in range(4)], [half] * 4
    )
    shapes = [half, half, ff] + [width] * 6
    gbq, gbv, gbu, gfg, gfs, gbo, gsg, gss, gbd = run(
        functools.partial(small_kernel, layers), 1, place,
        [(whole(*total.shape), total), (whole(*got.shape), got)],
        [(whole(layers, n), (layers, n), F32) for n in shapes], [], 16, "out",
    )
    return (
        encoded, token_grad, gwq, gbq, gwk, gwv, gbv, gwo, gbo, gfg, gfs, gwu, gbu, gwd, gbd, gsg, gss,
    )


def solution(mesh):
    cols, mats, rep = P(None, "mp"), P(None, None, "mp"), P()
    placed = (
        P("dp", "mp", None), P("dp", None), P("dp", "mp", None),
        mats, cols, mats, mats, cols, mats, rep, rep, rep, mats, cols, mats, rep, rep, rep,
    )
    grads = P(None, "dp", "mp")
    return jax.shard_map(
        functools.partial(shards, mesh.shape["dp"]),
        mesh=mesh,
        in_specs=placed,
        out_specs=(
            P("dp", "mp", None), P("dp", "mp", None), grads, cols, grads, grads, cols,
            grads, rep, rep, rep, grads, cols, grads, rep, rep, rep,
        ),
        check_vma=False,
    )
```

```python
import functools

import jax
import jax.numpy as jnp
from jax import lax
from jax.experimental import pallas as pl
from jax.experimental.pallas import tpu as pltpu
from jax.sharding import PartitionSpec as P

DH = 64
QSLOT = 32
BF = jnp.bfloat16
F32 = jnp.float32
PAIR = 2 * DH
CHUNK = 512


def nn(left, right):
    return lax.dot_general(left, right, (((1,), (0,)), ((), ())), preferred_element_type=F32)


def nt(left, right):
    return lax.dot_general(left, right, (((1,), (1,)), ((), ())), preferred_element_type=F32)


def tn(left, right):
    return lax.dot_general(left, right, (((0,), (0,)), ((), ())), preferred_element_type=F32)


def beside(*refs):
    return jnp.concatenate([r[...] for r in refs], axis=1)


def whole(*shape):
    return pl.BlockSpec(shape, lambda i, *s: (0,) * len(shape))


def columns(rows, width, start=0):
    return pl.BlockSpec((rows, width), lambda i, *s: (0, start + i))


def layer_columns(layer, array, width):
    at = layer if array.shape[0] > 1 else 0
    return pl.BlockSpec((None, array.shape[1], width), lambda i, *s: (at, 0, i)), array


def layer_whole(layer, array):
    at = layer if array.shape[0] > 1 else 0
    return pl.BlockSpec((None, *array.shape[1:]), lambda i, *s: (at, 0, 0)), array


def my_row(array):
    return pl.BlockSpec((None, *array.shape[1:]), lambda i, s: (s[0], 0, 0))


def sds(shape, dtype):
    return jax.ShapeDtypeStruct(shape, dtype)


class Order:
    last = None
    also = ()


def run(kernel, grid, scalars, ins, outs, scratch, megabytes, pinned=False, micros=0.05):
    shape = pltpu.HBM if pinned in (True, "out") else sds
    arrays = [a for _, a in ins]
    kept = range(len(arrays)) if pinned is True else pinned if isinstance(pinned, list) else ()
    for i in kept:
        arrays[i] = pltpu.with_memory_space_constraint(arrays[i], pltpu.HBM)
    extra = [pltpu.with_memory_space_constraint(a, pltpu.HBM) for a in Order.also]
    extra += [] if Order.last is None else [Order.last]
    Order.also = ()
    count = 1 + len(ins)

    def body(*refs):
        kernel(*refs[:count], *refs[count + len(extra) :])

    made = pl.pallas_call(
        body,
        grid_spec=pltpu.PrefetchScalarGridSpec(
            num_scalar_prefetch=1,
            grid=(grid,),
            in_specs=[b for b, _ in ins] + [pl.BlockSpec(memory_space=pl.ANY)] * len(extra),
            out_specs=[b for b, _, _ in outs],
            scratch_shapes=scratch,
        ),
        out_shape=[shape(dims, dtype) for _, dims, dtype in outs],
        compiler_params=pltpu.CompilerParams(vmem_limit_bytes=megabytes * 1024 * 1024),
        cost_estimate=pl.CostEstimate(flops=1000 + int(1e9 * micros), transcendentals=0, bytes_accessed=1000),
    )(scalars, *arrays, *extra)
    Order.last = made[-1]
    if shape is pltpu.HBM:
        Order.last = pltpu.with_memory_space_constraint(made[-1], pltpu.HBM)
    return made


def row_of(ref, layer):
    return ref[layer : layer + 1, :].astype(F32)


def segments(scalars, count, slots, dim):
    shape = (slots, 1) if dim == 0 else (1, slots)
    slot = lax.broadcasted_iota(jnp.int32, shape, dim) + scalars[0] * (slots // 2)
    slot = jnp.where(slot >= slots, slot - slots, slot)
    base = 1 + scalars[0] * count
    shift = jnp.where(scalars[base + 1] > 0, QSLOT.bit_length() - 1, slots.bit_length() - 1)
    segment = lax.shift_right_logical(slot, jnp.broadcast_to(shift, shape))
    inside = slot - lax.shift_left(segment, jnp.broadcast_to(shift, shape))
    length = jnp.zeros(shape, jnp.int32)
    for k in range(count):
        length = jnp.where(segment == k, scalars[base + k], length)
    return segment, jnp.where(inside < length, segment, -1)


def attend_kernel(layer, count, split, scalars, *refs):
    refs = list(refs)
    xs = [refs.pop(0) for _ in range(2 if split else 1)]
    qkv, co, cp, lse = refs[10:14]
    bias = refs[-1]
    x = refs[14] if split else xs[0]
    slots = co.shape[0]

    @pl.when(pl.program_id(0) == 0)
    def _():
        segment, _ = segments(scalars, count, slots, 0)
        _, live = segments(scalars, count, slots, 1)
        bias[...] = jnp.where(segment == live, 0.0, -1e9)
        if split:
            x[...] = jnp.concatenate([r[...] for r in xs], axis=0)

    attend_step(layer, x[...], refs[:10], qkv, (co, cp), lse, bias, 0)


def attend_step(layer, xv, operands, qkv, ctx, lse, bias, column):
    wqo, wqp, wko, wkp, wvo, wvp, bqo, bqp, bvo, bvp = operands
    q = (nn(xv, beside(wqo, wqp)) + both(bqo, bqp, layer)).astype(BF)
    k = nn(xv, beside(wko, wkp)).astype(BF)
    v = (nn(xv, beside(wvo, wvp)) + both(bvo, bvp, layer)).astype(BF)
    first = lax.broadcasted_iota(jnp.int32, (1, PAIR), 1) < DH
    lse[...] = jnp.zeros_like(lse)
    for pair, cr in enumerate(ctx):
        at = slice(pair * PAIR, (pair + 1) * PAIR)
        qq, kk, vv = q[:, at], k[:, at], v[:, at]
        for i, part in enumerate((qq, kk, vv)):
            qkv[2 * i + pair, :, :] = part
        outs, peaks = [], []
        for head in range(2):
            mine = first if head == 0 else ~first
            qm = jnp.where(mine, qq, jnp.zeros_like(qq)) * 0.125
            s = nt(qm.astype(BF), kk) + bias[...]
            peak = jnp.max(s, axis=1, keepdims=True)
            e = jnp.exp(s - peak).astype(BF)
            outs.append(nn(e, jnp.where(mine, vv, jnp.ones_like(vv))))
            peaks.append(peak)
        total = pltpu.roll(jnp.where(first, outs[1], outs[0]), DH, 1)
        cr[:, pl.ds(column, PAIR)] = (jnp.where(first, outs[0], outs[1]) / total).astype(BF)
        logs = jnp.where(first, peaks[0], peaks[1]) + jnp.log(total)
        flat = logs.T
        lse[2 * pair : 2 * pair + 1, :] = flat[0:1, :]
        lse[2 * pair + 1 : 2 * pair + 2, :] = flat[DH : DH + 1, :]


def triple(count, slots):
    return pl.BlockSpec((count, slots, PAIR), lambda i, *s: (0, 0, i))


def both(own, peer, layer):
    return jnp.concatenate([row_of(own, layer), row_of(peer, layer)], axis=1)


def attend(layer, scalars, count, x, own, peer):
    split = isinstance(x, tuple)
    layers, width, half = own["w_query"].shape
    slots = 2 * x[0].shape[1] if split else x.shape[0]
    steps = half // PAIR
    act = columns(slots, PAIR)
    ins = [(my_row(a), a) for a in x] if split else [(whole(slots, width), x)]
    for name in ("w_query", "w_key", "w_value"):
        ins += [layer_columns(layer, own[name], PAIR), layer_columns(layer, peer[name], PAIR)]
    ins += [(columns(layers, PAIR), own["b_query"]), (columns(layers, PAIR, 4 * steps), peer["biases"])]
    ins += [(columns(layers, PAIR), own["b_value"]), (columns(layers, PAIR, 5 * steps), peer["biases"])]
    outs = [(triple(6, slots), (6, slots, half), BF)] + [(act, (slots, half), BF)] * 2
    outs += [(pl.BlockSpec((None, 8, slots), lambda i, *s: (i, 0, 0)), (steps, 8, slots), F32)]
    if split:
        outs += [(whole(slots, width), (slots, width), BF)]
    kernel = functools.partial(attend_kernel, layer, count, split)
    return run(kernel, steps, scalars, ins, outs, [pltpu.VMEM((slots, slots), F32)], 32, True)


def normalize(r):
    mean = jnp.mean(r, axis=1, keepdims=True)
    c = r - mean
    rstd = lax.rsqrt(jnp.mean(c * c, axis=1, keepdims=True) + 1e-12)
    return c * rstd, rstd


def norm_back(dy, n, rstd, gain):
    gdy = dy * gain
    return (
        gdy - jnp.mean(gdy, axis=1, keepdims=True) - n * jnp.mean(gdy * n, axis=1, keepdims=True)
    ) * rstd


def colsum(v):
    return jnp.sum(v.astype(F32), axis=0, keepdims=True)


def norm_back_store(dy, n, rstd, gain, low, sums):
    lowv = norm_back(dy, n, rstd, gain).astype(BF)
    low[:, :] = lowv
    sums[...] = jnp.concatenate(
        [colsum(dy * n), colsum(dy), colsum(lowv), jnp.zeros((5, dy.shape[1]), F32)], axis=0
    )


def gelu_step(low, up, up_bias):
    u = nn(low, up) + up_bias
    cdf = 0.5 * (1.0 + lax.erf(u * 0.7071067811865476))
    act = (u * cdf).astype(BF)
    return act, (cdf + u * (jnp.exp(u * u * -0.5) * 0.3989422804014327)).astype(BF)


def first_norm(layer, x, ctx, projection, b_out, g1, s1):
    n, rstd = normalize(x.astype(F32) + (nt(ctx, projection) + row_of(b_out, layer)))
    return n, rstd, n * row_of(g1, layer) + row_of(s1, layer)


def feed_kernel(layer, scalars, *refs):
    (x, co, cp, woo, wop, b_out, g1, s1, wuo, wup, wdo, wdp, buo, bup, b_down, g2, s2) = refs[:17]
    (n1, rstd1, hlow, acto, actp, gp, y, n2, rstd2, h, acc) = refs[17:]
    step = pl.program_id(0)

    @pl.when(step == 0)
    def _():
        n, rstd, hv = first_norm(layer, x[...], beside(co, cp), beside(woo, wop), b_out, g1, s1)
        n1[...] = n.astype(BF)
        rstd1[...] = rstd
        h[...] = hv
        hlow[...] = hv.astype(BF)
        acc[...] = jnp.zeros_like(acc)

    act, slope = gelu_step(hlow[...], beside(wuo, wup), both(buo, bup, layer))
    acto[...] = act[:, :CHUNK]
    actp[...] = act[:, CHUNK:]
    gp[0, :, :] = slope[:, :CHUNK]
    gp[1, :, :] = slope[:, CHUNK:]
    acc[...] += nt(act, beside(wdo, wdp))

    @pl.when(step == pl.num_programs(0) - 1)
    def _():
        n, rstd = normalize(h[...] + (acc[...] + row_of(b_down, layer)))
        y[...] = (n * row_of(g2, layer) + row_of(s2, layer)).astype(BF)
        n2[...] = n.astype(BF)
        rstd2[...] = rstd


def feed(layer, scalars, x, ctx_own, ctx_peer, own, peer):
    layers, width, half = own["w_query"].shape
    slots = x.shape[0]
    ff = own["w_up"].shape[2]
    full = whole(slots, width)
    one = whole(slots, 1)
    vec = whole(layers, width)
    act = columns(slots, CHUNK)
    part = whole(slots, half)
    ins = [(full, x), (part, ctx_own), (part, ctx_peer), layer_whole(layer, own["w_out"]), layer_whole(layer, peer["w_out"])]
    ins += [(vec, own[n]) for n in ("b_out", "first_gain", "first_shift")]
    for name in ("w_up", "w_down"):
        ins += [layer_columns(layer, own[name], CHUNK), layer_columns(layer, peer[name], CHUNK)]
    ins += [(columns(layers, CHUNK), own["b_up"]), (columns(layers, CHUNK), peer["biases"])]
    ins += [(vec, own[n]) for n in ("b_down", "second_gain", "second_shift")]
    outs = [(full, (slots, width), BF), (one, (slots, 1), F32), (full, (slots, width), BF)]
    outs += [(act, (slots, ff), BF)] * 2
    outs += [(pl.BlockSpec((2, slots, CHUNK), lambda i, *s: (0, 0, i)), (2, slots, ff), BF)]
    outs += [(full, (slots, width), BF), (full, (slots, width), BF), (one, (slots, 1), F32)]
    scratch = [pltpu.VMEM((slots, width), F32)] * 2
    return run(functools.partial(feed_kernel, layer), ff // CHUNK, scalars, ins, outs, scratch, 60, True)


class Loads:
    def __init__(self, sources, targets, sems):
        self.copies = [pltpu.make_async_copy(s, t, sems.at[i]) for i, (s, t) in enumerate(zip(sources, targets))]

    def start(self):
        for c in self.copies:
            c.start()

    def wait(self):
        for c in self.copies:
            c.wait()


def layer_of(ref, layer):
    return ref.at[layer if ref.shape[0] > 1 else 0]


def slope_step(chunk, low, gp, down, up, duo, dup, gbuo, gbup):
    du = (nn(low, down) * gp.astype(F32)).astype(BF)
    duo[...] = du[:, :CHUNK]
    dup[...] = du[:, CHUNK:]
    total = colsum(du)
    gbuo[:, chunk] = total[:, :CHUNK]
    gbup[:, chunk] = total[:, CHUNK:]
    return nt(du, up)


def columns_of(refs, chunk):
    return jnp.concatenate([r[:, chunk] for r in refs], axis=1)


def turn_kernel(layer, count, scalars, *refs):
    x, attention, weights, rest = refs[0], refs[1:11], refs[11:17], list(refs[17:])
    (b_out, g1, s1, buo, bup, b_down, g2, s2, cot_a, cot_b) = rest[:10]
    (qkv, co, cp, lse, hlow, acto, actp, y, gbuo, gbup, sums2, duo, dup, both_low, sums1) = rest[10:25]
    (bias, woo, wop, wuo, wup, wdo, wdp, gp, h, acc, n1, rstd1, sems) = rest[25:]
    dff, datt = both_low.at[0], both_low.at[1]
    step = pl.program_id(0)
    slots = co.shape[0]
    attending = co.shape[1] // PAIR
    feeding = gp.shape[2] // CHUNK
    loads = Loads([layer_of(w, layer) for w in weights], (woo, wop, wuo, wup, wdo, wdp), sems)

    @pl.when(step == 0)
    def _():
        loads.start()
        segment, _ = segments(scalars, count, slots, 0)
        _, live = segments(scalars, count, slots, 1)
        bias[...] = jnp.where(segment == live, 0.0, -1e9)

    @pl.when(step < attending)
    def _():
        attend_step(layer, x[...], attention, qkv, (co, cp), lse, bias, pl.multiple_of(step * PAIR, PAIR))

    @pl.when(step == attending)
    def _():
        loads.wait()
        n, rstd, hv = first_norm(layer, x[...], beside(co, cp), beside(woo, wop), b_out, g1, s1)
        n1[...] = n
        rstd1[...] = rstd
        h[...] = hv
        hlow[...] = hv.astype(BF)
        acc[...] = jnp.zeros_like(acc)

    @pl.when((step >= attending) & (step < attending + feeding))
    def _():
        chunk = pl.ds(pl.multiple_of((step - attending) * CHUNK, CHUNK), CHUNK)
        up_bias = jnp.concatenate([r[layer : layer + 1, chunk].astype(F32) for r in (buo, bup)], axis=1)
        act, slope = gelu_step(hlow[...], columns_of((wuo, wup), chunk), up_bias)
        acto[...] = act[:, :CHUNK]
        actp[...] = act[:, CHUNK:]
        gp[0, :, chunk] = slope[:, :CHUNK]
        gp[1, :, chunk] = slope[:, CHUNK:]
        acc[...] += nt(act, columns_of((wdo, wdp), chunk))

    @pl.when(step == attending + feeding - 1)
    def _():
        n, rstd = normalize(h[...] + (acc[...] + row_of(b_down, layer)))
        result = (n * row_of(g2, layer) + row_of(s2, layer)).astype(BF)
        y[0, :, :] = result[: slots // 2]
        y[1, :, :] = result[slots // 2 :]
        dy = jnp.concatenate([cot_a[...], cot_b[...]], axis=0).astype(F32)
        norm_back_store(dy, n, rstd, row_of(g2, layer), dff, sums2)
        acc[...] = dff[...].astype(F32)

    @pl.when(step >= attending + feeding)
    def _():
        chunk = pl.ds(pl.multiple_of((step - attending - feeding) * CHUNK, CHUNK), CHUNK)
        slope = jnp.concatenate([gp[0, :, chunk], gp[1, :, chunk]], axis=1)
        acc[...] += slope_step(
            chunk, dff[...], slope, columns_of((wdo, wdp), chunk), columns_of((wuo, wup), chunk),
            duo, dup, gbuo, gbup,
        )

    @pl.when(step == pl.num_programs(0) - 1)
    def _():
        norm_back_store(acc[...], n1[...], rstd1[...], row_of(g1, layer), datt, sums1)


def turn(layer, scalars, count, x, own, peer, cotangent):
    layers, width, half = own["w_query"].shape
    slots, ff = x.shape[0], own["w_up"].shape[2]
    attending, feeding = half // PAIR, ff // CHUNK

    def early(rows, start=0):
        return pl.BlockSpec((rows, PAIR), lambda i, *s: (0, start + jnp.clip(i, 0, attending - 1)))

    def early_weight(array):
        at = layer if array.shape[0] > 1 else 0
        return pl.BlockSpec((None, width, PAIR), lambda i, *s: (at, 0, jnp.clip(i, 0, attending - 1))), array

    full, vec = whole(slots, width), whole(layers, width)
    anywhere = pl.BlockSpec(memory_space=pl.ANY)
    ins = [(full, x)]
    for name in ("w_query", "w_key", "w_value"):
        ins += [early_weight(own[name]), early_weight(peer[name])]
    ins += [(early(layers), own["b_query"]), (early(layers, 4 * attending), peer["biases"])]
    ins += [(early(layers), own["b_value"]), (early(layers, 5 * attending), peer["biases"])]
    for name in ("w_out", "w_up", "w_down"):
        ins += [(anywhere, own[name]), (anywhere, peer[name])]
    ins += [(vec, own[n]) for n in ("b_out", "first_gain", "first_shift")]
    ins += [(whole(*a.shape), a) for a in (own["b_up"], peer["biases"])]
    ins += [(vec, own[n]) for n in ("b_down", "second_gain", "second_shift")]
    ins += [(my_row(a), a) for a in cotangent]
    late = pl.BlockSpec((slots, CHUNK), lambda i, *s: (0, jnp.clip(i - attending, 0, feeding - 1)))
    halves = (2, slots // 2, width)
    outs = [
        (pl.BlockSpec((6, slots, PAIR), lambda i, *s: (0, 0, jnp.clip(i, 0, attending - 1))), (6, slots, half), BF)
    ]
    outs += [(whole(slots, half), (slots, half), BF)] * 2
    outs += [
        (pl.BlockSpec((None, 8, slots), lambda i, *s: (jnp.clip(i, 0, attending - 1), 0, 0)), (attending, 8, slots), F32)
    ]
    outs += [(full, (slots, width), BF)] + [(late, (slots, ff), BF)] * 2 + [(whole(*halves), halves, BF)]
    outs += [(whole(1, ff), (1, ff), F32)] * 2 + [(whole(8, width), (8, width), F32)]
    latest = pl.BlockSpec((slots, CHUNK), lambda i, *s: (0, jnp.clip(i - attending - feeding, 0, feeding - 1)))
    outs += [(latest, (slots, ff), BF)] * 2
    outs += [(whole(2, slots, width), (2, slots, width), BF), (whole(8, width), (8, width), F32)]
    scratch = [pltpu.VMEM((slots, slots), F32)] + [pltpu.VMEM((width, half), BF)] * 2
    scratch += [pltpu.VMEM((width, ff), BF)] * 4 + [pltpu.VMEM((2, slots, ff), BF)]
    scratch += [pltpu.VMEM((slots, width), F32)] * 3 + [pltpu.VMEM((slots, 1), F32), pltpu.SemaphoreType.DMA((6,))]
    kernel = functools.partial(turn_kernel, layer, count)
    return run(kernel, attending + 2 * feeding, scalars, ins, outs, scratch, 56, True)


def attend_back_kernel(layer, count, above, scalars, *refs):
    rest = list(refs)

    def take(n):
        return [rest.pop(0) for _ in range(n)]

    datt, woo, wop, wqo, wqp, wko, wkp, wvo, wvp, qkv, lse, sums1, sums2, gbuo, gbup = take(15)
    upper = take(2) if above else None
    if layer:
        n2, rstd2, gain2, n1, rstd1, gain1 = take(6)
        sources = take(5)
    ours, others, mine, theirs = take(4)
    if layer:
        below2, duo, dup, below_gbuo, below_gbup, both_low, below1 = take(7)
        dff, below_datt = both_low.at[0], both_low.at[1]
    else:
        dx_own, dx_peer = take(2)
    dx, bias = take(2)
    step = pl.program_id(0)
    slots = datt.shape[0]
    attending = down_steps(mine)
    if layer:
        wuo, wup, wdo, wdp, gp, sems = take(6)
        loads = Loads(
            [*[layer_of(w, layer - 1) for w in sources[:4]], sources[4]], (wuo, wup, wdo, wdp, gp), sems
        )

    @pl.when(step == 0)
    def _():
        if layer:
            loads.start()
        _, live = segments(scalars, count, slots, 0)
        segment, _ = segments(scalars, count, slots, 1)
        bias[...] = jnp.where(segment == live, 0.0, -1e9)
        rows = jnp.concatenate([sums1[0:3, :], sums2[0:3, :]], axis=0)
        for i, (pack, gbu) in enumerate(((mine, gbuo), (theirs, gbup))):
            width = pack.shape[1]
            pack[:16, :] = jnp.concatenate(
                [rows, gbu[:, :width], gbu[:, width:], jnp.zeros((8, width), F32)], axis=0
            )
            if above:
                pack[16:, :] = upper[i][...]
        dx[...] = datt[...].astype(F32)

    @pl.when(step < attending)
    def _():
        dctx = nn(datt[...], beside(woo, wop)).astype(BF)
        first = lax.broadcasted_iota(jnp.int32, (1, PAIR), 1) < DH
        grads = []
        for pair, pack in enumerate((mine, theirs)):
            qq, kk, vv = (qkv[2 * i + pair, :, :] for i in range(3))
            do = dctx[:, pair * PAIR : (pair + 1) * PAIR]
            dq_t, dk, dv = 0.0, 0.0, 0.0
            for head in range(2):
                sel = first if head == 0 else ~first
                qm = (jnp.where(sel, qq, jnp.zeros_like(qq)) * 0.125).astype(BF)
                km = (jnp.where(sel, kk, jnp.zeros_like(kk)) * 0.125).astype(BF)
                dom = jnp.where(sel, do, jnp.zeros_like(do))
                at = 2 * pair + head
                p = jnp.exp(nt(kk, qm) + bias[...] - lse[at : at + 1, :])
                dp = nt(vv, dom)
                delta = jnp.sum(p * dp, axis=0, keepdims=True)
                ds = (p * (dp - delta)).astype(BF)
                dv += nn(p.astype(BF), dom)
                dk += nn(ds, qm)
                dq_t += nn(km.T, ds)
            dq = dq_t.T.astype(BF)
            dk = dk.astype(BF)
            dv = dv.astype(BF)
            for i, part in enumerate((dq, dk, dv)):
                (others if pair else ours)[i, :, :] = part
            pack[8:9, pl.ds(pl.multiple_of(step * PAIR, PAIR), PAIR)] = colsum(dq)
            pack[8:9, pl.ds(pl.multiple_of((step + attending) * PAIR, PAIR), PAIR)] = colsum(dv)
            grads.append((dq, dk, dv))
        back = jnp.concatenate([g[i] for i in range(3) for g in grads], axis=1)
        dx[...] += nt(back, beside(wqo, wqp, wko, wkp, wvo, wvp))

    if not layer:

        @pl.when(step == attending - 1)
        def _():
            dx_own[...] = dx[: slots // 2, :]
            dx_peer[...] = dx[slots // 2 :, :].astype(BF)

        return

    @pl.when(step == attending)
    def _():
        loads.wait()
        norm_back_store(dx[...], n2[...].astype(F32), rstd2[...], row_of(gain2, layer - 1), dff, below2)
        dx[...] = dff[...].astype(F32)

    @pl.when(step >= attending)
    def _():
        chunk = pl.ds(pl.multiple_of((step - attending) * CHUNK, CHUNK), CHUNK)
        slope = jnp.concatenate([gp[0, :, chunk], gp[1, :, chunk]], axis=1)
        dx[...] += slope_step(
            chunk, dff[...], slope, columns_of((wdo, wdp), chunk), columns_of((wuo, wup), chunk),
            duo, dup, below_gbuo, below_gbup,
        )

    @pl.when(step == pl.num_programs(0) - 1)
    def _():
        norm_back_store(dx[...], n1[...].astype(F32), rstd1[...], row_of(gain1, layer - 1), below_datt, below1)


def down_steps(pack):
    return pack.shape[1] // 2 // PAIR


def attend_back(layer, scalars, count, lows, own, peer, saved, lse, sums, above, below):
    lows, pick = lows
    slots, width = lows.shape[1:]
    layers, _, half = own["w_query"].shape
    ff = own["w_up"].shape[2]
    attending, feeding = half // PAIR, ff // CHUNK if layer else 0

    def at(i):
        return jnp.clip(i, 0, attending - 1)

    def early_weight(array):
        k = layer if array.shape[0] > 1 else 0
        return pl.BlockSpec((None, width, PAIR), lambda i, *s: (k, 0, at(i))), array

    def stack(n):
        return pl.BlockSpec((n, slots, PAIR), lambda i, *s: (0, 0, at(i)))

    full, one = whole(slots, width), whole(slots, 1)
    vec = whole(layers, width)
    ins = [(pl.BlockSpec((None, slots, width), lambda i, *s: (pick, 0, 0)), lows)]
    for name in ("w_out", "w_query", "w_key", "w_value"):
        ins += [early_weight(own[name]), early_weight(peer[name])]
    ins += [(stack(6), saved), (pl.BlockSpec((None, 8, slots), lambda i, *s: (at(i), 0, 0)), lse)]
    ins += [(whole(*a.shape), a) for a in (*sums, *above)]
    packed = (16 * (layers - layer), width)
    outs = [(stack(3), (3, slots, half), BF)] * 2
    outs += [(whole(*packed), packed, F32)] * 2
    scratch = [pltpu.VMEM((slots, width), F32), pltpu.VMEM((slots, slots), F32)]
    row = (whole(8, width), (8, width), F32)
    if layer:
        n1, rstd1, slope, n2, rstd2, lower = below
        ins += [(full, n2), (one, rstd2), (vec, own["second_gain"]), (full, n1), (one, rstd1), (vec, own["first_gain"])]
        anywhere = pl.BlockSpec(memory_space=pl.ANY)
        ins += [(anywhere, a) for a in (own["w_up"], lower["w_up"], own["w_down"], lower["w_down"], slope)]
        latest = pl.BlockSpec((slots, CHUNK), lambda i, *s: (0, jnp.clip(i - attending, 0, feeding - 1)))
        outs += [row] + [(latest, (slots, ff), BF)] * 2
        outs += [(whole(1, ff), (1, ff), F32)] * 2 + [(whole(2, slots, width), (2, slots, width), BF), row]
        scratch += [pltpu.VMEM((width, ff), BF)] * 4 + [pltpu.VMEM((2, slots, ff), BF), pltpu.SemaphoreType.DMA((5,))]
    else:
        outs += [(whole(slots // 2, width), (slots // 2, width), t) for t in (F32, BF)]
    kernel = functools.partial(attend_back_kernel, layer, count, bool(above))
    return run(kernel, attending + feeding, scalars, ins, outs, scratch, 52, True)


def halves_of(value, bit, scalars, left, base):
    axis = left.index(bit)
    rows, width = value.shape
    cut = value.reshape(1 << axis, 2, rows >> (axis + 1), width)
    mine = (scalars[base] >> bit) & 1
    low, high = cut[:, 0].reshape(rows // 2, width), cut[:, 1].reshape(rows // 2, width)
    return jnp.where(mine == 0, low, high), jnp.where(mine == 0, high, low)


def weight_kernel(plan, lefts, left, scalars, *refs):
    bits, plan = plan
    step = pl.program_id(0)
    pieces = len(plan)
    sides, operands = refs[: 2 * lefts], refs[2 * lefts : 2 * lefts + 2 * pieces]
    outs, (lt, right) = refs[2 * lefts + 2 * pieces : -2], refs[-2:]
    slots = sides[0].shape[0]
    for n, (start, steps, block, side, fresh, places) in enumerate(plan):
        ro, rp = operands[2 * n : 2 * n + 2]
        if fresh:

            @pl.when(step == start)
            def _(side=side):
                lt[:, :slots] = sides[2 * side][...].T
                lt[:, slots:] = sides[2 * side + 1][...].T

        @pl.when((step >= start) & (step < start + steps))
        def _(ro=ro, rp=rp, block=block, start=start, places=places):
            right[:slots, :block] = ro[...]
            right[slots:, :block] = rp[...]
            value = nn(lt[...], right[:, :block])
            cut = 0
            for g, column, wide in places:
                part = value[:, cut : cut + wide]
                cut += wide
                at = pl.ds(pl.multiple_of(column + (step - start) * block, 128), wide)
                if bits[g] is None:
                    outs[g][:, at] = part.astype(BF)
                else:
                    keep, send = halves_of(part, bits[g], scalars, left, 1)
                    outs[2 * g][:, at] = keep.astype(BF)
                    outs[2 * g + 1][:, at] = send.astype(BF)


def weight_grads(scalars, orders, parts, size, block):
    bits = size.bit_length() - 1
    left = list(range(bits - 1, -1, -1))
    plan, ins, outs, wide, sides = [], [], [], [], {}
    at = 0

    def parted(operand):
        return operand if isinstance(operand, tuple) else (operand, None)

    def side_spec(pick):
        if pick is None:
            return pl.BlockSpec((slots, width), lambda i, *s: (0, 0), pipeline_mode=pl.Buffered(1))
        return pl.BlockSpec((None, slots, width), lambda i, *s: (pick, 0, 0), pipeline_mode=pl.Buffered(1))

    slots, width = parted(parts[0][0])[0].shape[-2:]
    split = (width // size) % 16 == 0
    before = None
    filled = [0] * len(orders)
    for lo, lp, ro, rp, *goal in parts:
        (lo, pick), (lp, _) = parted(lo), parted(lp)
        key = (id(lo), pick)
        if key not in sides:
            sides[key] = len(sides)
            wide += [(side_spec(pick), lo), (side_spec(pick), lp)]
        (ro, pick), (rp, _) = parted(ro), parted(rp)
        units = rp.shape[-1]
        blk = min(block, units)
        steps = units // blk
        places = []
        for g, many in goal if isinstance(goal[0], tuple) else ((goal[0], blk),):
            places.append((g, filled[g], many))
            filled[g] += many * steps
        plan.append((at, steps, blk, sides[key], sides[key] != before, places))
        before = sides[key]

        def spec(i, *s, a=at, n=steps, k=pick):
            place = jnp.clip(i - a, 0, n - 1)
            return (0, place) if k is None else (k, 0, place)

        shape = (slots, blk) if pick is None else (None, slots, blk)
        ins += [(pl.BlockSpec(shape, spec), ro), (pl.BlockSpec(shape, spec), rp)]
        at += steps
    rows = width // 2 if split else width
    for total in filled:
        outs += [(whole(rows, total), (rows, total), BF)] * (2 if split else 1)
    plan = ([o[0] if split else None for o in orders], plan)
    pins = [*range(len(wide) + len(ins))]
    scratch = [pltpu.VMEM((width, 2 * slots), BF), pltpu.VMEM((2 * slots, block), BF)]
    kernel = functools.partial(weight_kernel, plan, len(sides), left)
    made = run(kernel, at, scalars, [*wide, *ins], outs, scratch, 36, pins)
    if split:
        return [Scatter(scalars, o, size, made[2 * g], made[2 * g + 1]) for g, o in enumerate(orders)]
    return [Scatter(scalars, o, size, None, made[g]) for g, o in enumerate(orders)]


def add_kernel(plan, scalars, *refs):
    ins, outs = refs[: 2 * len(plan)], refs[2 * len(plan) :]
    for i, (bit, left) in enumerate(plan):
        value = ins[2 * i][...].astype(F32) + ins[2 * i + 1][...].astype(F32)
        if bit is None:
            outs[2 * i][...] = value
        else:
            kept, send = halves_of(value, bit, scalars, left, 1)
            outs[2 * i][...] = kept.astype(BF)
            outs[2 * i + 1][...] = send.astype(BF)


def merge_kernel(bit, left, scalars, *refs):
    ins, (keep, send) = refs[:-2], refs[-2:]
    at = 0
    for i in range(len(ins) // 2):
        value = ins[2 * i][...].astype(F32) + ins[2 * i + 1][...].astype(F32)
        kept, sent = halves_of(value, bit, scalars, left, 1)
        width = value.shape[1]
        keep[:, at : at + width] = kept.astype(BF)
        send[:, at : at + width] = sent.astype(BF)
        at += width


def land(*scatters, merge=False, micros=0.05):
    if not scatters:
        return None
    unit = scatters[0].keep.shape[0] >> len(scatters[0].order)
    if unit % 16:
        for f in scatters:
            f.part((f.keep.astype(F32) + f.value.astype(F32)).astype(BF))
        if merge:
            first = scatters[0]
            first.keep = jnp.concatenate([f.keep for f in scatters], axis=1)
            first.value = jnp.concatenate([f.value for f in scatters], axis=1)
            return first
        return None
    if merge:
        first = scatters[0]
        rows, total = first.keep.shape[0] // 2, sum(f.keep.shape[1] for f in scatters)
        ins = [(whole(*a.shape), a) for f in scatters for a in (f.keep, f.value)]
        kernel = functools.partial(merge_kernel, first.order[0], list(first.left))
        both_out = [(whole(rows, total), (rows, total), BF)] * 2
        first.keep, first.value = run(kernel, 1, first.scalars, ins, both_out, [], 32)
        return first
    steps = 1
    if max(f.keep.size for f in scatters) > 300000:
        steps = next(n for n in (3, 2, 1) if not any(f.keep.shape[1] % (128 * n) for f in scatters))
    ins, outs, plan = [], [], []
    for f in scatters:
        rows, width = f.keep.shape
        block = columns(rows, width // steps)
        ins += [(block, f.keep), (block, f.value)]
        outs += [(columns(rows // 2, width // steps), (rows // 2, width), BF)] * 2
        plan.append((f.order[0], list(f.left)))
    made = run(functools.partial(add_kernel, plan), steps, scatters[0].scalars, ins, outs, [], 32, micros=micros)
    for i, f in enumerate(scatters):
        f.keep, f.value = made[2 * i : 2 * i + 2]
    return None


class Scatter:
    def __init__(self, scalars, order, size, keep, send):
        bits = size.bit_length() - 1
        self.scalars, self.size = scalars, size
        self.order = [b for b in order if b < bits] + list(range(4, bits))
        self.left = list(range(bits - 1, -1, -1))
        self.keep, self.value = keep, send
        if keep is None:
            self.part(send)

    def part(self, value):
        bit = self.order[0]
        axis = self.left.index(bit)
        rows, width = value.shape
        cut = value.reshape(1 << axis, 2, rows >> (axis + 1), width)
        mine = (self.scalars[1] >> bit) & 1
        self.keep = lax.dynamic_index_in_dim(cut, mine, 1, keepdims=False).reshape(rows // 2, width)
        self.value = lax.dynamic_index_in_dim(cut, 1 - mine, 1, keepdims=False).reshape(rows // 2, width)

    def launch(self):
        bit = self.order.pop(0)
        self.left.remove(bit)
        self.value = flip(self.value, bit, self.size)
        return self


def settle_kernel(scalars, keep, got, out):
    out[...] = keep[...].astype(F32) + got[...].astype(F32)


def settle(scatter):
    rows, width = scatter.keep.shape
    block = whole(rows, width)
    (scatter.keep,) = run(
        settle_kernel, 1, scatter.scalars, [(block, scatter.keep), (block, scatter.value)],
        [(block, (rows, width), F32)], [], 16,
    )
    scatter.value = None


def last_kernel(plan, count, scalars, *refs):
    pairs, rest = [], list(refs)
    for n in count:
        pairs.append([rest.pop(0) for _ in range(n)])
    total, got = rest.pop(0), rest.pop(0)
    for out, layers in zip(rest, plan):
        for layer, (i, at) in enumerate(layers):
            cut = slice(at, at + out.shape[2])
            parts = [r[:, cut].astype(F32) for r in pairs[i]]
            out[layer, :, :] = sum(parts[1:], parts[0])
    gbq, gbv, gbu, *vectors = rest[len(plan) :]
    width = total.shape[1]
    sums = total[...] + got[...]
    for layer in range(len(plan[0])):
        mine = sums[16 * layer : 16 * layer + 16, :]
        row = slice(layer, layer + 1)
        for i, out in enumerate(vectors):
            out[row, :] = mine[i : i + 1, :]
        gbu[row, :width] = mine[6:7, :]
        gbu[row, width:] = mine[7:8, :]
        gbq[row, :] = mine[8:9, : width // 2]
        gbv[row, :] = mine[8:9, width // 2 :]


def last_sums(scalars, scatters, plan, widths, total, got, small):
    rows, layers = scatters[0].keep.shape[0], len(plan[0])
    arrays = [a for f in scatters for a in (f.keep, f.value) if a is not None] + [total, got]
    outs = [(whole(layers, rows, w), (layers, rows, w), F32) for w in widths]
    outs += [(whole(layers, n), (layers, n), F32) for n in small]
    kernel = functools.partial(last_kernel, plan, [1 if f.value is None else 2 for f in scatters])
    return run(kernel, 1, scalars, [(whole(*a.shape), a) for a in arrays], outs, [], 48, "out")


def sum_kernel(scalars, left, right, out):
    out[...] = left[...] + right[...]


def swap(value):
    return lax.ppermute(value, "mp", [(0, 1), (1, 0)])


def flip(value, bit, size):
    return lax.ppermute(value, "dp", [(i, i ^ (1 << bit)) for i in range(size)])


NAMES = (
    "w_query", "b_query", "w_key", "w_value", "b_value", "w_out", "b_out", "first_gain", "first_shift",
    "w_up", "b_up", "w_down", "b_down", "second_gain", "second_shift",
)
XY, YX = (0, 1, 2, 3), (1, 0, 2, 3)
TURNS = (0, 1, 2, 3), (1, 2, 0, 3), (2, 0, 1, 3)


def shards(dp, tokens, lengths, cotangent, *given):
    held = dict(zip(NAMES, given, strict=True))
    layers, width, half = held["w_query"].shape
    ff = held["w_up"].shape[2]
    slots = 2 * tokens.shape[1]
    count = lengths.shape[1]
    me = lax.axis_index("mp")
    scalars = jnp.concatenate([me[None], lengths.reshape(-1)]).astype(jnp.int32)
    place = jnp.stack([me, lax.axis_index("dp")]).astype(jnp.int32)

    def give_row(mine, other):
        other = swap(other).astype(mine.dtype)
        return jnp.stack([jnp.where(me == 0, mine, other), jnp.where(me == 0, other, mine)])

    Order.last, Order.also = None, ()
    biases = swap(jnp.concatenate([held["b_up"], held["b_query"], held["b_value"]], axis=1))
    x = (tokens, swap(tokens))
    early = {n: swap(held[n]) for n in ("w_query", "w_key", "w_value")}
    names = ("w_out", "w_up", "w_down")
    pieces, early, biases, x = lax.optimization_barrier(([held[n][:1] for n in names], early, biases, x))
    first = {n: swap(p) for n, p in zip(names, pieces, strict=True)}
    peers = [{"biases": biases, **early, **first} for _ in range(layers)]

    def last_wave(after):
        pieces, cot, fresh, after = lax.optimization_barrier(([held[n] for n in names], cotangent, first, after))
        later = {n: swap(p) for n, p in zip(names, pieces, strict=True)}
        for layer in range(layers):
            peers[layer].update(later if layer else fresh)
        return (cot, swap(cot)), after

    kept = []
    for layer in range(layers - 1):
        made = attend(layer, scalars, count, x, held, peers[layer])
        if layer == 0:
            x = made[4]
            cot, x = last_wave(x)
        fed = feed(layer, scalars, x, made[1], made[2], held, peers[layer])
        kept.append((x, made[:4], fed))
        x = fed[6]
    made = turn(layers - 1, scalars, count, x, held, peers[-1], cot)
    kept.append((x, made[:4], (None, None, *made[4:7])))
    y, gbu_own, gbu_peer, sums2, du_own, du_peer, lows, sums1 = made[7:]

    def step(*scatters, micros=0.05):
        land(*scatters, micros=micros)
        for f in scatters:
            f.launch()

    def step_as_one(*scatters):
        return land(*scatters, merge=True).launch()

    pack, flying, above = (), [], None
    theirs_of = [[swap(a) for a in (x, att[2], fed[2], fed[4])] for x, att, fed in kept]
    Order.also = [a for arrays in theirs_of[:-1] for a in arrays[:2]] + [theirs_of[-1][0]]
    for layer in reversed(range(layers)):
        x_in, (qkv, ctx_own, _, lse), fed = kept[layer]
        hlow, act_own = fed[2:4]
        x_peer, ctx_peer, h_peer, act_peer = theirs_of[layer]
        lows_peer, du_theirs = swap(lows), swap(du_peer)
        ahead = [((lows, 0), (lows_peer, 0), act_own, act_peer, 0), (hlow, h_peer, du_own, du_theirs, 1)]
        if not flying:
            (down,) = weight_grads(place, [XY], [ahead[0]], dp, 512)
            (up,) = weight_grads(place, [YX], [(*ahead[1][:4], 0)], dp, 512)
            down.launch()
            up.launch()
        else:
            group = weight_grads(place, TURNS[:2], ahead, dp, 512)
            group[0].launch()
            group[1].launch()
            high = step_as_one(*flying)
            group += weight_grads(place, TURNS[2:], [(*a, 0) for a in above], dp, half)
            group[2].launch()
        sums = (sums1, sums2, gbu_own, gbu_peer)
        below = ()
        if layer:
            n1, rstd1, _, _, _, slope, _, n2, rstd2 = kept[layer - 1][2]
            below = (n1, rstd1, slope, n2, rstd2, peers[layer - 1])
        back = attend_back(
            layer, scalars, count, (lows, 1), held, peers[layer], qkv, lse, sums, pack, below
        )
        ours, others, mine, theirs = back[:4]
        pack = (mine, theirs)
        others = swap(others)
        above = [((lows, 1), (lows_peer, 1), ctx_own, ctx_peer)]
        above += [(x_in, x_peer, (ours, i), (others, i)) for i in range(3)]
        if not layer:
            step(high, micros=12)
            step(*group, micros=8)
        if layer:
            Order.also = [*theirs_of[layer - 1][2:], ctx_peer]
            step(down, up, micros=8)
            sums2, du_own, du_peer, gbu_own, gbu_peer, lows, sums1 = back[4:]
            flying = [down, up]
    encoded = give_row(y[0], y[1])
    bits = dp.bit_length() - 1
    left = list(range(bits - 1, -1, -1))
    total, got = mine, swap(theirs)

    def small_step(total, got):
        whole_one = whole(*total.shape)
        (total,) = run(
            sum_kernel, 1, place, [(whole_one, total), (whole_one, got)], [(whole_one, total.shape, F32)], [], 8
        )
        return total, flip(total, left.pop(0), dp)

    third = half // 3
    goals = (0,), ((0, third), (1, 2 * third)), ((1, 2 * third), (2, third)), (2,)
    last = weight_grads(place, TURNS, [(*a, *g) for a, g in zip(above, goals)], dp, half)
    for f in last:
        f.launch()
    total, got = small_step(total, got)
    token_grad = give_row(back[4], back[5])
    while high.order:
        step(high)
    settle(high)
    step(*group)
    step(*last)
    total, got = small_step(total, got)
    middle = step_as_one(*group)
    step(*last)
    total, got = small_step(total, got)
    low = step_as_one(*last)
    total, got = small_step(total, got)
    rest = [middle, low]
    while any(f.order for f in rest) or left:
        for f in rest:
            if f.order:
                step(f)
        if left:
            total, got = small_step(total, got)

    starts = [*((0, 0), (0, ff)), *((2, i * half) for i in range(4))]
    upper = [*((1, 0), (1, ff)), *((0, 2 * ff + i * half) for i in range(4))]
    small = [half, half, ff] + [width] * 6
    gwd, gwu, gwo, gwq, gwk, gwv, gbq, gbv, gbu, gfg, gfs, gbo, gsg, gss, gbd = last_sums(
        place, [middle, high, low], [list(p) for p in zip(starts, upper)], [ff, ff] + [half] * 4, total, got, small
    )
    return (
        encoded, token_grad, gwq, gbq, gwk, gwv, gbv, gwo, gbo, gfg, gfs, gwu, gbu, gwd, gbd, gsg, gss,
    )


def solution(mesh):
    cols, mats, rep = P(None, "mp"), P(None, None, "mp"), P()
    placed = (
        P("dp", "mp", None), P("dp", None), P("dp", "mp", None),
        mats, cols, mats, mats, cols, mats, rep, rep, rep, mats, cols, mats, rep, rep, rep,
    )
    grads = P(None, "dp", "mp")
    return jax.shard_map(
        functools.partial(shards, mesh.shape["dp"]),
        mesh=mesh,
        in_specs=placed,
        out_specs=(
            P("dp", "mp", None), P("dp", "mp", None), grads, cols, grads, grads, cols,
            grads, rep, rep, rep, grads, cols, grads, rep, rep, rep,
        ),
        check_vma=False,
    )
```

```python
import functools

import jax
import jax.numpy as jnp
from jax import lax
from jax.experimental import pallas as pl
from jax.experimental.pallas import tpu as pltpu
from jax.sharding import PartitionSpec as P

DH = 64
QSLOT = 32
BF = jnp.bfloat16
F32 = jnp.float32
PAIR = 2 * DH
CHUNK = 512


def nn(left, right):
    return lax.dot_general(left, right, (((1,), (0,)), ((), ())), preferred_element_type=F32)


def nt(left, right):
    return lax.dot_general(left, right, (((1,), (1,)), ((), ())), preferred_element_type=F32)


def tn(left, right):
    return lax.dot_general(left, right, (((0,), (0,)), ((), ())), preferred_element_type=F32)


def beside(*refs):
    return jnp.concatenate([r[...] for r in refs], axis=1)


def whole(*shape):
    return pl.BlockSpec(shape, lambda i, *s: (0,) * len(shape))


def columns(rows, width, start=0):
    return pl.BlockSpec((rows, width), lambda i, *s: (0, start + i))


def layer_columns(layer, array, width):
    at = layer if array.shape[0] > 1 else 0
    return pl.BlockSpec((None, array.shape[1], width), lambda i, *s: (at, 0, i)), array


def layer_whole(layer, array):
    at = layer if array.shape[0] > 1 else 0
    return pl.BlockSpec((None, *array.shape[1:]), lambda i, *s: (at, 0, 0)), array


def my_row(array):
    return pl.BlockSpec((None, *array.shape[1:]), lambda i, s: (s[0], 0, 0))


def sds(shape, dtype):
    return jax.ShapeDtypeStruct(shape, dtype)


class Order:
    last = None
    also = ()


def run(kernel, grid, scalars, ins, outs, scratch, megabytes, pinned=False, micros=0.05):
    shape = pltpu.HBM if pinned in (True, "out") else sds
    arrays = [a for _, a in ins]
    kept = range(len(arrays)) if pinned is True else pinned if isinstance(pinned, list) else ()
    for i in kept:
        arrays[i] = pltpu.with_memory_space_constraint(arrays[i], pltpu.HBM)
    extra = [pltpu.with_memory_space_constraint(a, pltpu.HBM) for a in Order.also]
    extra += [] if Order.last is None else [Order.last]
    Order.also = ()
    count = 1 + len(ins)

    def body(*refs):
        kernel(*refs[:count], *refs[count + len(extra) :])

    made = pl.pallas_call(
        body,
        grid_spec=pltpu.PrefetchScalarGridSpec(
            num_scalar_prefetch=1,
            grid=(grid,),
            in_specs=[b for b, _ in ins] + [pl.BlockSpec(memory_space=pl.ANY)] * len(extra),
            out_specs=[b for b, _, _ in outs],
            scratch_shapes=scratch,
        ),
        out_shape=[shape(dims, dtype) for _, dims, dtype in outs],
        compiler_params=pltpu.CompilerParams(vmem_limit_bytes=megabytes * 1024 * 1024),
        cost_estimate=pl.CostEstimate(flops=1000 + int(1e9 * micros), transcendentals=0, bytes_accessed=1000),
    )(scalars, *arrays, *extra)
    Order.last = made[-1]
    if shape is pltpu.HBM:
        Order.last = pltpu.with_memory_space_constraint(made[-1], pltpu.HBM)
    return made


def row_of(ref, layer):
    return ref[layer : layer + 1, :].astype(F32)


def segments(scalars, count, slots, dim):
    shape = (slots, 1) if dim == 0 else (1, slots)
    slot = lax.broadcasted_iota(jnp.int32, shape, dim) + scalars[0] * (slots // 2)
    slot = jnp.where(slot >= slots, slot - slots, slot)
    base = 1 + scalars[0] * count
    shift = jnp.where(scalars[base + 1] > 0, QSLOT.bit_length() - 1, slots.bit_length() - 1)
    segment = lax.shift_right_logical(slot, jnp.broadcast_to(shift, shape))
    inside = slot - lax.shift_left(segment, jnp.broadcast_to(shift, shape))
    length = jnp.zeros(shape, jnp.int32)
    for k in range(count):
        length = jnp.where(segment == k, scalars[base + k], length)
    return segment, jnp.where(inside < length, segment, -1)


def attend_kernel(layer, count, split, scalars, *refs):
    refs = list(refs)
    xs = [refs.pop(0) for _ in range(2 if split else 1)]
    qkv, co, cp, lse = refs[10:14]
    bias = refs[-1]
    x = refs[14] if split else xs[0]
    slots = co.shape[0]

    @pl.when(pl.program_id(0) == 0)
    def _():
        segment, _ = segments(scalars, count, slots, 0)
        _, live = segments(scalars, count, slots, 1)
        bias[...] = jnp.where(segment == live, 0.0, -1e9)
        if split:
            x[...] = jnp.concatenate([r[...] for r in xs], axis=0)

    attend_step(layer, x[...], refs[:10], qkv, (co, cp), lse, bias, 0)


def attend_step(layer, xv, operands, qkv, ctx, lse, bias, column):
    wqo, wqp, wko, wkp, wvo, wvp, bqo, bqp, bvo, bvp = operands
    q = (nn(xv, beside(wqo, wqp)) + both(bqo, bqp, layer)).astype(BF)
    k = nn(xv, beside(wko, wkp)).astype(BF)
    v = (nn(xv, beside(wvo, wvp)) + both(bvo, bvp, layer)).astype(BF)
    first = lax.broadcasted_iota(jnp.int32, (1, PAIR), 1) < DH
    lse[...] = jnp.zeros_like(lse)
    for pair, cr in enumerate(ctx):
        at = slice(pair * PAIR, (pair + 1) * PAIR)
        qq, kk, vv = q[:, at], k[:, at], v[:, at]
        for i, part in enumerate((qq, kk, vv)):
            qkv[2 * i + pair, :, :] = part
        outs, peaks = [], []
        for head in range(2):
            mine = first if head == 0 else ~first
            qm = jnp.where(mine, qq, jnp.zeros_like(qq)) * 0.125
            s = nt(qm.astype(BF), kk) + bias[...]
            peak = jnp.max(s, axis=1, keepdims=True)
            e = jnp.exp(s - peak).astype(BF)
            outs.append(nn(e, jnp.where(mine, vv, jnp.ones_like(vv))))
            peaks.append(peak)
        total = pltpu.roll(jnp.where(first, outs[1], outs[0]), DH, 1)
        cr[:, pl.ds(column, PAIR)] = (jnp.where(first, outs[0], outs[1]) / total).astype(BF)
        logs = jnp.where(first, peaks[0], peaks[1]) + jnp.log(total)
        flat = logs.T
        lse[2 * pair : 2 * pair + 1, :] = flat[0:1, :]
        lse[2 * pair + 1 : 2 * pair + 2, :] = flat[DH : DH + 1, :]


def triple(count, slots):
    return pl.BlockSpec((count, slots, PAIR), lambda i, *s: (0, 0, i))


def both(own, peer, layer):
    return jnp.concatenate([row_of(own, layer), row_of(peer, layer)], axis=1)


def attend(layer, scalars, count, x, own, peer):
    split = isinstance(x, tuple)
    layers, width, half = own["w_query"].shape
    slots = 2 * x[0].shape[1] if split else x.shape[0]
    steps = half // PAIR
    act = columns(slots, PAIR)
    ins = [(my_row(a), a) for a in x] if split else [(whole(slots, width), x)]
    for name in ("w_query", "w_key", "w_value"):
        ins += [layer_columns(layer, own[name], PAIR), layer_columns(layer, peer[name], PAIR)]
    ins += [(columns(layers, PAIR), own["b_query"]), (columns(layers, PAIR, 4 * steps), peer["biases"])]
    ins += [(columns(layers, PAIR), own["b_value"]), (columns(layers, PAIR, 5 * steps), peer["biases"])]
    outs = [(triple(6, slots), (6, slots, half), BF)] + [(act, (slots, half), BF)] * 2
    outs += [(pl.BlockSpec((None, 8, slots), lambda i, *s: (i, 0, 0)), (steps, 8, slots), F32)]
    if split:
        outs += [(whole(slots, width), (slots, width), BF)]
    kernel = functools.partial(attend_kernel, layer, count, split)
    return run(kernel, steps, scalars, ins, outs, [pltpu.VMEM((slots, slots), F32)], 32, True)


def normalize(r):
    mean = jnp.mean(r, axis=1, keepdims=True)
    c = r - mean
    rstd = lax.rsqrt(jnp.mean(c * c, axis=1, keepdims=True) + 1e-12)
    return c * rstd, rstd


def norm_back(dy, n, rstd, gain):
    gdy = dy * gain
    return (
        gdy - jnp.mean(gdy, axis=1, keepdims=True) - n * jnp.mean(gdy * n, axis=1, keepdims=True)
    ) * rstd


def colsum(v):
    return jnp.sum(v.astype(F32), axis=0, keepdims=True)


def norm_back_store(dy, n, rstd, gain, low, sums):
    lowv = norm_back(dy, n, rstd, gain).astype(BF)
    low[:, :] = lowv
    sums[...] = jnp.concatenate(
        [colsum(dy * n), colsum(dy), colsum(lowv), jnp.zeros((5, dy.shape[1]), F32)], axis=0
    )


def gelu_step(low, up, up_bias):
    u = nn(low, up) + up_bias
    cdf = 0.5 * (1.0 + lax.erf(u * 0.7071067811865476))
    act = (u * cdf).astype(BF)
    return act, (cdf + u * (jnp.exp(u * u * -0.5) * 0.3989422804014327)).astype(BF)


def first_norm(layer, x, ctx, projection, b_out, g1, s1):
    n, rstd = normalize(x.astype(F32) + (nt(ctx, projection) + row_of(b_out, layer)))
    return n, rstd, n * row_of(g1, layer) + row_of(s1, layer)


def feed_kernel(layer, scalars, *refs):
    (x, co, cp, woo, wop, b_out, g1, s1, wuo, wup, wdo, wdp, buo, bup, b_down, g2, s2) = refs[:17]
    (n1, rstd1, hlow, acto, actp, gp, y, n2, rstd2, h, acc) = refs[17:]
    step = pl.program_id(0)

    @pl.when(step == 0)
    def _():
        n, rstd, hv = first_norm(layer, x[...], beside(co, cp), beside(woo, wop), b_out, g1, s1)
        n1[...] = n.astype(BF)
        rstd1[...] = rstd
        h[...] = hv
        hlow[...] = hv.astype(BF)
        acc[...] = jnp.zeros_like(acc)

    act, slope = gelu_step(hlow[...], beside(wuo, wup), both(buo, bup, layer))
    acto[...] = act[:, :CHUNK]
    actp[...] = act[:, CHUNK:]
    gp[0, :, :] = slope[:, :CHUNK]
    gp[1, :, :] = slope[:, CHUNK:]
    acc[...] += nt(act, beside(wdo, wdp))

    @pl.when(step == pl.num_programs(0) - 1)
    def _():
        n, rstd = normalize(h[...] + (acc[...] + row_of(b_down, layer)))
        y[...] = (n * row_of(g2, layer) + row_of(s2, layer)).astype(BF)
        n2[...] = n.astype(BF)
        rstd2[...] = rstd


def feed(layer, scalars, x, ctx_own, ctx_peer, own, peer):
    layers, width, half = own["w_query"].shape
    slots = x.shape[0]
    ff = own["w_up"].shape[2]
    full = whole(slots, width)
    one = whole(slots, 1)
    vec = whole(layers, width)
    act = columns(slots, CHUNK)
    part = whole(slots, half)
    ins = [(full, x), (part, ctx_own), (part, ctx_peer), layer_whole(layer, own["w_out"]), layer_whole(layer, peer["w_out"])]
    ins += [(vec, own[n]) for n in ("b_out", "first_gain", "first_shift")]
    for name in ("w_up", "w_down"):
        ins += [layer_columns(layer, own[name], CHUNK), layer_columns(layer, peer[name], CHUNK)]
    ins += [(columns(layers, CHUNK), own["b_up"]), (columns(layers, CHUNK), peer["biases"])]
    ins += [(vec, own[n]) for n in ("b_down", "second_gain", "second_shift")]
    outs = [(full, (slots, width), BF), (one, (slots, 1), F32), (full, (slots, width), BF)]
    outs += [(act, (slots, ff), BF)] * 2
    outs += [(pl.BlockSpec((2, slots, CHUNK), lambda i, *s: (0, 0, i)), (2, slots, ff), BF)]
    outs += [(full, (slots, width), BF), (full, (slots, width), BF), (one, (slots, 1), F32)]
    scratch = [pltpu.VMEM((slots, width), F32)] * 2
    return run(functools.partial(feed_kernel, layer), ff // CHUNK, scalars, ins, outs, scratch, 60, True)


class Loads:
    def __init__(self, sources, targets, sems):
        self.copies = [pltpu.make_async_copy(s, t, sems.at[i]) for i, (s, t) in enumerate(zip(sources, targets))]

    def start(self):
        for c in self.copies:
            c.start()

    def wait(self):
        for c in self.copies:
            c.wait()


def layer_of(ref, layer):
    return ref.at[layer if ref.shape[0] > 1 else 0]


def slope_step(chunk, low, gp, down, up, duo, dup, gbuo, gbup):
    du = (nn(low, down) * gp.astype(F32)).astype(BF)
    duo[...] = du[:, :CHUNK]
    dup[...] = du[:, CHUNK:]
    total = colsum(du)
    gbuo[:, chunk] = total[:, :CHUNK]
    gbup[:, chunk] = total[:, CHUNK:]
    return nt(du, up)


def columns_of(refs, chunk):
    return jnp.concatenate([r[:, chunk] for r in refs], axis=1)


def turn_kernel(layer, count, scalars, *refs):
    x, attention, weights, rest = refs[0], refs[1:11], refs[11:17], list(refs[17:])
    (b_out, g1, s1, buo, bup, b_down, g2, s2, cot_a, cot_b) = rest[:10]
    (qkv, co, cp, lse, hlow, acto, actp, y, gbuo, gbup, sums2, duo, dup, both_low, sums1) = rest[10:25]
    (bias, woo, wop, wuo, wup, wdo, wdp, gp, h, acc, n1, rstd1, sems) = rest[25:]
    dff, datt = both_low.at[0], both_low.at[1]
    step = pl.program_id(0)
    slots = co.shape[0]
    attending = co.shape[1] // PAIR
    feeding = gp.shape[2] // CHUNK
    loads = Loads([layer_of(w, layer) for w in weights], (woo, wop, wuo, wup, wdo, wdp), sems)

    @pl.when(step == 0)
    def _():
        loads.start()
        segment, _ = segments(scalars, count, slots, 0)
        _, live = segments(scalars, count, slots, 1)
        bias[...] = jnp.where(segment == live, 0.0, -1e9)

    @pl.when(step < attending)
    def _():
        attend_step(layer, x[...], attention, qkv, (co, cp), lse, bias, pl.multiple_of(step * PAIR, PAIR))

    @pl.when(step == attending)
    def _():
        loads.wait()
        n, rstd, hv = first_norm(layer, x[...], beside(co, cp), beside(woo, wop), b_out, g1, s1)
        n1[...] = n
        rstd1[...] = rstd
        h[...] = hv
        hlow[...] = hv.astype(BF)
        acc[...] = jnp.zeros_like(acc)

    @pl.when((step >= attending) & (step < attending + feeding))
    def _():
        chunk = pl.ds(pl.multiple_of((step - attending) * CHUNK, CHUNK), CHUNK)
        up_bias = jnp.concatenate([r[layer : layer + 1, chunk].astype(F32) for r in (buo, bup)], axis=1)
        act, slope = gelu_step(hlow[...], columns_of((wuo, wup), chunk), up_bias)
        acto[...] = act[:, :CHUNK]
        actp[...] = act[:, CHUNK:]
        gp[0, :, chunk] = slope[:, :CHUNK]
        gp[1, :, chunk] = slope[:, CHUNK:]
        acc[...] += nt(act, columns_of((wdo, wdp), chunk))

    @pl.when(step == attending + feeding - 1)
    def _():
        n, rstd = normalize(h[...] + (acc[...] + row_of(b_down, layer)))
        result = (n * row_of(g2, layer) + row_of(s2, layer)).astype(BF)
        y[0, :, :] = result[: slots // 2]
        y[1, :, :] = result[slots // 2 :]
        dy = jnp.concatenate([cot_a[...], cot_b[...]], axis=0).astype(F32)
        norm_back_store(dy, n, rstd, row_of(g2, layer), dff, sums2)
        acc[...] = dff[...].astype(F32)

    @pl.when(step >= attending + feeding)
    def _():
        chunk = pl.ds(pl.multiple_of((step - attending - feeding) * CHUNK, CHUNK), CHUNK)
        slope = jnp.concatenate([gp[0, :, chunk], gp[1, :, chunk]], axis=1)
        acc[...] += slope_step(
            chunk, dff[...], slope, columns_of((wdo, wdp), chunk), columns_of((wuo, wup), chunk),
            duo, dup, gbuo, gbup,
        )

    @pl.when(step == pl.num_programs(0) - 1)
    def _():
        norm_back_store(acc[...], n1[...], rstd1[...], row_of(g1, layer), datt, sums1)


def turn(layer, scalars, count, x, own, peer, cotangent):
    layers, width, half = own["w_query"].shape
    slots, ff = x.shape[0], own["w_up"].shape[2]
    attending, feeding = half // PAIR, ff // CHUNK

    def early(rows, start=0):
        return pl.BlockSpec((rows, PAIR), lambda i, *s: (0, start + jnp.clip(i, 0, attending - 1)))

    def early_weight(array):
        at = layer if array.shape[0] > 1 else 0
        return pl.BlockSpec((None, width, PAIR), lambda i, *s: (at, 0, jnp.clip(i, 0, attending - 1))), array

    full, vec = whole(slots, width), whole(layers, width)
    anywhere = pl.BlockSpec(memory_space=pl.ANY)
    ins = [(full, x)]
    for name in ("w_query", "w_key", "w_value"):
        ins += [early_weight(own[name]), early_weight(peer[name])]
    ins += [(early(layers), own["b_query"]), (early(layers, 4 * attending), peer["biases"])]
    ins += [(early(layers), own["b_value"]), (early(layers, 5 * attending), peer["biases"])]
    for name in ("w_out", "w_up", "w_down"):
        ins += [(anywhere, own[name]), (anywhere, peer[name])]
    ins += [(vec, own[n]) for n in ("b_out", "first_gain", "first_shift")]
    ins += [(whole(*a.shape), a) for a in (own["b_up"], peer["biases"])]
    ins += [(vec, own[n]) for n in ("b_down", "second_gain", "second_shift")]
    ins += [(my_row(a), a) for a in cotangent]
    late = pl.BlockSpec((slots, CHUNK), lambda i, *s: (0, jnp.clip(i - attending, 0, feeding - 1)))
    halves = (2, slots // 2, width)
    outs = [
        (pl.BlockSpec((6, slots, PAIR), lambda i, *s: (0, 0, jnp.clip(i, 0, attending - 1))), (6, slots, half), BF)
    ]
    outs += [(whole(slots, half), (slots, half), BF)] * 2
    outs += [
        (pl.BlockSpec((None, 8, slots), lambda i, *s: (jnp.clip(i, 0, attending - 1), 0, 0)), (attending, 8, slots), F32)
    ]
    outs += [(full, (slots, width), BF)] + [(late, (slots, ff), BF)] * 2 + [(whole(*halves), halves, BF)]
    outs += [(whole(1, ff), (1, ff), F32)] * 2 + [(whole(8, width), (8, width), F32)]
    latest = pl.BlockSpec((slots, CHUNK), lambda i, *s: (0, jnp.clip(i - attending - feeding, 0, feeding - 1)))
    outs += [(latest, (slots, ff), BF)] * 2
    outs += [(whole(2, slots, width), (2, slots, width), BF), (whole(8, width), (8, width), F32)]
    scratch = [pltpu.VMEM((slots, slots), F32)] + [pltpu.VMEM((width, half), BF)] * 2
    scratch += [pltpu.VMEM((width, ff), BF)] * 4 + [pltpu.VMEM((2, slots, ff), BF)]
    scratch += [pltpu.VMEM((slots, width), F32)] * 3 + [pltpu.VMEM((slots, 1), F32), pltpu.SemaphoreType.DMA((6,))]
    kernel = functools.partial(turn_kernel, layer, count)
    return run(kernel, attending + 2 * feeding, scalars, ins, outs, scratch, 56, True)


def attend_back_kernel(layer, count, above, scalars, *refs):
    rest = list(refs)

    def take(n):
        return [rest.pop(0) for _ in range(n)]

    datt, woo, wop, wqo, wqp, wko, wkp, wvo, wvp, qkv, lse, sums1, sums2, gbuo, gbup = take(15)
    upper = take(2) if above else None
    if layer:
        n2, rstd2, gain2, n1, rstd1, gain1 = take(6)
        sources = take(5)
    ours, others, mine, theirs = take(4)
    if layer:
        below2, duo, dup, below_gbuo, below_gbup, both_low, below1 = take(7)
        dff, below_datt = both_low.at[0], both_low.at[1]
    else:
        dx_own, dx_peer = take(2)
    dx, bias = take(2)
    step = pl.program_id(0)
    slots = datt.shape[0]
    attending = down_steps(mine)
    if layer:
        wuo, wup, wdo, wdp, gp, sems = take(6)
        loads = Loads(
            [*[layer_of(w, layer - 1) for w in sources[:4]], sources[4]], (wuo, wup, wdo, wdp, gp), sems
        )

    @pl.when(step == 0)
    def _():
        if layer:
            loads.start()
        _, live = segments(scalars, count, slots, 0)
        segment, _ = segments(scalars, count, slots, 1)
        bias[...] = jnp.where(segment == live, 0.0, -1e9)
        rows = jnp.concatenate([sums1[0:3, :], sums2[0:3, :]], axis=0)
        for i, (pack, gbu) in enumerate(((mine, gbuo), (theirs, gbup))):
            width = pack.shape[1]
            pack[:16, :] = jnp.concatenate(
                [rows, gbu[:, :width], gbu[:, width:], jnp.zeros((8, width), F32)], axis=0
            )
            if above:
                pack[16:, :] = upper[i][...]
        dx[...] = datt[...].astype(F32)

    @pl.when(step < attending)
    def _():
        dctx = nn(datt[...], beside(woo, wop)).astype(BF)
        first = lax.broadcasted_iota(jnp.int32, (1, PAIR), 1) < DH
        grads = []
        for pair, pack in enumerate((mine, theirs)):
            qq, kk, vv = (qkv[2 * i + pair, :, :] for i in range(3))
            do = dctx[:, pair * PAIR : (pair + 1) * PAIR]
            dq_t, dk, dv = 0.0, 0.0, 0.0
            for head in range(2):
                sel = first if head == 0 else ~first
                qm = (jnp.where(sel, qq, jnp.zeros_like(qq)) * 0.125).astype(BF)
                km = (jnp.where(sel, kk, jnp.zeros_like(kk)) * 0.125).astype(BF)
                dom = jnp.where(sel, do, jnp.zeros_like(do))
                at = 2 * pair + head
                p = jnp.exp(nt(kk, qm) + bias[...] - lse[at : at + 1, :])
                dp = nt(vv, dom)
                delta = jnp.sum(p * dp, axis=0, keepdims=True)
                ds = (p * (dp - delta)).astype(BF)
                dv += nn(p.astype(BF), dom)
                dk += nn(ds, qm)
                dq_t += nn(km.T, ds)
            dq = dq_t.T.astype(BF)
            dk = dk.astype(BF)
            dv = dv.astype(BF)
            for i, part in enumerate((dq, dk, dv)):
                (others if pair else ours)[i, :, :] = part
            pack[8:9, pl.ds(pl.multiple_of(step * PAIR, PAIR), PAIR)] = colsum(dq)
            pack[8:9, pl.ds(pl.multiple_of((step + attending) * PAIR, PAIR), PAIR)] = colsum(dv)
            grads.append((dq, dk, dv))
        back = jnp.concatenate([g[i] for i in range(3) for g in grads], axis=1)
        dx[...] += nt(back, beside(wqo, wqp, wko, wkp, wvo, wvp))

    if not layer:

        @pl.when(step == attending - 1)
        def _():
            dx_own[...] = dx[: slots // 2, :]
            dx_peer[...] = dx[slots // 2 :, :].astype(BF)

        return

    @pl.when(step == attending)
    def _():
        loads.wait()
        norm_back_store(dx[...], n2[...].astype(F32), rstd2[...], row_of(gain2, layer - 1), dff, below2)
        dx[...] = dff[...].astype(F32)

    @pl.when(step >= attending)
    def _():
        chunk = pl.ds(pl.multiple_of((step - attending) * CHUNK, CHUNK), CHUNK)
        slope = jnp.concatenate([gp[0, :, chunk], gp[1, :, chunk]], axis=1)
        dx[...] += slope_step(
            chunk, dff[...], slope, columns_of((wdo, wdp), chunk), columns_of((wuo, wup), chunk),
            duo, dup, below_gbuo, below_gbup,
        )

    @pl.when(step == pl.num_programs(0) - 1)
    def _():
        norm_back_store(dx[...], n1[...].astype(F32), rstd1[...], row_of(gain1, layer - 1), below_datt, below1)


def down_steps(pack):
    return pack.shape[1] // 2 // PAIR


def attend_back(layer, scalars, count, lows, own, peer, saved, lse, sums, above, below):
    lows, pick = lows
    slots, width = lows.shape[1:]
    layers, _, half = own["w_query"].shape
    ff = own["w_up"].shape[2]
    attending, feeding = half // PAIR, ff // CHUNK if layer else 0

    def at(i):
        return jnp.clip(i, 0, attending - 1)

    def early_weight(array):
        k = layer if array.shape[0] > 1 else 0
        return pl.BlockSpec((None, width, PAIR), lambda i, *s: (k, 0, at(i))), array

    def stack(n):
        return pl.BlockSpec((n, slots, PAIR), lambda i, *s: (0, 0, at(i)))

    full, one = whole(slots, width), whole(slots, 1)
    vec = whole(layers, width)
    ins = [(pl.BlockSpec((None, slots, width), lambda i, *s: (pick, 0, 0)), lows)]
    for name in ("w_out", "w_query", "w_key", "w_value"):
        ins += [early_weight(own[name]), early_weight(peer[name])]
    ins += [(stack(6), saved), (pl.BlockSpec((None, 8, slots), lambda i, *s: (at(i), 0, 0)), lse)]
    ins += [(whole(*a.shape), a) for a in (*sums, *above)]
    packed = (16 * (layers - layer), width)
    outs = [(stack(3), (3, slots, half), BF)] * 2
    outs += [(whole(*packed), packed, F32)] * 2
    scratch = [pltpu.VMEM((slots, width), F32), pltpu.VMEM((slots, slots), F32)]
    row = (whole(8, width), (8, width), F32)
    if layer:
        n1, rstd1, slope, n2, rstd2, lower = below
        ins += [(full, n2), (one, rstd2), (vec, own["second_gain"]), (full, n1), (one, rstd1), (vec, own["first_gain"])]
        anywhere = pl.BlockSpec(memory_space=pl.ANY)
        ins += [(anywhere, a) for a in (own["w_up"], lower["w_up"], own["w_down"], lower["w_down"], slope)]
        latest = pl.BlockSpec((slots, CHUNK), lambda i, *s: (0, jnp.clip(i - attending, 0, feeding - 1)))
        outs += [row] + [(latest, (slots, ff), BF)] * 2
        outs += [(whole(1, ff), (1, ff), F32)] * 2 + [(whole(2, slots, width), (2, slots, width), BF), row]
        scratch += [pltpu.VMEM((width, ff), BF)] * 4 + [pltpu.VMEM((2, slots, ff), BF), pltpu.SemaphoreType.DMA((5,))]
    else:
        outs += [(whole(slots // 2, width), (slots // 2, width), t) for t in (F32, BF)]
    kernel = functools.partial(attend_back_kernel, layer, count, bool(above))
    return run(kernel, attending + feeding, scalars, ins, outs, scratch, 52, True)


def halves_of(value, bit, scalars, left, base):
    axis = left.index(bit)
    rows, width = value.shape
    cut = value.reshape(1 << axis, 2, rows >> (axis + 1), width)
    mine = (scalars[base] >> bit) & 1
    low, high = cut[:, 0].reshape(rows // 2, width), cut[:, 1].reshape(rows // 2, width)
    return jnp.where(mine == 0, low, high), jnp.where(mine == 0, high, low)


def weight_kernel(plan, lefts, left, scalars, *refs):
    bits, plan = plan
    step = pl.program_id(0)
    pieces = len(plan)
    sides, operands = refs[: 2 * lefts], refs[2 * lefts : 2 * lefts + 2 * pieces]
    outs, (lt, right) = refs[2 * lefts + 2 * pieces : -2], refs[-2:]
    slots = sides[0].shape[0]
    for n, (start, steps, block, side, fresh, places) in enumerate(plan):
        ro, rp = operands[2 * n : 2 * n + 2]
        if fresh:

            @pl.when(step == start)
            def _(side=side):
                lt[:, :slots] = sides[2 * side][...].T
                lt[:, slots:] = sides[2 * side + 1][...].T

        @pl.when((step >= start) & (step < start + steps))
        def _(ro=ro, rp=rp, block=block, start=start, places=places):
            right[:slots, :block] = ro[...]
            right[slots:, :block] = rp[...]
            value = nn(lt[...], right[:, :block])
            cut = 0
            for g, column, wide in places:
                part = value[:, cut : cut + wide]
                cut += wide
                at = pl.ds(pl.multiple_of(column + (step - start) * block, 128), wide)
                if bits[g] is None:
                    outs[g][:, at] = part.astype(BF)
                else:
                    keep, send = halves_of(part, bits[g], scalars, left, 1)
                    outs[2 * g][:, at] = keep.astype(BF)
                    outs[2 * g + 1][:, at] = send.astype(BF)


def weight_grads(scalars, orders, parts, size, block):
    bits = size.bit_length() - 1
    left = list(range(bits - 1, -1, -1))
    plan, ins, outs, wide, sides = [], [], [], [], {}
    at = 0

    def parted(operand):
        return operand if isinstance(operand, tuple) else (operand, None)

    def side_spec(pick):
        if pick is None:
            return pl.BlockSpec((slots, width), lambda i, *s: (0, 0), pipeline_mode=pl.Buffered(1))
        return pl.BlockSpec((None, slots, width), lambda i, *s: (pick, 0, 0), pipeline_mode=pl.Buffered(1))

    slots, width = parted(parts[0][0])[0].shape[-2:]
    split = (width // size) % 16 == 0
    before = None
    filled = [0] * len(orders)
    for lo, lp, ro, rp, *goal in parts:
        (lo, pick), (lp, _) = parted(lo), parted(lp)
        key = (id(lo), pick)
        if key not in sides:
            sides[key] = len(sides)
            wide += [(side_spec(pick), lo), (side_spec(pick), lp)]
        (ro, pick), (rp, _) = parted(ro), parted(rp)
        units = rp.shape[-1]
        blk = min(block, units)
        steps = units // blk
        places = []
        for g, many in goal if isinstance(goal[0], tuple) else ((goal[0], blk),):
            places.append((g, filled[g], many))
            filled[g] += many * steps
        plan.append((at, steps, blk, sides[key], sides[key] != before, places))
        before = sides[key]

        def spec(i, *s, a=at, n=steps, k=pick):
            place = jnp.clip(i - a, 0, n - 1)
            return (0, place) if k is None else (k, 0, place)

        shape = (slots, blk) if pick is None else (None, slots, blk)
        ins += [(pl.BlockSpec(shape, spec), ro), (pl.BlockSpec(shape, spec), rp)]
        at += steps
    rows = width // 2 if split else width
    for total in filled:
        outs += [(whole(rows, total), (rows, total), BF)] * (2 if split else 1)
    plan = ([o[0] if split else None for o in orders], plan)
    pins = [*range(len(wide) + len(ins))]
    scratch = [pltpu.VMEM((width, 2 * slots), BF), pltpu.VMEM((2 * slots, block), BF)]
    kernel = functools.partial(weight_kernel, plan, len(sides), left)
    made = run(kernel, at, scalars, [*wide, *ins], outs, scratch, 36, pins)
    if split:
        return [Scatter(scalars, o, size, made[2 * g], made[2 * g + 1]) for g, o in enumerate(orders)]
    return [Scatter(scalars, o, size, None, made[g]) for g, o in enumerate(orders)]


def add_kernel(plan, scalars, *refs):
    ins, outs = refs[: 2 * len(plan)], refs[2 * len(plan) :]
    for i, (bit, left) in enumerate(plan):
        value = ins[2 * i][...].astype(F32) + ins[2 * i + 1][...].astype(F32)
        if bit is None:
            outs[2 * i][...] = value
        else:
            kept, send = halves_of(value, bit, scalars, left, 1)
            outs[2 * i][...] = kept.astype(BF)
            outs[2 * i + 1][...] = send.astype(BF)


def merge_kernel(bit, left, scalars, *refs):
    ins, (keep, send) = refs[:-2], refs[-2:]
    at = 0
    for i in range(len(ins) // 2):
        value = ins[2 * i][...].astype(F32) + ins[2 * i + 1][...].astype(F32)
        kept, sent = halves_of(value, bit, scalars, left, 1)
        width = value.shape[1]
        keep[:, at : at + width] = kept.astype(BF)
        send[:, at : at + width] = sent.astype(BF)
        at += width


def land(*scatters, merge=False, micros=0.05):
    if not scatters:
        return None
    unit = scatters[0].keep.shape[0] >> len(scatters[0].order)
    if unit % 16:
        for f in scatters:
            f.part((f.keep.astype(F32) + f.value.astype(F32)).astype(BF))
        if merge:
            first = scatters[0]
            first.keep = jnp.concatenate([f.keep for f in scatters], axis=1)
            first.value = jnp.concatenate([f.value for f in scatters], axis=1)
            return first
        return None
    if merge:
        first = scatters[0]
        rows, total = first.keep.shape[0] // 2, sum(f.keep.shape[1] for f in scatters)
        ins = [(whole(*a.shape), a) for f in scatters for a in (f.keep, f.value)]
        kernel = functools.partial(merge_kernel, first.order[0], list(first.left))
        both_out = [(whole(rows, total), (rows, total), BF)] * 2
        first.keep, first.value = run(kernel, 1, first.scalars, ins, both_out, [], 32)
        return first
    steps = 1
    if max(f.keep.size for f in scatters) > 300000:
        steps = next(n for n in (3, 2, 1) if not any(f.keep.shape[1] % (128 * n) for f in scatters))
    ins, outs, plan = [], [], []
    for f in scatters:
        rows, width = f.keep.shape
        block = columns(rows, width // steps)
        ins += [(block, f.keep), (block, f.value)]
        outs += [(columns(rows // 2, width // steps), (rows // 2, width), BF)] * 2
        plan.append((f.order[0], list(f.left)))
    made = run(functools.partial(add_kernel, plan), steps, scatters[0].scalars, ins, outs, [], 32, micros=micros)
    for i, f in enumerate(scatters):
        f.keep, f.value = made[2 * i : 2 * i + 2]
    return None


class Scatter:
    def __init__(self, scalars, order, size, keep, send):
        bits = size.bit_length() - 1
        self.scalars, self.size = scalars, size
        self.order = [b for b in order if b < bits] + list(range(4, bits))
        self.left = list(range(bits - 1, -1, -1))
        self.keep, self.value = keep, send
        if keep is None:
            self.part(send)

    def part(self, value):
        bit = self.order[0]
        axis = self.left.index(bit)
        rows, width = value.shape
        cut = value.reshape(1 << axis, 2, rows >> (axis + 1), width)
        mine = (self.scalars[1] >> bit) & 1
        self.keep = lax.dynamic_index_in_dim(cut, mine, 1, keepdims=False).reshape(rows // 2, width)
        self.value = lax.dynamic_index_in_dim(cut, 1 - mine, 1, keepdims=False).reshape(rows // 2, width)

    def launch(self):
        bit = self.order.pop(0)
        self.left.remove(bit)
        self.value = flip(self.value, bit, self.size)
        return self


def settle_kernel(scalars, keep, got, out):
    out[...] = keep[...].astype(F32) + got[...].astype(F32)


def settle(scatter):
    rows, width = scatter.keep.shape
    block = whole(rows, width)
    (scatter.keep,) = run(
        settle_kernel, 1, scatter.scalars, [(block, scatter.keep), (block, scatter.value)],
        [(block, (rows, width), F32)], [], 16,
    )
    scatter.value = None


def last_kernel(plan, count, scalars, *refs):
    pairs, rest = [], list(refs)
    for n in count:
        pairs.append([rest.pop(0) for _ in range(n)])
    total, got = rest.pop(0), rest.pop(0)
    for out, layers in zip(rest, plan):
        for layer, (i, at) in enumerate(layers):
            cut = slice(at, at + out.shape[2])
            parts = [r[:, cut].astype(F32) for r in pairs[i]]
            out[layer, :, :] = sum(parts[1:], parts[0])
    gbq, gbv, gbu, *vectors = rest[len(plan) :]
    width = total.shape[1]
    sums = total[...] + got[...]
    for layer in range(len(plan[0])):
        mine = sums[16 * layer : 16 * layer + 16, :]
        row = slice(layer, layer + 1)
        for i, out in enumerate(vectors):
            out[row, :] = mine[i : i + 1, :]
        gbu[row, :width] = mine[6:7, :]
        gbu[row, width:] = mine[7:8, :]
        gbq[row, :] = mine[8:9, : width // 2]
        gbv[row, :] = mine[8:9, width // 2 :]


def last_sums(scalars, scatters, plan, widths, total, got, small):
    rows, layers = scatters[0].keep.shape[0], len(plan[0])
    arrays = [a for f in scatters for a in (f.keep, f.value) if a is not None] + [total, got]
    outs = [(whole(layers, rows, w), (layers, rows, w), F32) for w in widths]
    outs += [(whole(layers, n), (layers, n), F32) for n in small]
    kernel = functools.partial(last_kernel, plan, [1 if f.value is None else 2 for f in scatters])
    return run(kernel, 1, scalars, [(whole(*a.shape), a) for a in arrays], outs, [], 48, "out")


def copy_kernel(scalars, value, out):
    out[...] = value[...]


def sum_kernel(scalars, left, right, out):
    out[...] = left[...] + right[...]


def swap(value):
    return lax.ppermute(value, "mp", [(0, 1), (1, 0)])


def flip(value, bit, size):
    return lax.ppermute(value, "dp", [(i, i ^ (1 << bit)) for i in range(size)])


NAMES = (
    "w_query", "b_query", "w_key", "w_value", "b_value", "w_out", "b_out", "first_gain", "first_shift",
    "w_up", "b_up", "w_down", "b_down", "second_gain", "second_shift",
)
XY, YX = (0, 1, 2, 3), (1, 0, 2, 3)
TURNS = (0, 1, 2, 3), (1, 2, 0, 3), (2, 0, 1, 3)


def shards(dp, tokens, lengths, cotangent, *given):
    held = dict(zip(NAMES, given, strict=True))
    layers, width, half = held["w_query"].shape
    ff = held["w_up"].shape[2]
    slots = 2 * tokens.shape[1]
    count = lengths.shape[1]
    me = lax.axis_index("mp")
    scalars = jnp.concatenate([me[None], lengths.reshape(-1)]).astype(jnp.int32)
    place = jnp.stack([me, lax.axis_index("dp")]).astype(jnp.int32)

    def give_row(mine, other):
        other = swap(other).astype(mine.dtype)
        return jnp.stack([jnp.where(me == 0, mine, other), jnp.where(me == 0, other, mine)])

    Order.last, Order.also = None, ()
    biases = swap(jnp.concatenate([held["b_up"], held["b_query"], held["b_value"]], axis=1))
    x = (tokens, swap(tokens))
    early = {n: swap(held[n]) for n in ("w_query", "w_key", "w_value")}
    names = ("w_out", "w_up", "w_down")
    pieces, early, biases, x = lax.optimization_barrier(([held[n][:1] for n in names], early, biases, x))
    first = {n: swap(p) for n, p in zip(names, pieces, strict=True)}
    peers = [{"biases": biases, **early, **first} for _ in range(layers)]

    def last_wave(after):
        pieces, cot, fresh, after = lax.optimization_barrier(([held[n] for n in names], cotangent, first, after))
        later = {n: swap(p) for n, p in zip(names, pieces, strict=True)}
        for layer in range(layers):
            peers[layer].update(later if layer else fresh)
        return (cot, swap(cot)), after

    kept = []
    for layer in range(layers - 1):
        made = attend(layer, scalars, count, x, held, peers[layer])
        if layer == 0:
            x = made[4]
            cot, x = last_wave(x)
        fed = feed(layer, scalars, x, made[1], made[2], held, peers[layer])
        kept.append((x, made[:4], fed))
        x = fed[6]
    made = turn(layers - 1, scalars, count, x, held, peers[-1], cot)
    kept.append((x, made[:4], (None, None, *made[4:7])))
    y, gbu_own, gbu_peer, sums2, du_own, du_peer, lows, sums1 = made[7:]

    def step(*scatters, micros=0.05):
        land(*scatters, micros=micros)
        for f in scatters:
            f.launch()

    def step_as_one(*scatters):
        return land(*scatters, merge=True).launch()

    pack, flying, above = (), [], None
    theirs_of = [[swap(a) for a in (x, att[2], fed[2], fed[4])] for x, att, fed in kept]
    Order.also = [a for arrays in theirs_of[:-1] for a in arrays[:2]] + [theirs_of[-1][0]]
    (sums1,) = run(
        copy_kernel, 1, place, [(whole(*sums1.shape), sums1)], [(whole(*sums1.shape), sums1.shape, F32)], [], 8,
        True, 20,
    )
    for layer in reversed(range(layers)):
        x_in, (qkv, ctx_own, _, lse), fed = kept[layer]
        hlow, act_own = fed[2:4]
        x_peer, ctx_peer, h_peer, act_peer = theirs_of[layer]
        lows_peer, du_theirs = swap(lows), swap(du_peer)
        ahead = [((lows, 0), (lows_peer, 0), act_own, act_peer, 0), (hlow, h_peer, du_own, du_theirs, 1)]
        if not flying:
            (down,) = weight_grads(place, [XY], [ahead[0]], dp, 512)
            (up,) = weight_grads(place, [YX], [(*ahead[1][:4], 0)], dp, 512)
            down.launch()
            up.launch()
        else:
            group = weight_grads(place, TURNS[:2], ahead, dp, 512)
            group[0].launch()
            group[1].launch()
            high = step_as_one(*flying)
            group += weight_grads(place, TURNS[2:], [(*a, 0) for a in above], dp, half)
            group[2].launch()
        sums = (sums1, sums2, gbu_own, gbu_peer)
        below = ()
        if layer:
            n1, rstd1, _, _, _, slope, _, n2, rstd2 = kept[layer - 1][2]
            below = (n1, rstd1, slope, n2, rstd2, peers[layer - 1])
        back = attend_back(
            layer, scalars, count, (lows, 1), held, peers[layer], qkv, lse, sums, pack, below
        )
        ours, others, mine, theirs = back[:4]
        pack = (mine, theirs)
        others = swap(others)
        above = [((lows, 1), (lows_peer, 1), ctx_own, ctx_peer)]
        above += [(x_in, x_peer, (ours, i), (others, i)) for i in range(3)]
        if not layer:
            step(high, micros=12)
            step(*group, micros=8)
        if layer:
            Order.also = [*theirs_of[layer - 1][2:], ctx_peer]
            step(down, up, micros=8)
            sums2, du_own, du_peer, gbu_own, gbu_peer, lows, sums1 = back[4:]
            flying = [down, up]
    encoded = give_row(y[0], y[1])
    bits = dp.bit_length() - 1
    left = list(range(bits - 1, -1, -1))
    total, got = mine, swap(theirs)

    def small_step(total, got):
        whole_one = whole(*total.shape)
        (total,) = run(
            sum_kernel, 1, place, [(whole_one, total), (whole_one, got)], [(whole_one, total.shape, F32)], [], 8
        )
        return total, flip(total, left.pop(0), dp)

    third = half // 3
    goals = (0,), ((0, third), (1, 2 * third)), ((1, 2 * third), (2, third)), (2,)
    last = weight_grads(place, TURNS, [(*a, *g) for a, g in zip(above, goals)], dp, half)
    for f in last:
        f.launch()
    total, got = small_step(total, got)
    token_grad = give_row(back[4], back[5])
    while high.order:
        step(high)
    settle(high)
    step(*group)
    step(*last)
    total, got = small_step(total, got)
    middle = step_as_one(*group)
    step(*last)
    total, got = small_step(total, got)
    low = step_as_one(*last)
    total, got = small_step(total, got)
    rest = [middle, low]
    while any(f.order for f in rest) or left:
        for f in rest:
            if f.order:
                step(f)
        if left:
            total, got = small_step(total, got)

    starts = [*((0, 0), (0, ff)), *((2, i * half) for i in range(4))]
    upper = [*((1, 0), (1, ff)), *((0, 2 * ff + i * half) for i in range(4))]
    small = [half, half, ff] + [width] * 6
    gwd, gwu, gwo, gwq, gwk, gwv, gbq, gbv, gbu, gfg, gfs, gbo, gsg, gss, gbd = last_sums(
        place, [middle, high, low], [list(p) for p in zip(starts, upper)], [ff, ff] + [half] * 4, total, got, small
    )
    return (
        encoded, token_grad, gwq, gbq, gwk, gwv, gbv, gwo, gbo, gfg, gfs, gwu, gbu, gwd, gbd, gsg, gss,
    )


def solution(mesh):
    cols, mats, rep = P(None, "mp"), P(None, None, "mp"), P()
    placed = (
        P("dp", "mp", None), P("dp", None), P("dp", "mp", None),
        mats, cols, mats, mats, cols, mats, rep, rep, rep, mats, cols, mats, rep, rep, rep,
    )
    grads = P(None, "dp", "mp")
    return jax.shard_map(
        functools.partial(shards, mesh.shape["dp"]),
        mesh=mesh,
        in_specs=placed,
        out_specs=(
            P("dp", "mp", None), P("dp", "mp", None), grads, cols, grads, grads, cols,
            grads, rep, rep, rep, grads, cols, grads, rep, rep, rep,
        ),
        check_vma=False,
    )
```

```python
import functools

import jax
import jax.numpy as jnp
from jax import lax
from jax.experimental import pallas as pl
from jax.experimental.pallas import tpu as pltpu
from jax.sharding import PartitionSpec as P

DH = 64
QSLOT = 32
BF = jnp.bfloat16
F32 = jnp.float32
PAIR = 2 * DH
CHUNK = 512


def nn(left, right):
    return lax.dot_general(left, right, (((1,), (0,)), ((), ())), preferred_element_type=F32)


def nt(left, right):
    return lax.dot_general(left, right, (((1,), (1,)), ((), ())), preferred_element_type=F32)


def tn(left, right):
    return lax.dot_general(left, right, (((0,), (0,)), ((), ())), preferred_element_type=F32)


def beside(*refs):
    return jnp.concatenate([r[...] for r in refs], axis=1)


def whole(*shape):
    return pl.BlockSpec(shape, lambda i, *s: (0,) * len(shape))


def columns(rows, width, start=0):
    return pl.BlockSpec((rows, width), lambda i, *s: (0, start + i))


def layer_columns(layer, array, width):
    at = layer if array.shape[0] > 1 else 0
    return pl.BlockSpec((None, array.shape[1], width), lambda i, *s: (at, 0, i)), array


def layer_whole(layer, array):
    at = layer if array.shape[0] > 1 else 0
    return pl.BlockSpec((None, *array.shape[1:]), lambda i, *s: (at, 0, 0)), array


def my_row(array):
    return pl.BlockSpec((None, *array.shape[1:]), lambda i, s: (s[0], 0, 0))


def sds(shape, dtype):
    return jax.ShapeDtypeStruct(shape, dtype)


class Order:
    last = None
    also = ()


def run(kernel, grid, scalars, ins, outs, scratch, megabytes, pinned=False, micros=0.05):
    shape = pltpu.HBM if pinned in (True, "out") else sds
    arrays = [a for _, a in ins]
    kept = range(len(arrays)) if pinned is True else pinned if isinstance(pinned, list) else ()
    for i in kept:
        arrays[i] = pltpu.with_memory_space_constraint(arrays[i], pltpu.HBM)
    extra = [pltpu.with_memory_space_constraint(a, pltpu.HBM) for a in Order.also]
    extra += [] if Order.last is None else [Order.last]
    Order.also = ()
    count = 1 + len(ins)

    def body(*refs):
        kernel(*refs[:count], *refs[count + len(extra) :])

    made = pl.pallas_call(
        body,
        grid_spec=pltpu.PrefetchScalarGridSpec(
            num_scalar_prefetch=1,
            grid=(grid,),
            in_specs=[b for b, _ in ins] + [pl.BlockSpec(memory_space=pl.ANY)] * len(extra),
            out_specs=[b for b, _, _ in outs],
            scratch_shapes=scratch,
        ),
        out_shape=[shape(dims, dtype) for _, dims, dtype in outs],
        compiler_params=pltpu.CompilerParams(vmem_limit_bytes=megabytes * 1024 * 1024),
        cost_estimate=pl.CostEstimate(flops=1000 + int(1e9 * micros), transcendentals=0, bytes_accessed=1000),
    )(scalars, *arrays, *extra)
    Order.last = made[-1]
    if shape is pltpu.HBM:
        Order.last = pltpu.with_memory_space_constraint(made[-1], pltpu.HBM)
    return made


def row_of(ref, layer):
    return ref[layer : layer + 1, :].astype(F32)


def segments(scalars, count, slots, dim):
    shape = (slots, 1) if dim == 0 else (1, slots)
    slot = lax.broadcasted_iota(jnp.int32, shape, dim) + scalars[0] * (slots // 2)
    slot = jnp.where(slot >= slots, slot - slots, slot)
    base = 1 + scalars[0] * count
    shift = jnp.where(scalars[base + 1] > 0, QSLOT.bit_length() - 1, slots.bit_length() - 1)
    segment = lax.shift_right_logical(slot, jnp.broadcast_to(shift, shape))
    inside = slot - lax.shift_left(segment, jnp.broadcast_to(shift, shape))
    length = jnp.zeros(shape, jnp.int32)
    for k in range(count):
        length = jnp.where(segment == k, scalars[base + k], length)
    return segment, jnp.where(inside < length, segment, -1)


def attend_kernel(layer, count, split, scalars, *refs):
    refs = list(refs)
    xs = [refs.pop(0) for _ in range(2 if split else 1)]
    qkv, co, cp, lse = refs[10:14]
    bias = refs[-1]
    x = refs[14] if split else xs[0]
    slots = co.shape[0]

    @pl.when(pl.program_id(0) == 0)
    def _():
        segment, _ = segments(scalars, count, slots, 0)
        _, live = segments(scalars, count, slots, 1)
        bias[...] = jnp.where(segment == live, 0.0, -1e9)
        if split:
            x[...] = jnp.concatenate([r[...] for r in xs], axis=0)

    attend_step(layer, x[...], refs[:10], qkv, (co, cp), lse, bias, 0)


def attend_step(layer, xv, operands, qkv, ctx, lse, bias, column):
    wqo, wqp, wko, wkp, wvo, wvp, bqo, bqp, bvo, bvp = operands
    q = (nn(xv, beside(wqo, wqp)) + both(bqo, bqp, layer)).astype(BF)
    k = nn(xv, beside(wko, wkp)).astype(BF)
    v = (nn(xv, beside(wvo, wvp)) + both(bvo, bvp, layer)).astype(BF)
    first = lax.broadcasted_iota(jnp.int32, (1, PAIR), 1) < DH
    lse[...] = jnp.zeros_like(lse)
    for pair, cr in enumerate(ctx):
        at = slice(pair * PAIR, (pair + 1) * PAIR)
        qq, kk, vv = q[:, at], k[:, at], v[:, at]
        for i, part in enumerate((qq, kk, vv)):
            qkv[2 * i + pair, :, :] = part
        outs, peaks = [], []
        for head in range(2):
            mine = first if head == 0 else ~first
            qm = jnp.where(mine, qq, jnp.zeros_like(qq)) * 0.125
            s = nt(qm.astype(BF), kk) + bias[...]
            peak = jnp.max(s, axis=1, keepdims=True)
            e = jnp.exp(s - peak).astype(BF)
            outs.append(nn(e, jnp.where(mine, vv, jnp.ones_like(vv))))
            peaks.append(peak)
        total = pltpu.roll(jnp.where(first, outs[1], outs[0]), DH, 1)
        cr[:, pl.ds(column, PAIR)] = (jnp.where(first, outs[0], outs[1]) / total).astype(BF)
        logs = jnp.where(first, peaks[0], peaks[1]) + jnp.log(total)
        flat = logs.T
        lse[2 * pair : 2 * pair + 1, :] = flat[0:1, :]
        lse[2 * pair + 1 : 2 * pair + 2, :] = flat[DH : DH + 1, :]


def triple(count, slots):
    return pl.BlockSpec((count, slots, PAIR), lambda i, *s: (0, 0, i))


def both(own, peer, layer):
    return jnp.concatenate([row_of(own, layer), row_of(peer, layer)], axis=1)


def attend(layer, scalars, count, x, own, peer):
    split = isinstance(x, tuple)
    layers, width, half = own["w_query"].shape
    slots = 2 * x[0].shape[1] if split else x.shape[0]
    steps = half // PAIR
    act = columns(slots, PAIR)
    ins = [(my_row(a), a) for a in x] if split else [(whole(slots, width), x)]
    for name in ("w_query", "w_key", "w_value"):
        ins += [layer_columns(layer, own[name], PAIR), layer_columns(layer, peer[name], PAIR)]
    ins += [(columns(layers, PAIR), own["b_query"]), (columns(layers, PAIR, 4 * steps), peer["biases"])]
    ins += [(columns(layers, PAIR), own["b_value"]), (columns(layers, PAIR, 5 * steps), peer["biases"])]
    outs = [(triple(6, slots), (6, slots, half), BF)] + [(act, (slots, half), BF)] * 2
    outs += [(pl.BlockSpec((None, 8, slots), lambda i, *s: (i, 0, 0)), (steps, 8, slots), F32)]
    if split:
        outs += [(whole(slots, width), (slots, width), BF)]
    kernel = functools.partial(attend_kernel, layer, count, split)
    return run(kernel, steps, scalars, ins, outs, [pltpu.VMEM((slots, slots), F32)], 32, True)


def normalize(r):
    mean = jnp.mean(r, axis=1, keepdims=True)
    c = r - mean
    rstd = lax.rsqrt(jnp.mean(c * c, axis=1, keepdims=True) + 1e-12)
    return c * rstd, rstd


def norm_back(dy, n, rstd, gain):
    gdy = dy * gain
    return (
        gdy - jnp.mean(gdy, axis=1, keepdims=True) - n * jnp.mean(gdy * n, axis=1, keepdims=True)
    ) * rstd


def colsum(v):
    return jnp.sum(v.astype(F32), axis=0, keepdims=True)


def norm_back_store(dy, n, rstd, gain, low, sums):
    lowv = norm_back(dy, n, rstd, gain).astype(BF)
    low[:, :] = lowv
    sums[...] = jnp.concatenate(
        [colsum(dy * n), colsum(dy), colsum(lowv), jnp.zeros((5, dy.shape[1]), F32)], axis=0
    )


def gelu_step(low, up, up_bias):
    u = nn(low, up) + up_bias
    cdf = 0.5 * (1.0 + lax.erf(u * 0.7071067811865476))
    act = (u * cdf).astype(BF)
    return act, (cdf + u * (jnp.exp(u * u * -0.5) * 0.3989422804014327)).astype(BF)


def first_norm(layer, x, ctx, projection, b_out, g1, s1):
    n, rstd = normalize(x.astype(F32) + (nt(ctx, projection) + row_of(b_out, layer)))
    return n, rstd, n * row_of(g1, layer) + row_of(s1, layer)


def feed_kernel(layer, scalars, *refs):
    (x, co, cp, woo, wop, b_out, g1, s1, wuo, wup, wdo, wdp, buo, bup, b_down, g2, s2) = refs[:17]
    (n1, rstd1, hlow, acto, actp, gp, y, n2, rstd2, h, acc) = refs[17:]
    step = pl.program_id(0)

    @pl.when(step == 0)
    def _():
        n, rstd, hv = first_norm(layer, x[...], beside(co, cp), beside(woo, wop), b_out, g1, s1)
        n1[...] = n.astype(BF)
        rstd1[...] = rstd
        h[...] = hv
        hlow[...] = hv.astype(BF)
        acc[...] = jnp.zeros_like(acc)

    act, slope = gelu_step(hlow[...], beside(wuo, wup), both(buo, bup, layer))
    acto[...] = act[:, :CHUNK]
    actp[...] = act[:, CHUNK:]
    gp[0, :, :] = slope[:, :CHUNK]
    gp[1, :, :] = slope[:, CHUNK:]
    acc[...] += nt(act, beside(wdo, wdp))

    @pl.when(step == pl.num_programs(0) - 1)
    def _():
        n, rstd = normalize(h[...] + (acc[...] + row_of(b_down, layer)))
        y[...] = (n * row_of(g2, layer) + row_of(s2, layer)).astype(BF)
        n2[...] = n.astype(BF)
        rstd2[...] = rstd


def feed(layer, scalars, x, ctx_own, ctx_peer, own, peer):
    layers, width, half = own["w_query"].shape
    slots = x.shape[0]
    ff = own["w_up"].shape[2]
    full = whole(slots, width)
    one = whole(slots, 1)
    vec = whole(layers, width)
    act = columns(slots, CHUNK)
    part = whole(slots, half)
    ins = [(full, x), (part, ctx_own), (part, ctx_peer), layer_whole(layer, own["w_out"]), layer_whole(layer, peer["w_out"])]
    ins += [(vec, own[n]) for n in ("b_out", "first_gain", "first_shift")]
    for name in ("w_up", "w_down"):
        ins += [layer_columns(layer, own[name], CHUNK), layer_columns(layer, peer[name], CHUNK)]
    ins += [(columns(layers, CHUNK), own["b_up"]), (columns(layers, CHUNK), peer["biases"])]
    ins += [(vec, own[n]) for n in ("b_down", "second_gain", "second_shift")]
    outs = [(full, (slots, width), BF), (one, (slots, 1), F32), (full, (slots, width), BF)]
    outs += [(act, (slots, ff), BF)] * 2
    outs += [(pl.BlockSpec((2, slots, CHUNK), lambda i, *s: (0, 0, i)), (2, slots, ff), BF)]
    outs += [(full, (slots, width), BF), (full, (slots, width), BF), (one, (slots, 1), F32)]
    scratch = [pltpu.VMEM((slots, width), F32)] * 2
    return run(functools.partial(feed_kernel, layer), ff // CHUNK, scalars, ins, outs, scratch, 60, True)


class Loads:
    def __init__(self, sources, targets, sems):
        self.copies = [pltpu.make_async_copy(s, t, sems.at[i]) for i, (s, t) in enumerate(zip(sources, targets))]

    def start(self):
        for c in self.copies:
            c.start()

    def wait(self):
        for c in self.copies:
            c.wait()


def layer_of(ref, layer):
    return ref.at[layer if ref.shape[0] > 1 else 0]


def slope_step(chunk, low, gp, down, up, duo, dup, gbuo, gbup):
    du = (nn(low, down) * gp.astype(F32)).astype(BF)
    duo[...] = du[:, :CHUNK]
    dup[...] = du[:, CHUNK:]
    total = colsum(du)
    gbuo[:, chunk] = total[:, :CHUNK]
    gbup[:, chunk] = total[:, CHUNK:]
    return nt(du, up)


def columns_of(refs, chunk):
    return jnp.concatenate([r[:, chunk] for r in refs], axis=1)


def turn_kernel(layer, count, scalars, *refs):
    x, attention, weights, rest = refs[0], refs[1:11], refs[11:17], list(refs[17:])
    (b_out, g1, s1, buo, bup, b_down, g2, s2, cot_a, cot_b) = rest[:10]
    (qkv, co, cp, lse, hlow, acto, actp, y, gbuo, gbup, sums2, duo, dup, both_low, sums1) = rest[10:25]
    (bias, woo, wop, wuo, wup, wdo, wdp, gp, h, acc, n1, rstd1, sems) = rest[25:]
    dff, datt = both_low.at[0], both_low.at[1]
    step = pl.program_id(0)
    slots = co.shape[0]
    attending = co.shape[1] // PAIR
    feeding = gp.shape[2] // CHUNK
    loads = Loads([layer_of(w, layer) for w in weights], (woo, wop, wuo, wup, wdo, wdp), sems)

    @pl.when(step == 0)
    def _():
        loads.start()
        segment, _ = segments(scalars, count, slots, 0)
        _, live = segments(scalars, count, slots, 1)
        bias[...] = jnp.where(segment == live, 0.0, -1e9)

    @pl.when(step < attending)
    def _():
        attend_step(layer, x[...], attention, qkv, (co, cp), lse, bias, pl.multiple_of(step * PAIR, PAIR))

    @pl.when(step == attending)
    def _():
        loads.wait()
        n, rstd, hv = first_norm(layer, x[...], beside(co, cp), beside(woo, wop), b_out, g1, s1)
        n1[...] = n
        rstd1[...] = rstd
        h[...] = hv
        hlow[...] = hv.astype(BF)
        acc[...] = jnp.zeros_like(acc)

    @pl.when((step >= attending) & (step < attending + feeding))
    def _():
        chunk = pl.ds(pl.multiple_of((step - attending) * CHUNK, CHUNK), CHUNK)
        up_bias = jnp.concatenate([r[layer : layer + 1, chunk].astype(F32) for r in (buo, bup)], axis=1)
        act, slope = gelu_step(hlow[...], columns_of((wuo, wup), chunk), up_bias)
        acto[...] = act[:, :CHUNK]
        actp[...] = act[:, CHUNK:]
        gp[0, :, chunk] = slope[:, :CHUNK]
        gp[1, :, chunk] = slope[:, CHUNK:]
        acc[...] += nt(act, columns_of((wdo, wdp), chunk))

    @pl.when(step == attending + feeding - 1)
    def _():
        n, rstd = normalize(h[...] + (acc[...] + row_of(b_down, layer)))
        result = (n * row_of(g2, layer) + row_of(s2, layer)).astype(BF)
        y[0, :, :] = result[: slots // 2]
        y[1, :, :] = result[slots // 2 :]
        dy = jnp.concatenate([cot_a[...], cot_b[...]], axis=0).astype(F32)
        norm_back_store(dy, n, rstd, row_of(g2, layer), dff, sums2)
        acc[...] = dff[...].astype(F32)

    @pl.when(step >= attending + feeding)
    def _():
        chunk = pl.ds(pl.multiple_of((step - attending - feeding) * CHUNK, CHUNK), CHUNK)
        slope = jnp.concatenate([gp[0, :, chunk], gp[1, :, chunk]], axis=1)
        acc[...] += slope_step(
            chunk, dff[...], slope, columns_of((wdo, wdp), chunk), columns_of((wuo, wup), chunk),
            duo, dup, gbuo, gbup,
        )

    @pl.when(step == pl.num_programs(0) - 1)
    def _():
        norm_back_store(acc[...], n1[...], rstd1[...], row_of(g1, layer), datt, sums1)


def turn(layer, scalars, count, x, own, peer, cotangent):
    layers, width, half = own["w_query"].shape
    slots, ff = x.shape[0], own["w_up"].shape[2]
    attending, feeding = half // PAIR, ff // CHUNK

    def early(rows, start=0):
        return pl.BlockSpec((rows, PAIR), lambda i, *s: (0, start + jnp.clip(i, 0, attending - 1)))

    def early_weight(array):
        at = layer if array.shape[0] > 1 else 0
        return pl.BlockSpec((None, width, PAIR), lambda i, *s: (at, 0, jnp.clip(i, 0, attending - 1))), array

    full, vec = whole(slots, width), whole(layers, width)
    anywhere = pl.BlockSpec(memory_space=pl.ANY)
    ins = [(full, x)]
    for name in ("w_query", "w_key", "w_value"):
        ins += [early_weight(own[name]), early_weight(peer[name])]
    ins += [(early(layers), own["b_query"]), (early(layers, 4 * attending), peer["biases"])]
    ins += [(early(layers), own["b_value"]), (early(layers, 5 * attending), peer["biases"])]
    for name in ("w_out", "w_up", "w_down"):
        ins += [(anywhere, own[name]), (anywhere, peer[name])]
    ins += [(vec, own[n]) for n in ("b_out", "first_gain", "first_shift")]
    ins += [(whole(*a.shape), a) for a in (own["b_up"], peer["biases"])]
    ins += [(vec, own[n]) for n in ("b_down", "second_gain", "second_shift")]
    ins += [(my_row(a), a) for a in cotangent]
    late = pl.BlockSpec((slots, CHUNK), lambda i, *s: (0, jnp.clip(i - attending, 0, feeding - 1)))
    halves = (2, slots // 2, width)
    outs = [
        (pl.BlockSpec((6, slots, PAIR), lambda i, *s: (0, 0, jnp.clip(i, 0, attending - 1))), (6, slots, half), BF)
    ]
    outs += [(whole(slots, half), (slots, half), BF)] * 2
    outs += [
        (pl.BlockSpec((None, 8, slots), lambda i, *s: (jnp.clip(i, 0, attending - 1), 0, 0)), (attending, 8, slots), F32)
    ]
    outs += [(full, (slots, width), BF)] + [(late, (slots, ff), BF)] * 2 + [(whole(*halves), halves, BF)]
    outs += [(whole(1, ff), (1, ff), F32)] * 2 + [(whole(8, width), (8, width), F32)]
    latest = pl.BlockSpec((slots, CHUNK), lambda i, *s: (0, jnp.clip(i - attending - feeding, 0, feeding - 1)))
    outs += [(latest, (slots, ff), BF)] * 2
    outs += [(whole(2, slots, width), (2, slots, width), BF), (whole(8, width), (8, width), F32)]
    scratch = [pltpu.VMEM((slots, slots), F32)] + [pltpu.VMEM((width, half), BF)] * 2
    scratch += [pltpu.VMEM((width, ff), BF)] * 4 + [pltpu.VMEM((2, slots, ff), BF)]
    scratch += [pltpu.VMEM((slots, width), F32)] * 3 + [pltpu.VMEM((slots, 1), F32), pltpu.SemaphoreType.DMA((6,))]
    kernel = functools.partial(turn_kernel, layer, count)
    return run(kernel, attending + 2 * feeding, scalars, ins, outs, scratch, 56, True)


def attend_back_kernel(layer, count, above, scalars, *refs):
    rest = list(refs)

    def take(n):
        return [rest.pop(0) for _ in range(n)]

    datt, woo, wop, wqo, wqp, wko, wkp, wvo, wvp, qkv, lse, sums1, sums2, gbuo, gbup = take(15)
    upper = take(2) if above else None
    if layer:
        n2, rstd2, gain2, n1, rstd1, gain1 = take(6)
        sources = take(5)
    ours, others, mine, theirs = take(4)
    if layer:
        below2, duo, dup, below_gbuo, below_gbup, both_low, below1 = take(7)
        dff, below_datt = both_low.at[0], both_low.at[1]
    else:
        dx_own, dx_peer = take(2)
    dx, bias = take(2)
    step = pl.program_id(0)
    slots = datt.shape[0]
    attending = down_steps(mine)
    if layer:
        wuo, wup, wdo, wdp, gp, sems = take(6)
        loads = Loads(
            [*[layer_of(w, layer - 1) for w in sources[:4]], sources[4]], (wuo, wup, wdo, wdp, gp), sems
        )

    @pl.when(step == 0)
    def _():
        if layer:
            loads.start()
        _, live = segments(scalars, count, slots, 0)
        segment, _ = segments(scalars, count, slots, 1)
        bias[...] = jnp.where(segment == live, 0.0, -1e9)
        rows = jnp.concatenate([sums1[0:3, :], sums2[0:3, :]], axis=0)
        for i, (pack, gbu) in enumerate(((mine, gbuo), (theirs, gbup))):
            width = pack.shape[1]
            pack[:16, :] = jnp.concatenate(
                [rows, gbu[:, :width], gbu[:, width:], jnp.zeros((8, width), F32)], axis=0
            )
            if above:
                pack[16:, :] = upper[i][...]
        dx[...] = datt[...].astype(F32)

    @pl.when(step < attending)
    def _():
        dctx = nn(datt[...], beside(woo, wop)).astype(BF)
        first = lax.broadcasted_iota(jnp.int32, (1, PAIR), 1) < DH
        grads = []
        for pair, pack in enumerate((mine, theirs)):
            qq, kk, vv = (qkv[2 * i + pair, :, :] for i in range(3))
            do = dctx[:, pair * PAIR : (pair + 1) * PAIR]
            dq_t, dk, dv = 0.0, 0.0, 0.0
            for head in range(2):
                sel = first if head == 0 else ~first
                qm = (jnp.where(sel, qq, jnp.zeros_like(qq)) * 0.125).astype(BF)
                km = (jnp.where(sel, kk, jnp.zeros_like(kk)) * 0.125).astype(BF)
                dom = jnp.where(sel, do, jnp.zeros_like(do))
                at = 2 * pair + head
                p = jnp.exp(nt(kk, qm) + bias[...] - lse[at : at + 1, :])
                dp = nt(vv, dom)
                delta = jnp.sum(p * dp, axis=0, keepdims=True)
                ds = (p * (dp - delta)).astype(BF)
                dv += nn(p.astype(BF), dom)
                dk += nn(ds, qm)
                dq_t += nn(km.T, ds)
            dq = dq_t.T.astype(BF)
            dk = dk.astype(BF)
            dv = dv.astype(BF)
            for i, part in enumerate((dq, dk, dv)):
                (others if pair else ours)[i, :, :] = part
            pack[8:9, pl.ds(pl.multiple_of(step * PAIR, PAIR), PAIR)] = colsum(dq)
            pack[8:9, pl.ds(pl.multiple_of((step + attending) * PAIR, PAIR), PAIR)] = colsum(dv)
            grads.append((dq, dk, dv))
        back = jnp.concatenate([g[i] for i in range(3) for g in grads], axis=1)
        dx[...] += nt(back, beside(wqo, wqp, wko, wkp, wvo, wvp))

    if not layer:

        @pl.when(step == attending - 1)
        def _():
            dx_own[...] = dx[: slots // 2, :]
            dx_peer[...] = dx[slots // 2 :, :].astype(BF)

        return

    @pl.when(step == attending)
    def _():
        loads.wait()
        norm_back_store(dx[...], n2[...].astype(F32), rstd2[...], row_of(gain2, layer - 1), dff, below2)
        dx[...] = dff[...].astype(F32)

    @pl.when(step >= attending)
    def _():
        chunk = pl.ds(pl.multiple_of((step - attending) * CHUNK, CHUNK), CHUNK)
        slope = jnp.concatenate([gp[0, :, chunk], gp[1, :, chunk]], axis=1)
        dx[...] += slope_step(
            chunk, dff[...], slope, columns_of((wdo, wdp), chunk), columns_of((wuo, wup), chunk),
            duo, dup, below_gbuo, below_gbup,
        )

    @pl.when(step == pl.num_programs(0) - 1)
    def _():
        norm_back_store(dx[...], n1[...].astype(F32), rstd1[...], row_of(gain1, layer - 1), below_datt, below1)


def down_steps(pack):
    return pack.shape[1] // 2 // PAIR


def attend_back(layer, scalars, count, lows, own, peer, saved, lse, sums, above, below):
    lows, pick = lows
    slots, width = lows.shape[1:]
    layers, _, half = own["w_query"].shape
    ff = own["w_up"].shape[2]
    attending, feeding = half // PAIR, ff // CHUNK if layer else 0

    def at(i):
        return jnp.clip(i, 0, attending - 1)

    def early_weight(array):
        k = layer if array.shape[0] > 1 else 0
        return pl.BlockSpec((None, width, PAIR), lambda i, *s: (k, 0, at(i))), array

    def stack(n):
        return pl.BlockSpec((n, slots, PAIR), lambda i, *s: (0, 0, at(i)))

    full, one = whole(slots, width), whole(slots, 1)
    vec = whole(layers, width)
    ins = [(pl.BlockSpec((None, slots, width), lambda i, *s: (pick, 0, 0)), lows)]
    for name in ("w_out", "w_query", "w_key", "w_value"):
        ins += [early_weight(own[name]), early_weight(peer[name])]
    ins += [(stack(6), saved), (pl.BlockSpec((None, 8, slots), lambda i, *s: (at(i), 0, 0)), lse)]
    ins += [(whole(*a.shape), a) for a in (*sums, *above)]
    packed = (16 * (layers - layer), width)
    outs = [(stack(3), (3, slots, half), BF)] * 2
    outs += [(whole(*packed), packed, F32)] * 2
    scratch = [pltpu.VMEM((slots, width), F32), pltpu.VMEM((slots, slots), F32)]
    row = (whole(8, width), (8, width), F32)
    if layer:
        n1, rstd1, slope, n2, rstd2, lower = below
        ins += [(full, n2), (one, rstd2), (vec, own["second_gain"]), (full, n1), (one, rstd1), (vec, own["first_gain"])]
        anywhere = pl.BlockSpec(memory_space=pl.ANY)
        ins += [(anywhere, a) for a in (own["w_up"], lower["w_up"], own["w_down"], lower["w_down"], slope)]
        latest = pl.BlockSpec((slots, CHUNK), lambda i, *s: (0, jnp.clip(i - attending, 0, feeding - 1)))
        outs += [row] + [(latest, (slots, ff), BF)] * 2
        outs += [(whole(1, ff), (1, ff), F32)] * 2 + [(whole(2, slots, width), (2, slots, width), BF), row]
        scratch += [pltpu.VMEM((width, ff), BF)] * 4 + [pltpu.VMEM((2, slots, ff), BF), pltpu.SemaphoreType.DMA((5,))]
    else:
        outs += [(whole(slots // 2, width), (slots // 2, width), t) for t in (F32, BF)]
    kernel = functools.partial(attend_back_kernel, layer, count, bool(above))
    return run(kernel, attending + feeding, scalars, ins, outs, scratch, 52, True)


def halves_of(value, bit, scalars, left, base):
    axis = left.index(bit)
    rows, width = value.shape
    cut = value.reshape(1 << axis, 2, rows >> (axis + 1), width)
    mine = (scalars[base] >> bit) & 1
    low, high = cut[:, 0].reshape(rows // 2, width), cut[:, 1].reshape(rows // 2, width)
    return jnp.where(mine == 0, low, high), jnp.where(mine == 0, high, low)


def weight_kernel(plan, lefts, left, scalars, *refs):
    bits, plan = plan
    step = pl.program_id(0)
    pieces = len(plan)
    sides, operands = refs[: 2 * lefts], refs[2 * lefts : 2 * lefts + 2 * pieces]
    outs, (lt, right) = refs[2 * lefts + 2 * pieces : -2], refs[-2:]
    slots = sides[0].shape[0]
    for n, (start, steps, block, side, fresh, places) in enumerate(plan):
        ro, rp = operands[2 * n : 2 * n + 2]
        if fresh:

            @pl.when(step == start)
            def _(side=side):
                lt[:, :slots] = sides[2 * side][...].T
                lt[:, slots:] = sides[2 * side + 1][...].T

        @pl.when((step >= start) & (step < start + steps))
        def _(ro=ro, rp=rp, block=block, start=start, places=places):
            right[:slots, :block] = ro[...]
            right[slots:, :block] = rp[...]
            value = nn(lt[...], right[:, :block])
            cut = 0
            for g, column, wide in places:
                part = value[:, cut : cut + wide]
                cut += wide
                at = pl.ds(pl.multiple_of(column + (step - start) * block, 128), wide)
                if bits[g] is None:
                    outs[g][:, at] = part.astype(BF)
                else:
                    keep, send = halves_of(part, bits[g], scalars, left, 1)
                    outs[2 * g][:, at] = keep.astype(BF)
                    outs[2 * g + 1][:, at] = send.astype(BF)


def weight_grads(scalars, orders, parts, size, block):
    bits = size.bit_length() - 1
    left = list(range(bits - 1, -1, -1))
    plan, ins, outs, wide, sides = [], [], [], [], {}
    at = 0

    def parted(operand):
        return operand if isinstance(operand, tuple) else (operand, None)

    def side_spec(pick):
        if pick is None:
            return pl.BlockSpec((slots, width), lambda i, *s: (0, 0), pipeline_mode=pl.Buffered(1))
        return pl.BlockSpec((None, slots, width), lambda i, *s: (pick, 0, 0), pipeline_mode=pl.Buffered(1))

    slots, width = parted(parts[0][0])[0].shape[-2:]
    split = (width // size) % 16 == 0
    before = None
    filled = [0] * len(orders)
    for lo, lp, ro, rp, *goal in parts:
        (lo, pick), (lp, _) = parted(lo), parted(lp)
        key = (id(lo), pick)
        if key not in sides:
            sides[key] = len(sides)
            wide += [(side_spec(pick), lo), (side_spec(pick), lp)]
        (ro, pick), (rp, _) = parted(ro), parted(rp)
        units = rp.shape[-1]
        blk = min(block, units)
        steps = units // blk
        places = []
        for g, many in goal if isinstance(goal[0], tuple) else ((goal[0], blk),):
            places.append((g, filled[g], many))
            filled[g] += many * steps
        plan.append((at, steps, blk, sides[key], sides[key] != before, places))
        before = sides[key]

        def spec(i, *s, a=at, n=steps, k=pick):
            place = jnp.clip(i - a, 0, n - 1)
            return (0, place) if k is None else (k, 0, place)

        shape = (slots, blk) if pick is None else (None, slots, blk)
        ins += [(pl.BlockSpec(shape, spec), ro), (pl.BlockSpec(shape, spec), rp)]
        at += steps
    rows = width // 2 if split else width
    for total in filled:
        outs += [(whole(rows, total), (rows, total), BF)] * (2 if split else 1)
    plan = ([o[0] if split else None for o in orders], plan)
    pins = [*range(len(wide) + len(ins))]
    scratch = [pltpu.VMEM((width, 2 * slots), BF), pltpu.VMEM((2 * slots, block), BF)]
    kernel = functools.partial(weight_kernel, plan, len(sides), left)
    made = run(kernel, at, scalars, [*wide, *ins], outs, scratch, 36, pins)
    if split:
        return [Scatter(scalars, o, size, made[2 * g], made[2 * g + 1]) for g, o in enumerate(orders)]
    return [Scatter(scalars, o, size, None, made[g]) for g, o in enumerate(orders)]


def add_kernel(plan, scalars, *refs):
    ins, outs = refs[: 2 * len(plan)], refs[2 * len(plan) :]
    for i, (bit, left) in enumerate(plan):
        value = ins[2 * i][...].astype(F32) + ins[2 * i + 1][...].astype(F32)
        if bit is None:
            outs[2 * i][...] = value
        else:
            kept, send = halves_of(value, bit, scalars, left, 1)
            outs[2 * i][...] = kept.astype(BF)
            outs[2 * i + 1][...] = send.astype(BF)


def merge_kernel(bit, left, scalars, *refs):
    ins, (keep, send) = refs[:-2], refs[-2:]
    at = 0
    for i in range(len(ins) // 2):
        value = ins[2 * i][...].astype(F32) + ins[2 * i + 1][...].astype(F32)
        kept, sent = halves_of(value, bit, scalars, left, 1)
        width = value.shape[1]
        keep[:, at : at + width] = kept.astype(BF)
        send[:, at : at + width] = sent.astype(BF)
        at += width


def land(*scatters, merge=False, micros=0.05):
    if not scatters:
        return None
    unit = scatters[0].keep.shape[0] >> len(scatters[0].order)
    if unit % 16:
        for f in scatters:
            f.part((f.keep.astype(F32) + f.value.astype(F32)).astype(BF))
        if merge:
            first = scatters[0]
            first.keep = jnp.concatenate([f.keep for f in scatters], axis=1)
            first.value = jnp.concatenate([f.value for f in scatters], axis=1)
            return first
        return None
    if merge:
        first = scatters[0]
        rows, total = first.keep.shape[0] // 2, sum(f.keep.shape[1] for f in scatters)
        ins = [(whole(*a.shape), a) for f in scatters for a in (f.keep, f.value)]
        kernel = functools.partial(merge_kernel, first.order[0], list(first.left))
        both_out = [(whole(rows, total), (rows, total), BF)] * 2
        first.keep, first.value = run(kernel, 1, first.scalars, ins, both_out, [], 32)
        return first
    steps = 1
    if max(f.keep.size for f in scatters) > 300000:
        steps = next(n for n in (3, 2, 1) if not any(f.keep.shape[1] % (128 * n) for f in scatters))
    ins, outs, plan = [], [], []
    for f in scatters:
        rows, width = f.keep.shape
        block = columns(rows, width // steps)
        ins += [(block, f.keep), (block, f.value)]
        outs += [(columns(rows // 2, width // steps), (rows // 2, width), BF)] * 2
        plan.append((f.order[0], list(f.left)))
    made = run(functools.partial(add_kernel, plan), steps, scatters[0].scalars, ins, outs, [], 32, micros=micros)
    for i, f in enumerate(scatters):
        f.keep, f.value = made[2 * i : 2 * i + 2]
    return None


class Scatter:
    def __init__(self, scalars, order, size, keep, send):
        bits = size.bit_length() - 1
        self.scalars, self.size = scalars, size
        self.order = [b for b in order if b < bits] + list(range(4, bits))
        self.left = list(range(bits - 1, -1, -1))
        self.keep, self.value = keep, send
        if keep is None:
            self.part(send)

    def part(self, value):
        bit = self.order[0]
        axis = self.left.index(bit)
        rows, width = value.shape
        cut = value.reshape(1 << axis, 2, rows >> (axis + 1), width)
        mine = (self.scalars[1] >> bit) & 1
        self.keep = lax.dynamic_index_in_dim(cut, mine, 1, keepdims=False).reshape(rows // 2, width)
        self.value = lax.dynamic_index_in_dim(cut, 1 - mine, 1, keepdims=False).reshape(rows // 2, width)

    def launch(self):
        bit = self.order.pop(0)
        self.left.remove(bit)
        self.value = flip(self.value, bit, self.size)
        return self


def settle_kernel(scalars, keep, got, out):
    out[...] = keep[...].astype(F32) + got[...].astype(F32)


def settle(scatter):
    rows, width = scatter.keep.shape
    block = whole(rows, width)
    (scatter.keep,) = run(
        settle_kernel, 1, scatter.scalars, [(block, scatter.keep), (block, scatter.value)],
        [(block, (rows, width), F32)], [], 16,
    )
    scatter.value = None


def last_kernel(plan, count, scalars, *refs):
    pairs, rest = [], list(refs)
    for n in count:
        pairs.append([rest.pop(0) for _ in range(n)])
    total, got = rest.pop(0), rest.pop(0)
    for out, layers in zip(rest, plan):
        for layer, (i, at) in enumerate(layers):
            cut = slice(at, at + out.shape[2])
            parts = [r[:, cut].astype(F32) for r in pairs[i]]
            out[layer, :, :] = sum(parts[1:], parts[0])
    gbq, gbv, gbu, *vectors = rest[len(plan) :]
    width = total.shape[1]
    sums = total[...] + got[...]
    for layer in range(len(plan[0])):
        mine = sums[16 * layer : 16 * layer + 16, :]
        row = slice(layer, layer + 1)
        for i, out in enumerate(vectors):
            out[row, :] = mine[i : i + 1, :]
        gbu[row, :width] = mine[6:7, :]
        gbu[row, width:] = mine[7:8, :]
        gbq[row, :] = mine[8:9, : width // 2]
        gbv[row, :] = mine[8:9, width // 2 :]


def last_sums(scalars, scatters, plan, widths, total, got, small):
    rows, layers = scatters[0].keep.shape[0], len(plan[0])
    arrays = [a for f in scatters for a in (f.keep, f.value) if a is not None] + [total, got]
    outs = [(whole(layers, rows, w), (layers, rows, w), F32) for w in widths]
    outs += [(whole(layers, n), (layers, n), F32) for n in small]
    kernel = functools.partial(last_kernel, plan, [1 if f.value is None else 2 for f in scatters])
    return run(kernel, 1, scalars, [(whole(*a.shape), a) for a in arrays], outs, [], 48, "out")


def copy_kernel(scalars, value, out):
    out[...] = value[...]


def sum_kernel(scalars, left, right, out):
    out[...] = left[...] + right[...]


def swap(value):
    return lax.ppermute(value, "mp", [(0, 1), (1, 0)])


def flip(value, bit, size):
    return lax.ppermute(value, "dp", [(i, i ^ (1 << bit)) for i in range(size)])


NAMES = (
    "w_query", "b_query", "w_key", "w_value", "b_value", "w_out", "b_out", "first_gain", "first_shift",
    "w_up", "b_up", "w_down", "b_down", "second_gain", "second_shift",
)
XY, YX = (0, 1, 2, 3), (1, 0, 2, 3)
TURNS = (0, 1, 2, 3), (1, 2, 0, 3), (2, 0, 1, 3)


def shards(dp, tokens, lengths, cotangent, *given):
    held = dict(zip(NAMES, given, strict=True))
    layers, width, half = held["w_query"].shape
    ff = held["w_up"].shape[2]
    slots = 2 * tokens.shape[1]
    count = lengths.shape[1]
    me = lax.axis_index("mp")
    scalars = jnp.concatenate([me[None], lengths.reshape(-1)]).astype(jnp.int32)
    place = jnp.stack([me, lax.axis_index("dp")]).astype(jnp.int32)

    def give_row(mine, other):
        other = swap(other).astype(mine.dtype)
        return jnp.stack([jnp.where(me == 0, mine, other), jnp.where(me == 0, other, mine)])

    Order.last, Order.also = None, ()
    biases = swap(jnp.concatenate([held["b_up"], held["b_query"], held["b_value"]], axis=1))
    x = (tokens, swap(tokens))
    early = {n: swap(held[n]) for n in ("w_query", "w_key", "w_value")}
    names = ("w_out", "w_up", "w_down")
    pieces, early, biases, x = lax.optimization_barrier(([held[n][:1] for n in names], early, biases, x))
    first = {n: swap(p) for n, p in zip(names, pieces, strict=True)}
    peers = [{"biases": biases, **early, **first} for _ in range(layers)]

    def last_wave(after):
        pieces, cot, fresh, after = lax.optimization_barrier(([held[n] for n in names], cotangent, first, after))
        later = {n: swap(p) for n, p in zip(names, pieces, strict=True)}
        for layer in range(layers):
            peers[layer].update(later if layer else fresh)
        return (cot, swap(cot)), after

    kept = []
    for layer in range(layers - 1):
        made = attend(layer, scalars, count, x, held, peers[layer])
        if layer == 0:
            x = made[4]
            cot, x = last_wave(x)
        fed = feed(layer, scalars, x, made[1], made[2], held, peers[layer])
        kept.append((x, made[:4], fed))
        x = fed[6]
    made = turn(layers - 1, scalars, count, x, held, peers[-1], cot)
    kept.append((x, made[:4], (None, None, *made[4:7])))
    y, gbu_own, gbu_peer, sums2, du_own, du_peer, lows, sums1 = made[7:]

    def step(*scatters, micros=0.05):
        land(*scatters, micros=micros)
        for f in scatters:
            f.launch()

    def step_as_one(*scatters):
        return land(*scatters, merge=True).launch()

    pack, flying, above = (), [], None
    theirs_of = [[swap(a) for a in (x, att[2], fed[2], fed[4])] for x, att, fed in kept]
    Order.also = [a for arrays in theirs_of[:-1] for a in arrays[:2]] + [theirs_of[-1][0]]
    (sums1,) = run(
        copy_kernel, 1, place, [(whole(*sums1.shape), sums1)], [(whole(*sums1.shape), sums1.shape, F32)], [], 8,
        True, 20,
    )
    for layer in reversed(range(layers)):
        x_in, (qkv, ctx_own, _, lse), fed = kept[layer]
        hlow, act_own = fed[2:4]
        x_peer, ctx_peer, h_peer, act_peer = theirs_of[layer]
        lows_peer, du_theirs = swap(lows), swap(du_peer)
        ahead = [((lows, 0), (lows_peer, 0), act_own, act_peer, 0), (hlow, h_peer, du_own, du_theirs, 1)]
        if not flying:
            (down,) = weight_grads(place, [XY], [ahead[0]], dp, 512)
            (up,) = weight_grads(place, [YX], [(*ahead[1][:4], 0)], dp, 512)
            down.launch()
            up.launch()
        else:
            group = weight_grads(place, TURNS[:2], ahead, dp, 512)
            group[0].launch()
            group[1].launch()
            high = step_as_one(*flying)
            group += weight_grads(place, TURNS[2:], [(*a, 0) for a in above], dp, half)
            group[2].launch()
        sums = (sums1, sums2, gbu_own, gbu_peer)
        below = ()
        if layer:
            n1, rstd1, _, _, _, slope, _, n2, rstd2 = kept[layer - 1][2]
            below = (n1, rstd1, slope, n2, rstd2, peers[layer - 1])
        back = attend_back(
            layer, scalars, count, (lows, 1), held, peers[layer], qkv, lse, sums, pack, below
        )
        ours, others, mine, theirs = back[:4]
        pack = (mine, theirs)
        others = swap(others)
        above = [((lows, 1), (lows_peer, 1), ctx_own, ctx_peer)]
        above += [(x_in, x_peer, (ours, i), (others, i)) for i in range(3)]
        if not layer:
            step(high, micros=12)
            step(*group, micros=8)
        if layer:
            Order.also = [*theirs_of[layer - 1][2:], ctx_peer]
            step(down, up, micros=8)
            sums2, du_own, du_peer, gbu_own, gbu_peer, lows, sums1 = back[4:]
            flying = [down, up]
    encoded = give_row(y[0], y[1])
    bits = dp.bit_length() - 1
    left = list(range(bits - 1, -1, -1))
    total, got = mine, swap(theirs)

    def small_step(total, got):
        whole_one = whole(*total.shape)
        (total,) = run(
            sum_kernel, 1, place, [(whole_one, total), (whole_one, got)], [(whole_one, total.shape, F32)], [], 8
        )
        return total, flip(total, left.pop(0), dp)

    third = half // 3
    goals = (0,), ((0, third), (1, 2 * third)), ((1, 2 * third), (2, third)), (2,)
    last = weight_grads(place, TURNS, [(*a, *g) for a, g in zip(above, goals)], dp, half)
    for f in last:
        f.launch()
    total, got = small_step(total, got)
    token_grad = give_row(back[4], back[5])
    while high.order:
        step(high)
    settle(high)
    step(*group)
    step(*last)
    middle = step_as_one(*group)
    total, got = small_step(total, got)
    step(*last)
    total, got = small_step(total, got)
    low = step_as_one(*last)
    total, got = small_step(total, got)
    rest = [middle, low]
    while any(f.order for f in rest) or left:
        for f in rest:
            if f.order:
                step(f)
        if left:
            total, got = small_step(total, got)

    starts = [*((0, 0), (0, ff)), *((2, i * half) for i in range(4))]
    upper = [*((1, 0), (1, ff)), *((0, 2 * ff + i * half) for i in range(4))]
    small = [half, half, ff] + [width] * 6
    gwd, gwu, gwo, gwq, gwk, gwv, gbq, gbv, gbu, gfg, gfs, gbo, gsg, gss, gbd = last_sums(
        place, [middle, high, low], [list(p) for p in zip(starts, upper)], [ff, ff] + [half] * 4, total, got, small
    )
    return (
        encoded, token_grad, gwq, gbq, gwk, gwv, gbv, gwo, gbo, gfg, gfs, gwu, gbu, gwd, gbd, gsg, gss,
    )


def solution(mesh):
    cols, mats, rep = P(None, "mp"), P(None, None, "mp"), P()
    placed = (
        P("dp", "mp", None), P("dp", None), P("dp", "mp", None),
        mats, cols, mats, mats, cols, mats, rep, rep, rep, mats, cols, mats, rep, rep, rep,
    )
    grads = P(None, "dp", "mp")
    return jax.shard_map(
        functools.partial(shards, mesh.shape["dp"]),
        mesh=mesh,
        in_specs=placed,
        out_specs=(
            P("dp", "mp", None), P("dp", "mp", None), grads, cols, grads, grads, cols,
            grads, rep, rep, rep, grads, cols, grads, rep, rep, rep,
        ),
        check_vma=False,
    )
```
